32 devices in a mesh: stream: 2 (over x), seq: 8 (over z, y), head: 2 (over core).
Axes of the slice: x: 2, y: 2, z: 4, core: 2. Of those that a mesh axis runs over, the one named last changes fastest.
Arguments:
- tokens: bfloat16 [4, 2048, 2048], P('stream', 'seq'), may hold values from -6 to 6
- doc_starts: int32 [4, 8], P('stream'), may hold values from 0 to 2047, as said below
- query_weight: bfloat16 [2048, 2048], P(('stream', 'seq'), 'head'), may hold values from -0.125 to 0.125
- key_weight: bfloat16 [2048, 2048], P(('stream', 'seq'), 'head'), may hold values from -0.125 to 0.125
- value_weight: bfloat16 [2048, 2048], P(('stream', 'seq'), 'head'), may hold values from -0.125 to 0.125
- out_weight: bfloat16 [2048, 2048], P('head', ('stream', 'seq')), may hold values from -1 to 1
- gate_weight: bfloat16 [2048, 5504], P(('stream', 'seq'), 'head'), may hold values from -0.125 to 0.125
- up_weight: bfloat16 [2048, 5504], P(('stream', 'seq'), 'head'), may hold values from -0.125 to 0.125
- down_weight: bfloat16 [5504, 2048], P('head', ('stream', 'seq')), may hold values from -0.078125 to 0.078125
- attention_gain: bfloat16 [2048], P(('stream', 'seq')), may hold values from 0.25 to 1.75
- feedforward_gain: bfloat16 [2048], P(('stream', 'seq')), may hold values from 0.25 to 1.75
- cotangent: bfloat16 [4, 2048, 2048], P('stream', 'seq'), may hold values from -6 to 6
Outputs:
- output: bfloat16 [4, 2048, 2048], P('stream', 'seq')
- grad_tokens: float32 [4, 2048, 2048], P('stream', 'seq')
- grad_query_weight: float32 [2048, 2048], P(('stream', 'seq'), 'head')
- grad_key_weight: float32 [2048, 2048], P(('stream', 'seq'), 'head')
- grad_value_weight: float32 [2048, 2048], P(('stream', 'seq'), 'head')
- grad_out_weight: float32 [2048, 2048], P('head', ('stream', 'seq'))
- grad_gate_weight: float32 [2048, 5504], P(('stream', 'seq'), 'head')
- grad_up_weight: float32 [2048, 5504], P(('stream', 'seq'), 'head')
- grad_down_weight: float32 [5504, 2048], P('head', ('stream', 'seq'))
- grad_attention_gain: float32 [2048], P(('stream', 'seq'))
- grad_feedforward_gain: float32 [2048], P(('stream', 'seq'))
The draws below stay inside these ranges and needn't reach their ends.
Inputs may be any that keep to these rules, and one draw needn't show every extreme that they name: `doc_starts`: row s gives the first positions of the 8 documents of stream s in strictly rising order: the first is 0, the next three lie in positions 1 to 255, the next three in positions 1793 to 2046, and the last is 2047.
All inputs are finite; a program needn't handle non-finite values.
Results may differ from the reference program's by a relative error of at most 0.014.
Values may be sent and summed in bfloat16 or wider, within the bound.
A program may use at most 256 MiB of HBM per device.

```python
import math
import jax
import jax.numpy as jnp
from jax import lax

D = 2048
HEADS = 16
HEAD_DIM = 128
FF = 5504
WIN = 2048
TOK_DEV = 256
STREAMS = 4
STREAM_LEN = 2048


def draw_doc_starts(key, part):
    length = STREAM_LEN

    def one_stream(stream_key):
        early_key, late_key = jax.random.split(stream_key)
        early_starts = jax.random.permutation(early_key, TOK_DEV - 1)[:3] + 1
        late_starts = jax.random.permutation(late_key, TOK_DEV - 2)[:3] + (length - TOK_DEV + 1)
        final_start = jnp.full((1,), length - 1, jnp.int32)
        return jnp.concatenate([jnp.zeros((1,), jnp.int32), jnp.sort(early_starts).astype(jnp.int32), jnp.sort(late_starts).astype(jnp.int32), final_start]).astype(jnp.int32)
    return jax.vmap(one_stream)(jax.random.split(key, STREAMS))


def raised(drawn, key, source, target, parts, factor):
    def block_of(axis_at):
        return (jnp.arange(drawn.shape[axis_at]) // (drawn.shape[axis_at] // parts)).reshape((-1,) + (1,) * (drawn.ndim - 1 - axis_at))

    near = jax.random.permutation(key, parts)[block_of(target)]
    far = (block_of(target) + parts // 2) % parts
    return jnp.where((block_of(source) == near) | (block_of(source) == far), factor * drawn, drawn)


def steps_of(own_key, extent, cuts, low, high):
    level, own = 1.0, jax.random.fold_in(own_key, 6)
    for axis_at, blocks in cuts:
        heights = jnp.exp(jax.random.uniform(jax.random.fold_in(own, axis_at), (blocks,), jnp.float32, low / len(cuts), high / len(cuts)))
        level = level * jnp.repeat(heights, extent[axis_at] // blocks).reshape([-1 if axis == axis_at else 1 for axis in range(len(extent))])
    return level


def normal_values(own_key, shape, scale, reach, cuts=(), held_as=jnp.bfloat16):
    result = jax.random.normal(own_key, shape, jnp.float32) * scale
    if len(cuts) > 0:
        result = steps_of(own_key, shape, cuts, -0.22, 0.18) * result
    return jnp.clip(result, min=-reach, max=reach).astype(held_as)


def bell_draw_with(key, shape, width, bound, cuts, heavy, kind=jnp.bfloat16):
    drawn = width * jax.random.normal(key, shape, jnp.float32)
    if cuts:
        drawn = drawn * steps_of(key, shape, cuts, -0.22, 0.18)
    return jnp.clip(raised(drawn, jax.random.fold_in(key, 3), *heavy), -bound, bound).astype(kind)


def setup_inputs(seed: int = 0) -> dict:
    streams_of = jax.random.split(jax.random.key(seed), 13)
    return {
        "tokens": normal_values(streams_of[0], (STREAMS, STREAM_LEN, D), 1.0, 6.0, ((0, 2), (1, 8))),
        "doc_starts": draw_doc_starts(jax.random.fold_in(streams_of[12], 71), 0),
        "query_weight": normal_values(streams_of[2], (D, D), D ** -0.5, 0.125, ((0, 16), (1, 2))),
        "key_weight": normal_values(streams_of[3], (D, D), D ** -0.5, 0.125, ((0, 16), (1, 2))),
        "value_weight": normal_values(streams_of[4], (D, D), D ** -0.5, 0.125, ((0, 16), (1, 2))),
        "out_weight": normal_values(streams_of[5], (D, D), (HEAD_DIM // 4) ** -0.5, 1.0, ((0, 2), (1, 16))),
        "gate_weight": normal_values(streams_of[6], (D, FF), D ** -0.5, 0.125, ((0, 16), (1, 2))),
        "up_weight": normal_values(streams_of[7], (D, FF), D ** -0.5, 0.125, ((0, 16), (1, 2))),
        "down_weight": normal_values(streams_of[8], (FF, D), FF ** -0.5, 0.078125, ((0, 2), (1, 16))),
        "attention_gain": jnp.clip(1.0 + 0.15 * jax.random.normal(streams_of[9], (D,), jnp.float32), 0.25, 1.75).astype(jnp.bfloat16),
        "feedforward_gain": jnp.clip(1.0 + 0.15 * jax.random.normal(streams_of[10], (D,), jnp.float32), 0.25, 1.75).astype(jnp.bfloat16),
        "cotangent": bell_draw_with(streams_of[11], (STREAMS, STREAM_LEN, D), 1.0, 6.0, ((0, 2), (1, 8)), (1, 2, 8, 2.0)),
    }


@jax.custom_vjp
def low(v):
    return lax.optimization_barrier(v.astype(jnp.bfloat16)).astype(jnp.float32)

@jax.custom_vjp
def low_back(v):
    return v

def low_keep(v):
    return (low(v), None)

def low_pass(kept, grad):
    return (grad,)

def back_keep(v):
    return (v, None)

def back_low(kept, grad):
    return (low(grad),)
low.defvjp(low_keep, low_pass)
low_back.defvjp(back_keep, back_low)
epsilon = 1e-06
masked_score = -1e+30

def matmul(left, right):
    return jnp.dot(left, right, preferred_element_type=jnp.float32, precision=lax.Precision.HIGHEST)

def rotary_tables(positions):
    half_dim = HEAD_DIM // 2
    frequency = jnp.exp(jnp.arange(half_dim).astype(jnp.float32) * (-2.0 * math.log(10000.0) / HEAD_DIM))
    angles = positions.astype(jnp.float32)[:, None] * frequency[None, :]
    return (jnp.cos(angles), jnp.sin(angles))

def rotate_pairs(values, cosine, sine_table):
    half_dim = values.shape[-1] // 2
    first_half = values[..., :half_dim]
    second_half = values[..., half_dim:]
    return jnp.concatenate([first_half * cosine - second_half * sine_table, second_half * cosine + first_half * sine_table], axis=-1)

def block_forward(inputs, query_weight, key_weight, value_weight, out_weight, gate_weight, up_weight, down_weight, attention_gain, feedforward_gain, starts):
    length = inputs.shape[0]
    block_rows = min(512, length)
    positions = jnp.arange(length, dtype=jnp.int32)
    documents = lax.optimization_barrier(jnp.sum((starts[None, :] <= positions[:, None]).astype(jnp.int32), axis=1))
    scale_first = lax.rsqrt(lax.optimization_barrier(jnp.mean(inputs * inputs, axis=-1, keepdims=True)) + epsilon)
    normed = low(inputs * scale_first * attention_gain)
    query_proj = low_back(matmul(normed, query_weight)).reshape(length, HEADS, HEAD_DIM)
    key_proj = low_back(matmul(normed, key_weight)).reshape(length, HEADS, HEAD_DIM)
    value_proj = low_back(matmul(normed, value_weight)).reshape(length, HEADS, HEAD_DIM)
    cosine, sine_table = rotary_tables(positions)
    cosine = cosine[:, None, :]
    sine_table = sine_table[:, None, :]
    query_rot = low(rotate_pairs(query_proj, cosine, sine_table) * HEAD_DIM ** (-0.5))
    key_rot = low(rotate_pairs(key_proj, cosine, sine_table))
    value_low = low(value_proj)

    def attend(row_start):
        query_block = lax.dynamic_slice_in_dim(query_rot, row_start, block_rows, 0)
        block_positions = row_start + jnp.arange(block_rows, dtype=jnp.int32)
        block_docs = lax.dynamic_slice_in_dim(documents, row_start, block_rows, 0)
        scores = low_back(jnp.einsum('qhe,khe->hqk', query_block, key_rot, precision=lax.Precision.HIGHEST))
        offsets = block_positions[:, None] - positions[None, :]
        allowed = (offsets >= 0) & (offsets < WIN) & (block_docs[:, None] == documents[None, :])
        scores = jnp.where(allowed[None], scores, masked_score)
        largest = lax.optimization_barrier(jnp.max(scores, axis=-1, keepdims=True))
        weights = jnp.exp(scores - largest)
        probability = weights / lax.optimization_barrier(jnp.sum(weights, axis=-1, keepdims=True))
        return jnp.einsum('hqk,khe->qhe', low(probability), value_low, precision=lax.Precision.HIGHEST)
    block_starts = (jnp.arange(length // block_rows, dtype=jnp.int32) * block_rows).astype(jnp.int32)
    attended = lax.map(jax.checkpoint(attend), block_starts).reshape(length, HEADS * HEAD_DIM)
    heads_out = low(low_back(attended))
    branch = low_back(matmul(heads_out, out_weight))
    residual = inputs + branch
    scale_second = lax.rsqrt(lax.optimization_barrier(jnp.mean(residual * residual, axis=-1, keepdims=True)) + epsilon)
    normed_ffn = low(residual * scale_second * feedforward_gain)
    gate_proj = low_back(matmul(normed_ffn, gate_weight))
    up_proj = low_back(matmul(normed_ffn, up_weight))
    mixed_hidden = low(jax.nn.silu(gate_proj) * up_proj)
    return residual + matmul(mixed_hidden, down_weight)

def reference(tokens, doc_starts, query_weight, key_weight, value_weight, out_weight, gate_weight, up_weight, down_weight, attention_gain, feedforward_gain, cotangent):
    float_weights = tuple((weight.astype(jnp.float32) for weight in (query_weight, key_weight, value_weight, out_weight, gate_weight, up_weight, down_weight, attention_gain, feedforward_gain)))

    def stream_step(totals, stream):
        stream_tokens, stream_starts, stream_cotangent = stream

        def forward(inputs, *weight_list):
            return block_forward(inputs, *weight_list, stream_starts)
        output, pullback = jax.vjp(forward, stream_tokens.astype(jnp.float32), *float_weights)
        gradients = pullback(stream_cotangent.astype(jnp.float32))
        totals = tuple((summed + gradient for summed, gradient in zip(totals, gradients[1:])))
        return (totals, (output.astype(jnp.bfloat16), gradients[0]))
    zeros = tuple((jnp.zeros(weight.shape, jnp.float32) for weight in float_weights))
    totals, (output, grad_tokens) = lax.scan(stream_step, zeros, (tokens, doc_starts, cotangent))
    return (output, grad_tokens, totals[0], totals[1], totals[2], totals[3], totals[4], totals[5], totals[6], totals[7], totals[8])
```

```python
import math

import jax
import jax.numpy as jnp
from jax import lax
from jax.experimental import pallas as pl
from jax.experimental.pallas import tpu as pltpu
from jax.sharding import Mesh
from jax.sharding import PartitionSpec as P

HEAD_DIM = 128
WIN = 2048


epsilon = 1e-06
masked_score = -1e30


def from_behind(value, axis, steps):
    count = lax.axis_size(axis)
    initial, last = (max(0, -steps), min(count, count - steps))
    return lax.ppermute(value, axis, [(source, source + steps) for source in range(initial, last)])


def matmul(left, right):
    return jnp.dot(left, right, preferred_element_type=jnp.float32)


def contract_rows(left, right):
    return lax.dot_general(
        left, right, (((0,), (0,)), ((), ())), preferred_element_type=jnp.float32
    )


def contract_cols(left, right):
    return lax.dot_general(
        left, right, (((1,), (1,)), ((), ())), preferred_element_type=jnp.float32
    )


def rotary_tables(positions):
    half_dim = HEAD_DIM // 2
    frequency = jnp.exp(
        jnp.arange(half_dim).astype(jnp.float32) * (-2.0 * math.log(10000.0) / HEAD_DIM)
    )
    angles = positions.astype(jnp.float32)[:, None] * frequency[None, :]
    return (jnp.cos(angles), jnp.sin(angles))


def rotate_pairs(values, cosine, sine_table):
    half_dim = values.shape[-1] // 2
    first_half = values[..., :half_dim]
    second_half = values[..., half_dim:]
    return jnp.concatenate(
        [
            first_half * cosine - second_half * sine_table,
            second_half * cosine + first_half * sine_table,
        ],
        axis=-1,
    )


def unrotate_pairs(values, cosine, sine_table):
    half_dim = values.shape[-1] // 2
    first_half = values[..., :half_dim]
    second_half = values[..., half_dim:]
    return jnp.concatenate(
        [
            first_half * cosine + second_half * sine_table,
            second_half * cosine - first_half * sine_table,
        ],
        axis=-1,
    )


def document_number(starts, positions):
    return jnp.sum((starts[:, None, :] <= positions[None, :, None]).astype(jnp.int32), axis=2)


def rms_scale(values):
    return lax.rsqrt(jnp.mean(values * values, axis=-1, keepdims=True) + epsilon)


def norm_backward(grad_normed, inputs, row_scale, gain_vector):
    gain_grad = jnp.sum(grad_normed * inputs * row_scale, axis=0)
    weighted = grad_normed * gain_vector
    grad_inputs = row_scale * weighted - inputs * row_scale**3 * jnp.mean(
        weighted * inputs, axis=-1, keepdims=True
    )
    return (grad_inputs, gain_grad)


def per_device(
    tokens,
    doc_starts,
    query_weight,
    key_weight,
    value_weight,
    out_weight,
    gate_weight,
    up_weight,
    down_weight,
    attention_gain,
    feedforward_gain,
    cotangent,
):
    gathered = (
        lax.all_gather(query_weight, ("stream", "seq"), axis=0, tiled=True),
        lax.all_gather(key_weight, ("stream", "seq"), axis=0, tiled=True),
        lax.all_gather(value_weight, ("stream", "seq"), axis=0, tiled=True),
        lax.all_gather(out_weight, ("stream", "seq"), axis=1, tiled=True),
        lax.all_gather(gate_weight, ("stream", "seq"), axis=0, tiled=True),
        lax.all_gather(up_weight, ("stream", "seq"), axis=0, tiled=True),
        lax.all_gather(down_weight, ("stream", "seq"), axis=1, tiled=True),
        lax.all_gather(attention_gain, ("stream", "seq"), axis=0, tiled=True),
        lax.all_gather(feedforward_gain, ("stream", "seq"), axis=0, tiled=True),
    )
    (
        full_query,
        full_key,
        full_value,
        full_out,
        full_gate,
        full_up,
        full_down,
        full_gain_first,
        full_gain_second,
    ) = gathered
    streams, shard_rows, model_width = tokens.shape
    head_width = full_query.shape[1]
    local_heads = head_width // HEAD_DIM
    flat_rows = streams * shard_rows
    seq_index = lax.axis_index("seq")
    halo_shards = min(WIN // shard_rows, lax.axis_size("seq") - 1)
    window_rows = (halo_shards + 1) * shard_rows
    inputs = tokens.reshape(flat_rows, model_width).astype(jnp.float32)
    scale_first = rms_scale(inputs)
    gain_first = full_gain_first.astype(jnp.float32)
    normed = (inputs * scale_first * gain_first).astype(jnp.bfloat16)
    query_proj = matmul(normed, full_query).reshape(streams, shard_rows, local_heads, HEAD_DIM)
    key_proj = matmul(normed, full_key).reshape(streams, shard_rows, local_heads, HEAD_DIM)
    value_low = (
        matmul(normed, full_value).astype(jnp.bfloat16).reshape(streams, shard_rows, head_width)
    )
    positions = seq_index * shard_rows + jnp.arange(shard_rows, dtype=jnp.int32)
    cosine, sine_table = rotary_tables(positions)
    cosine = cosine[None, :, None, :]
    sine_table = sine_table[None, :, None, :]
    query_rot = (rotate_pairs(query_proj, cosine, sine_table) * HEAD_DIM ** (-0.5)).astype(
        jnp.bfloat16
    )
    key_rot = rotate_pairs(key_proj, cosine, sine_table).astype(jnp.bfloat16)
    paired = jnp.stack([key_rot.reshape(streams, shard_rows, head_width), value_low])
    pieces = []
    for distance in range(halo_shards, 0, -1):
        pieces.append(from_behind(paired, "seq", distance))
    window = jnp.concatenate(pieces + [paired], axis=2)
    key_positions = (seq_index - halo_shards) * shard_rows + jnp.arange(
        window_rows, dtype=jnp.int32
    )
    query_docs = document_number(doc_starts, positions)
    key_docs = document_number(doc_starts, key_positions)
    offsets = positions[:, None] - key_positions[None, :]
    allowed = ((offsets >= 0) & (offsets < WIN))[None] & (
        query_docs[:, :, None] == key_docs[:, None, :]
    )
    query_heads = jnp.transpose(query_rot, (2, 0, 1, 3))
    key_heads = jnp.transpose(
        window[0].reshape(streams, window_rows, local_heads, HEAD_DIM), (2, 0, 1, 3)
    )
    value_heads = jnp.transpose(
        window[1].reshape(streams, window_rows, local_heads, HEAD_DIM), (2, 0, 1, 3)
    )

    def head_forward(operands):
        query_one, key_one, value_one = operands
        scores = jnp.einsum("sqe,ske->sqk", query_one, key_one, preferred_element_type=jnp.float32)
        scores = jnp.where(allowed, scores, masked_score)
        largest = jnp.max(scores, axis=-1, keepdims=True)
        weights = jnp.exp(scores - largest)
        totals = jnp.sum(weights, axis=-1, keepdims=True)
        probability = (weights / totals).astype(jnp.bfloat16)
        attended = jnp.einsum(
            "sqk,ske->sqe", probability, value_one, preferred_element_type=jnp.float32
        )
        return (attended, (largest + jnp.log(totals))[..., 0])

    attended, log_totals = lax.map(head_forward, (query_heads, key_heads, value_heads))
    heads_out = (
        jnp.transpose(attended, (1, 2, 0, 3)).reshape(flat_rows, head_width).astype(jnp.bfloat16)
    )
    attention_sum = lax.psum(matmul(heads_out, full_out), "head")
    residual = inputs + attention_sum
    scale_second = rms_scale(residual)
    gain_second = full_gain_second.astype(jnp.float32)
    normed_ffn = (residual * scale_second * gain_second).astype(jnp.bfloat16)
    gate_proj = matmul(normed_ffn, full_gate)
    up_proj = matmul(normed_ffn, full_up)
    sigmoid_gate = jax.nn.sigmoid(gate_proj)
    silu_gate = gate_proj * sigmoid_gate
    mixed_hidden = (silu_gate * up_proj).astype(jnp.bfloat16)
    feedforward_sum = lax.psum(matmul(mixed_hidden, full_down).astype(jnp.bfloat16), "head").astype(
        jnp.float32
    )
    output = (
        (residual + feedforward_sum).astype(jnp.bfloat16).reshape(streams, shard_rows, model_width)
    )
    gathered = (
        lax.all_gather(query_weight, ("stream", "seq"), axis=0, tiled=True),
        lax.all_gather(key_weight, ("stream", "seq"), axis=0, tiled=True),
        lax.all_gather(value_weight, ("stream", "seq"), axis=0, tiled=True),
        lax.all_gather(out_weight, ("stream", "seq"), axis=1, tiled=True),
        lax.all_gather(gate_weight, ("stream", "seq"), axis=0, tiled=True),
        lax.all_gather(up_weight, ("stream", "seq"), axis=0, tiled=True),
        lax.all_gather(down_weight, ("stream", "seq"), axis=1, tiled=True),
        lax.all_gather(attention_gain, ("stream", "seq"), axis=0, tiled=True),
        lax.all_gather(feedforward_gain, ("stream", "seq"), axis=0, tiled=True),
    )
    (
        full_query,
        full_key,
        full_value,
        full_out,
        full_gate,
        full_up,
        full_down,
        full_gain_first,
        full_gain_second,
    ) = gathered
    grad_output = cotangent.reshape(flat_rows, model_width)
    grad_down = contract_rows(mixed_hidden, grad_output)
    grad_mixed = contract_cols(grad_output, full_down)
    grad_gate_low = (
        grad_mixed * up_proj * sigmoid_gate * (1.0 + gate_proj * (1.0 - sigmoid_gate))
    ).astype(jnp.bfloat16)
    grad_up_low = (grad_mixed * silu_gate).astype(jnp.bfloat16)
    grad_gate_w = contract_rows(normed_ffn, grad_gate_low)
    grad_up_w = contract_rows(normed_ffn, grad_up_low)
    grad_normed_ffn = lax.psum(
        contract_cols(grad_gate_low, full_gate) + contract_cols(grad_up_low, full_up), "head"
    )
    grad_residual_norm, grad_gain_second = norm_backward(
        grad_normed_ffn, residual, scale_second, gain_second
    )
    grad_residual = grad_output.astype(jnp.float32) + grad_residual_norm
    grad_branch = grad_residual.astype(jnp.bfloat16)
    grad_out_w = contract_rows(heads_out, grad_branch)
    grad_heads = contract_cols(grad_branch, full_out).astype(jnp.bfloat16)
    grad_heads_major = jnp.transpose(
        grad_heads.reshape(streams, shard_rows, local_heads, HEAD_DIM), (2, 0, 1, 3)
    )

    def head_backward(operands):
        query_one, key_one, value_one, grad_one, log_one = operands
        scores = jnp.einsum("sqe,ske->sqk", query_one, key_one, preferred_element_type=jnp.float32)
        scores = jnp.where(allowed, scores, masked_score)
        probability = jnp.exp(scores - log_one[..., None])
        grad_prob = jnp.einsum(
            "sqe,ske->sqk", grad_one, value_one, preferred_element_type=jnp.float32
        )
        centre = jnp.sum(probability * grad_prob, axis=-1, keepdims=True)
        grad_scores = (probability * (grad_prob - centre)).astype(jnp.bfloat16)
        grad_query_one = jnp.einsum(
            "sqk,ske->sqe", grad_scores, key_one, preferred_element_type=jnp.float32
        )
        grad_key_one = jnp.einsum(
            "sqk,sqe->ske", grad_scores, query_one, preferred_element_type=jnp.float32
        )
        grad_value_one = jnp.einsum(
            "sqk,sqe->ske",
            probability.astype(jnp.bfloat16),
            grad_one,
            preferred_element_type=jnp.float32,
        )
        return (grad_query_one, grad_key_one, grad_value_one)

    grad_query_heads, grad_key_heads, grad_value_heads = lax.map(
        head_backward, (query_heads, key_heads, value_heads, grad_heads_major, log_totals)
    )
    grad_window = jnp.transpose(
        jnp.stack([grad_key_heads, grad_value_heads]), (0, 2, 3, 1, 4)
    ).reshape(2, streams, window_rows, head_width)
    grad_paired = grad_window[:, :, halo_shards * shard_rows :]
    for distance in range(halo_shards, 0, -1):
        index_piece = halo_shards - distance
        grad_paired = grad_paired + from_behind(
            grad_window[:, :, index_piece * shard_rows : (index_piece + 1) * shard_rows],
            "seq",
            -distance,
        )
    grad_key_rot = grad_paired[0].reshape(streams, shard_rows, local_heads, HEAD_DIM)
    grad_query_rot = jnp.transpose(grad_query_heads, (1, 2, 0, 3))
    grad_query_low = (
        (unrotate_pairs(grad_query_rot, cosine, sine_table) * HEAD_DIM ** (-0.5))
        .reshape(flat_rows, head_width)
        .astype(jnp.bfloat16)
    )
    grad_key_low = (
        unrotate_pairs(grad_key_rot, cosine, sine_table)
        .reshape(flat_rows, head_width)
        .astype(jnp.bfloat16)
    )
    grad_value_low = grad_paired[1].reshape(flat_rows, head_width).astype(jnp.bfloat16)
    grad_query_w = contract_rows(normed, grad_query_low)
    grad_key_w = contract_rows(normed, grad_key_low)
    grad_value_w = contract_rows(normed, grad_value_low)
    grad_normed = lax.psum(
        contract_cols(grad_query_low, full_query)
        + contract_cols(grad_key_low, full_key)
        + contract_cols(grad_value_low, full_value),
        "head",
    )
    grad_inputs_norm, grad_gain_first = norm_backward(grad_normed, inputs, scale_first, gain_first)
    grad_tokens = (grad_residual + grad_inputs_norm).reshape(streams, shard_rows, model_width)
    reduced = (
        lax.psum_scatter(grad_query_w, ("stream", "seq"), scatter_dimension=0, tiled=True),
        lax.psum_scatter(grad_key_w, ("stream", "seq"), scatter_dimension=0, tiled=True),
        lax.psum_scatter(grad_value_w, ("stream", "seq"), scatter_dimension=0, tiled=True),
        lax.psum_scatter(grad_out_w, ("stream", "seq"), scatter_dimension=1, tiled=True),
        lax.psum_scatter(grad_gate_w, ("stream", "seq"), scatter_dimension=0, tiled=True),
        lax.psum_scatter(grad_up_w, ("stream", "seq"), scatter_dimension=0, tiled=True),
        lax.psum_scatter(grad_down, ("stream", "seq"), scatter_dimension=1, tiled=True),
        lax.psum_scatter(grad_gain_first, ("stream", "seq"), scatter_dimension=0, tiled=True),
        lax.psum_scatter(grad_gain_second, ("stream", "seq"), scatter_dimension=0, tiled=True),
    )
    return (
        output,
        grad_tokens,
        reduced[0],
        reduced[1],
        reduced[2],
        reduced[3],
        reduced[4],
        reduced[5],
        reduced[6],
        reduced[7],
        reduced[8],
    )


GROUP = ("zl", "y", "c")
SQUARE = ("zl", "y")
MEMBERS = 8
QUARTERS = 4


def swap(value, axis):
    return lax.ppermute(value, axis, [(0, 1), (1, 0)])


def attention_forward_kernel(query, key, value, first, attended, log_total):
    tile = pl.program_id(1)
    rows = query.shape[0]
    query_tile = query[...]
    first_key = first[...]
    row_index = lax.broadcasted_iota(jnp.int32, (rows, rows), 0)
    column_index = lax.broadcasted_iota(jnp.int32, (rows, rows), 1)

    def block(index, carry, diagonal):
        largest, total, summed = carry
        at = pl.ds(pl.multiple_of(index * rows, rows), rows)
        scores = contract_cols(query_tile, key[at, :])
        visible = column_index + index * rows >= first_key
        if diagonal:
            visible = visible & (column_index <= row_index)
        scores = jnp.where(visible, scores, masked_score)
        new_largest = jnp.maximum(largest, jnp.max(scores, axis=1, keepdims=True))
        weights = jnp.where(visible, jnp.exp(scores - new_largest), 0.0)
        scaling = jnp.exp(largest - new_largest)
        total = total * scaling + jnp.sum(weights, axis=1, keepdims=True)
        summed = summed * scaling + matmul(weights.astype(jnp.bfloat16), value[at, :])
        return (new_largest, total, summed)

    carry = (
        jnp.full((rows, 1), masked_score, jnp.float32),
        jnp.zeros((rows, 1), jnp.float32),
        jnp.zeros((rows, HEAD_DIM), jnp.float32),
    )
    carry = lax.fori_loop(0, tile, lambda index, kept: block(index, kept, False), carry)
    largest, total, summed = block(tile, carry, True)
    attended[...] = summed / total
    log_total[0, :, :] = jnp.broadcast_to(
        jnp.transpose(largest + jnp.log(total)), log_total.shape[1:]
    )


def attention_forward(query, key, value, first_key, tile_rows):
    length, width = query.shape
    heads = width // HEAD_DIM
    whole = pl.BlockSpec((length, HEAD_DIM), lambda head, tile: (0, head))
    part = pl.BlockSpec((tile_rows, HEAD_DIM), lambda head, tile: (tile, head))
    return pl.pallas_call(
        attention_forward_kernel,
        grid=(heads, length // tile_rows),
        in_specs=[
            part,
            whole,
            whole,
            pl.BlockSpec((tile_rows, 1), lambda head, tile: (tile, 0)),
        ],
        out_specs=[part, pl.BlockSpec((1, 8, tile_rows), lambda head, tile: (head, 0, tile))],
        out_shape=[
            jax.ShapeDtypeStruct((length, width), jnp.float32),
            jax.ShapeDtypeStruct((heads, 8, length), jnp.float32),
        ],
        compiler_params=pltpu.CompilerParams(vmem_limit_bytes=48 * 1024 * 1024),
        cost_estimate=pl.CostEstimate(
            flops=2 * length * length * width,
            bytes_accessed=10 * length * width,
            transcendentals=length * length * heads // 2,
        ),
        name="attention_forward",
    )(query, key, value, first_key)


def attention_backward_kernel(
    query, key, value, grad, centre, log_total, first, grad_query, grad_key, grad_value
):
    tile = pl.program_id(1)
    rows = query.shape[0]
    query_tile = query[...]
    grad_tile = grad[...]
    centre_row = centre[0, :1, :]
    log_row = log_total[0, :1, :]
    first_row = first[:1, :]
    key_index = lax.broadcasted_iota(jnp.int32, (rows, rows), 0)
    query_index = lax.broadcasted_iota(jnp.int32, (rows, rows), 1)

    def block(index, summed, diagonal):
        at = pl.ds(pl.multiple_of(index * rows, rows), rows)
        key_block = key[at, :]
        scores = contract_cols(key_block, query_tile)
        visible = key_index + index * rows >= first_row
        if diagonal:
            visible = visible & (key_index <= query_index)
        probability = jnp.where(visible, jnp.exp(scores - log_row), 0.0)
        grad_prob = contract_cols(value[at, :], grad_tile)
        grad_scores = (probability * (grad_prob - centre_row)).astype(jnp.bfloat16)
        key_part = matmul(grad_scores, query_tile)
        value_part = matmul(probability.astype(jnp.bfloat16), grad_tile)
        if diagonal:
            grad_key[at, :] = key_part
            grad_value[at, :] = value_part
        else:
            grad_key[at, :] += key_part
            grad_value[at, :] += value_part
        return summed + contract_rows(grad_scores, key_block)

    summed = lax.fori_loop(
        0,
        tile,
        lambda index, kept: block(index, kept, False),
        jnp.zeros((rows, HEAD_DIM), jnp.float32),
    )
    grad_query[...] = block(tile, summed, True)


def attention_backward(query, key, value, grad, centre, log_total, first_key, tile_rows):
    length, width = query.shape
    heads = width // HEAD_DIM
    whole = pl.BlockSpec((length, HEAD_DIM), lambda head, tile: (0, head))
    part = pl.BlockSpec((tile_rows, HEAD_DIM), lambda head, tile: (tile, head))
    row = pl.BlockSpec((1, 8, tile_rows), lambda head, tile: (head, 0, tile))
    shape = jax.ShapeDtypeStruct((length, width), jnp.float32)
    return pl.pallas_call(
        attention_backward_kernel,
        grid=(heads, length // tile_rows),
        in_specs=[
            part,
            whole,
            whole,
            part,
            row,
            row,
            pl.BlockSpec((8, tile_rows), lambda head, tile: (0, tile)),
        ],
        out_specs=[part, whole, whole],
        out_shape=[shape, shape, shape],
        compiler_params=pltpu.CompilerParams(vmem_limit_bytes=48 * 1024 * 1024),
        cost_estimate=pl.CostEstimate(
            flops=5 * length * length * width,
            bytes_accessed=24 * length * width,
            transcendentals=length * length * heads // 2,
        ),
        name="attention_backward",
    )(query, key, value, grad, centre, log_total, first_key)


def group_device(
    tokens,
    doc_starts,
    query_weight,
    key_weight,
    value_weight,
    out_weight,
    gate_weight,
    up_weight,
    down_weight,
    attention_gain,
    feedforward_gain,
    cotangent,
):
    bf16, f32 = jnp.bfloat16, jnp.float32
    x_at, zh_at, core = (lax.axis_index(name) for name in ("x", "zh", "c"))
    streams, shard_rows, model_width = tokens.shape
    slice_width = query_weight.shape[0]
    half_rows = shard_rows // 2
    own_rows = 2 * half_rows
    length = MEMBERS * own_rows
    block_width = QUARTERS * slice_width
    head_width = query_weight.shape[1] // QUARTERS
    hidden = gate_weight.shape[1] // QUARTERS
    local_heads = head_width // HEAD_DIM

    def reorder(values):
        quarters = [values[..., i * block_width : (i + 1) * block_width] for i in range(4)]
        even = zh_at == 0
        pairs = [
            jnp.where(even, quarters[i], quarters[i ^ 1]) for i in range(4)
        ]
        near = x_at == 0
        return jnp.concatenate([jnp.where(near, pairs[i], pairs[i ^ 2]) for i in range(4)], axis=-1)

    def to_group(values):
        mine = lax.dynamic_slice_in_dim(values, core * half_rows, half_rows, 1)
        keep = lax.dynamic_index_in_dim(mine, zh_at, 0, keepdims=False)
        got = swap(lax.dynamic_index_in_dim(mine, 1 - zh_at, 0, keepdims=False), "zh")
        even = zh_at == 0
        return reorder(jnp.stack([jnp.where(even, keep, got), jnp.where(even, got, keep)]))

    def from_group(values):
        keep = lax.dynamic_index_in_dim(values, zh_at, 0, keepdims=False)
        got = swap(lax.dynamic_index_in_dim(values, 1 - zh_at, 0, keepdims=False).astype(bf16), "zh")
        got = got.astype(values.dtype)
        even = zh_at == 0
        mine = jnp.stack([jnp.where(even, keep, got), jnp.where(even, got, keep)])
        other = swap(mine, "c")
        first = core == 0
        return jnp.concatenate(
            [jnp.where(first, mine, other), jnp.where(first, other, mine)], axis=1
        )

    def gather_rows(values):
        return lax.all_gather(values, GROUP, axis=1, tiled=True).reshape(length, model_width)

    def scatter_rows(values):
        return lax.psum_scatter(
            values.astype(bf16).reshape(2, length // 2, model_width),
            GROUP,
            scatter_dimension=1,
            tiled=True,
        ).reshape(own_rows, model_width)

    def gather_units(parts):
        units = jnp.concatenate(parts, axis=1)
        got = lax.all_to_all(units, SQUARE, 0, 0)
        near = jnp.concatenate([got[i] for i in range(QUARTERS)], axis=1)
        other = swap(near, "zh")
        return jnp.concatenate([near, other, swap(near, "x"), swap(other, "x")], axis=1)

    def reduce_units(grads):
        width = 2 * block_width
        near = grads[:, :width] + swap(grads[:, width:].astype(bf16), "x").astype(f32)
        own = near[:, :block_width] + swap(near[:, block_width:].astype(bf16), "zh").astype(f32)
        own = own.astype(bf16)
        parts = jnp.stack(
            [own[:, i * slice_width : (i + 1) * slice_width] for i in range(QUARTERS)]
        )
        return lax.all_to_all(parts, SQUARE, 0, 0).astype(f32)

    def units_of(weight):
        return weight.reshape(QUARTERS, -1, slice_width)

    gains = jnp.concatenate(
        [attention_gain[None], feedforward_gain[None], jnp.zeros((14, slice_width), bf16)]
    )
    gains = jnp.broadcast_to(gains[None], (QUARTERS, 16, slice_width))
    own_tokens = to_group(tokens)
    all_tokens = gather_rows(own_tokens)
    attention_units = gather_units(
        [
            units_of(query_weight.T),
            units_of(key_weight.T),
            units_of(value_weight.T),
            units_of(out_weight),
            gains,
        ]
    )
    pair_units = gather_units([units_of(gate_weight.T), units_of(up_weight.T)])
    down_units = gather_units([units_of(down_weight)])
    own_cotangent = to_group(cotangent)
    all_cotangent = gather_rows(own_cotangent)

    qkv_units = attention_units[: 3 * head_width]
    out_units = attention_units[3 * head_width : 4 * head_width]
    gain_first = attention_units[4 * head_width].astype(f32)
    gain_second = attention_units[4 * head_width + 1].astype(f32)
    gate_units = pair_units[:hidden]
    up_units = pair_units[hidden:]

    all_inputs = all_tokens.astype(f32)
    normed = (all_inputs * rms_scale(all_inputs) * gain_first).astype(bf16)
    inputs = own_tokens.reshape(own_rows, model_width).astype(f32)
    scale_first = rms_scale(inputs)

    positions = jnp.arange(length, dtype=jnp.int32)
    cosine, sine_table = rotary_tables(positions)
    cosine = cosine[:, None, :]
    sine_table = sine_table[:, None, :]
    starts = lax.dynamic_index_in_dim(doc_starts, zh_at, 0, keepdims=False)
    first_key = jnp.max(
        jnp.where(starts[None, :] <= positions[:, None], starts[None, :], 0), axis=1
    )

    projected = contract_cols(normed, qkv_units)
    query_proj, key_proj, value_proj = (
        projected[:, i * head_width : (i + 1) * head_width] for i in range(3)
    )
    by_head = (length, local_heads, HEAD_DIM)
    query_rot = (
        (rotate_pairs(query_proj.reshape(by_head), cosine, sine_table) * HEAD_DIM ** (-0.5))
        .astype(bf16)
        .reshape(length, head_width)
    )
    key_rot = (
        rotate_pairs(key_proj.reshape(by_head), cosine, sine_table)
        .astype(bf16)
        .reshape(length, head_width)
    )
    value_low = value_proj.astype(bf16)
    tile_rows = min(512, length)
    attended, log_total = attention_forward(
        query_rot, key_rot, value_low, first_key[:, None], tile_rows
    )
    heads_out = attended.astype(bf16)
    branch = scatter_rows(matmul(heads_out, out_units)).astype(f32)
    residual = inputs + branch
    scale_second = rms_scale(residual)
    normed_own = (residual * scale_second * gain_second).astype(bf16)
    normed_ffn = gather_rows(normed_own.reshape(2, half_rows, model_width))

    gate_proj = contract_cols(normed_ffn, gate_units)
    up_proj = contract_cols(normed_ffn, up_units)
    sigmoid_gate = jax.nn.sigmoid(gate_proj)
    silu_gate = gate_proj * sigmoid_gate
    mixed_hidden = (silu_gate * up_proj).astype(bf16)
    grad_mixed = contract_cols(all_cotangent, down_units)
    grad_gate_low = (
        grad_mixed * up_proj * sigmoid_gate * (1.0 + gate_proj * (1.0 - sigmoid_gate))
    ).astype(bf16)
    grad_up_low = (grad_mixed * silu_gate).astype(bf16)
    grad_normed_ffn = scatter_rows(
        matmul(grad_gate_low, gate_units) + matmul(grad_up_low, up_units)
    ).astype(f32)
    feedforward = scatter_rows(matmul(mixed_hidden, down_units)).astype(f32)
    output = from_group(
        reorder((residual + feedforward).astype(bf16)).reshape(2, half_rows, model_width)
    )
    grad_down = reduce_units(contract_rows(mixed_hidden, all_cotangent))
    grad_pair = reduce_units(
        jnp.concatenate(
            [contract_rows(grad_gate_low, normed_ffn), contract_rows(grad_up_low, normed_ffn)]
        )
    )

    weighted = grad_normed_ffn * gain_second
    grad_residual = (
        own_cotangent.reshape(own_rows, model_width).astype(f32)
        + scale_second * weighted
        - residual * scale_second**3 * jnp.mean(weighted * residual, axis=-1, keepdims=True)
    )
    grad_branch = gather_rows(grad_residual.astype(bf16).reshape(2, half_rows, model_width))
    grad_out = contract_rows(heads_out, grad_branch)
    grad_heads = contract_cols(grad_branch, out_units).astype(bf16)
    centre = jnp.sum((grad_heads.astype(f32) * attended).reshape(by_head), axis=-1)
    centre = jnp.broadcast_to(jnp.transpose(centre)[:, None, :], (local_heads, 8, length))
    grad_query_rot, grad_key_rot, grad_value = attention_backward(
        query_rot,
        key_rot,
        value_low,
        grad_heads,
        centre,
        log_total,
        jnp.broadcast_to(first_key[None], (8, length)),
        tile_rows,
    )
    grad_query_low = (
        unrotate_pairs(grad_query_rot.reshape(by_head), cosine, sine_table) * HEAD_DIM ** (-0.5)
    )
    grad_key_low = unrotate_pairs(grad_key_rot.reshape(by_head), cosine, sine_table)
    grad_qkv = jnp.concatenate(
        [
            grad_query_low.reshape(length, head_width).astype(bf16),
            grad_key_low.reshape(length, head_width).astype(bf16),
            grad_value.astype(bf16),
        ],
        axis=1,
    )
    grad_normed = scatter_rows(matmul(grad_qkv, qkv_units)).astype(f32)
    grad_attention = reduce_units(
        jnp.concatenate([contract_rows(grad_qkv, normed), grad_out])
    )
    weighted = grad_normed * gain_first
    grad_own = (
        grad_residual
        + scale_first * weighted
        - inputs * scale_first**3 * jnp.mean(weighted * inputs, axis=-1, keepdims=True)
    )
    grad_tokens = from_group(reorder(grad_own).reshape(2, half_rows, model_width))

    def columns(grads, start, rows):
        return grads[:, start : start + rows].reshape(QUARTERS * rows, slice_width)

    grad_query_w = columns(grad_attention, 0, head_width).T
    grad_key_w = columns(grad_attention, head_width, head_width).T
    grad_value_w = columns(grad_attention, 2 * head_width, head_width).T
    grad_out_w = columns(grad_attention, 3 * head_width, head_width)
    grad_gate_w = columns(grad_pair, 0, hidden).T
    grad_up_w = columns(grad_pair, hidden, hidden).T
    grad_down_w = columns(grad_down, 0, hidden)

    def gain_sum(*pairs):
        return sum(jnp.sum(weight.astype(f32) * grad, axis=1) for weight, grad in pairs)

    sums = jnp.stack(
        [
            gain_sum(
                (query_weight, grad_query_w), (key_weight, grad_key_w), (value_weight, grad_value_w)
            ),
            gain_sum((gate_weight, grad_gate_w), (up_weight, grad_up_w)),
        ]
    )
    sums = sums + swap(sums, "c")
    return (
        output,
        grad_tokens,
        grad_query_w,
        grad_key_w,
        grad_value_w,
        grad_out_w,
        grad_gate_w,
        grad_up_w,
        grad_down_w,
        sums[0] / attention_gain.astype(f32),
        sums[1] / feedforward_gain.astype(f32),
    )


def placements(stream, seq, head):
    both = (stream + seq) if isinstance(stream, tuple) else (stream, seq)
    in_specs = (
        P(stream, seq, None),
        P(stream, None),
        P(both, head),
        P(both, head),
        P(both, head),
        P(head, both),
        P(both, head),
        P(both, head),
        P(head, both),
        P(both),
        P(both),
        P(stream, seq, None),
    )
    out_specs = (
        P(stream, seq, None),
        P(stream, seq, None),
        P(both, head),
        P(both, head),
        P(both, head),
        P(head, both),
        P(both, head),
        P(both, head),
        P(head, both),
        P(both),
        P(both),
    )
    return in_specs, out_specs


def solution(mesh):
    def run(*arguments):
        tokens, doc_starts = arguments[:2]
        sizes = dict(mesh.shape)
        grouped = (
            (sizes["stream"], sizes["seq"], sizes["head"]) == (2, 8, 2)
            and tokens.shape[0] == 4
            and tokens.shape[1] <= WIN
        )
        if grouped:
            split = Mesh(mesh.devices.reshape(2, 2, 2, 2, 2), ("x", "zh", "zl", "y", "c"))
            in_specs, out_specs = placements(("x",), ("zh", "zl", "y"), "c")
            step = group_device
        else:
            split = mesh
            in_specs, out_specs = placements("stream", "seq", "head")
            step = per_device
        return jax.shard_map(
            step, mesh=split, in_specs=in_specs, out_specs=out_specs, check_vma=False
        )(*arguments)

    return run
```

```python
import functools
import math

import jax
import jax.numpy as jnp
from jax import lax
from jax.experimental import pallas as pl
from jax.experimental.pallas import tpu as pltpu
from jax.sharding import Mesh
from jax.sharding import PartitionSpec as P

HEAD_DIM = 128
WIN = 2048


epsilon = 1e-06
masked_score = -1e30


def from_behind(value, axis, steps):
    count = lax.axis_size(axis)
    initial, last = (max(0, -steps), min(count, count - steps))
    return lax.ppermute(value, axis, [(source, source + steps) for source in range(initial, last)])


def matmul(left, right):
    return jnp.dot(left, right, preferred_element_type=jnp.float32)


def contract_rows(left, right):
    return lax.dot_general(
        left, right, (((0,), (0,)), ((), ())), preferred_element_type=jnp.float32
    )


def contract_cols(left, right):
    return lax.dot_general(
        left, right, (((1,), (1,)), ((), ())), preferred_element_type=jnp.float32
    )


def rotary_tables(positions):
    half_dim = HEAD_DIM // 2
    frequency = jnp.exp(
        jnp.arange(half_dim).astype(jnp.float32) * (-2.0 * math.log(10000.0) / HEAD_DIM)
    )
    angles = positions.astype(jnp.float32)[:, None] * frequency[None, :]
    return (jnp.cos(angles), jnp.sin(angles))


def rotate_pairs(values, cosine, sine_table):
    half_dim = values.shape[-1] // 2
    first_half = values[..., :half_dim]
    second_half = values[..., half_dim:]
    return jnp.concatenate(
        [
            first_half * cosine - second_half * sine_table,
            second_half * cosine + first_half * sine_table,
        ],
        axis=-1,
    )


def unrotate_pairs(values, cosine, sine_table):
    half_dim = values.shape[-1] // 2
    first_half = values[..., :half_dim]
    second_half = values[..., half_dim:]
    return jnp.concatenate(
        [
            first_half * cosine + second_half * sine_table,
            second_half * cosine - first_half * sine_table,
        ],
        axis=-1,
    )


def document_number(starts, positions):
    return jnp.sum((starts[:, None, :] <= positions[None, :, None]).astype(jnp.int32), axis=2)


def rms_scale(values):
    return lax.rsqrt(jnp.mean(values * values, axis=-1, keepdims=True) + epsilon)


def norm_backward(grad_normed, inputs, row_scale, gain_vector):
    gain_grad = jnp.sum(grad_normed * inputs * row_scale, axis=0)
    weighted = grad_normed * gain_vector
    grad_inputs = row_scale * weighted - inputs * row_scale**3 * jnp.mean(
        weighted * inputs, axis=-1, keepdims=True
    )
    return (grad_inputs, gain_grad)


def per_device(
    tokens,
    doc_starts,
    query_weight,
    key_weight,
    value_weight,
    out_weight,
    gate_weight,
    up_weight,
    down_weight,
    attention_gain,
    feedforward_gain,
    cotangent,
):
    gathered = (
        lax.all_gather(query_weight, ("stream", "seq"), axis=0, tiled=True),
        lax.all_gather(key_weight, ("stream", "seq"), axis=0, tiled=True),
        lax.all_gather(value_weight, ("stream", "seq"), axis=0, tiled=True),
        lax.all_gather(out_weight, ("stream", "seq"), axis=1, tiled=True),
        lax.all_gather(gate_weight, ("stream", "seq"), axis=0, tiled=True),
        lax.all_gather(up_weight, ("stream", "seq"), axis=0, tiled=True),
        lax.all_gather(down_weight, ("stream", "seq"), axis=1, tiled=True),
        lax.all_gather(attention_gain, ("stream", "seq"), axis=0, tiled=True),
        lax.all_gather(feedforward_gain, ("stream", "seq"), axis=0, tiled=True),
    )
    (
        full_query,
        full_key,
        full_value,
        full_out,
        full_gate,
        full_up,
        full_down,
        full_gain_first,
        full_gain_second,
    ) = gathered
    streams, shard_rows, model_width = tokens.shape
    head_width = full_query.shape[1]
    local_heads = head_width // HEAD_DIM
    flat_rows = streams * shard_rows
    seq_index = lax.axis_index("seq")
    halo_shards = min(WIN // shard_rows, lax.axis_size("seq") - 1)
    window_rows = (halo_shards + 1) * shard_rows
    inputs = tokens.reshape(flat_rows, model_width).astype(jnp.float32)
    scale_first = rms_scale(inputs)
    gain_first = full_gain_first.astype(jnp.float32)
    normed = (inputs * scale_first * gain_first).astype(jnp.bfloat16)
    query_proj = matmul(normed, full_query).reshape(streams, shard_rows, local_heads, HEAD_DIM)
    key_proj = matmul(normed, full_key).reshape(streams, shard_rows, local_heads, HEAD_DIM)
    value_low = (
        matmul(normed, full_value).astype(jnp.bfloat16).reshape(streams, shard_rows, head_width)
    )
    positions = seq_index * shard_rows + jnp.arange(shard_rows, dtype=jnp.int32)
    cosine, sine_table = rotary_tables(positions)
    cosine = cosine[None, :, None, :]
    sine_table = sine_table[None, :, None, :]
    query_rot = (rotate_pairs(query_proj, cosine, sine_table) * HEAD_DIM ** (-0.5)).astype(
        jnp.bfloat16
    )
    key_rot = rotate_pairs(key_proj, cosine, sine_table).astype(jnp.bfloat16)
    paired = jnp.stack([key_rot.reshape(streams, shard_rows, head_width), value_low])
    pieces = []
    for distance in range(halo_shards, 0, -1):
        pieces.append(from_behind(paired, "seq", distance))
    window = jnp.concatenate(pieces + [paired], axis=2)
    key_positions = (seq_index - halo_shards) * shard_rows + jnp.arange(
        window_rows, dtype=jnp.int32
    )
    query_docs = document_number(doc_starts, positions)
    key_docs = document_number(doc_starts, key_positions)
    offsets = positions[:, None] - key_positions[None, :]
    allowed = ((offsets >= 0) & (offsets < WIN))[None] & (
        query_docs[:, :, None] == key_docs[:, None, :]
    )
    query_heads = jnp.transpose(query_rot, (2, 0, 1, 3))
    key_heads = jnp.transpose(
        window[0].reshape(streams, window_rows, local_heads, HEAD_DIM), (2, 0, 1, 3)
    )
    value_heads = jnp.transpose(
        window[1].reshape(streams, window_rows, local_heads, HEAD_DIM), (2, 0, 1, 3)
    )

    def head_forward(operands):
        query_one, key_one, value_one = operands
        scores = jnp.einsum("sqe,ske->sqk", query_one, key_one, preferred_element_type=jnp.float32)
        scores = jnp.where(allowed, scores, masked_score)
        largest = jnp.max(scores, axis=-1, keepdims=True)
        weights = jnp.exp(scores - largest)
        totals = jnp.sum(weights, axis=-1, keepdims=True)
        probability = (weights / totals).astype(jnp.bfloat16)
        attended = jnp.einsum(
            "sqk,ske->sqe", probability, value_one, preferred_element_type=jnp.float32
        )
        return (attended, (largest + jnp.log(totals))[..., 0])

    attended, log_totals = lax.map(head_forward, (query_heads, key_heads, value_heads))
    heads_out = (
        jnp.transpose(attended, (1, 2, 0, 3)).reshape(flat_rows, head_width).astype(jnp.bfloat16)
    )
    attention_sum = lax.psum(matmul(heads_out, full_out), "head")
    residual = inputs + attention_sum
    scale_second = rms_scale(residual)
    gain_second = full_gain_second.astype(jnp.float32)
    normed_ffn = (residual * scale_second * gain_second).astype(jnp.bfloat16)
    gate_proj = matmul(normed_ffn, full_gate)
    up_proj = matmul(normed_ffn, full_up)
    sigmoid_gate = jax.nn.sigmoid(gate_proj)
    silu_gate = gate_proj * sigmoid_gate
    mixed_hidden = (silu_gate * up_proj).astype(jnp.bfloat16)
    feedforward_sum = lax.psum(matmul(mixed_hidden, full_down).astype(jnp.bfloat16), "head").astype(
        jnp.float32
    )
    output = (
        (residual + feedforward_sum).astype(jnp.bfloat16).reshape(streams, shard_rows, model_width)
    )
    gathered = (
        lax.all_gather(query_weight, ("stream", "seq"), axis=0, tiled=True),
        lax.all_gather(key_weight, ("stream", "seq"), axis=0, tiled=True),
        lax.all_gather(value_weight, ("stream", "seq"), axis=0, tiled=True),
        lax.all_gather(out_weight, ("stream", "seq"), axis=1, tiled=True),
        lax.all_gather(gate_weight, ("stream", "seq"), axis=0, tiled=True),
        lax.all_gather(up_weight, ("stream", "seq"), axis=0, tiled=True),
        lax.all_gather(down_weight, ("stream", "seq"), axis=1, tiled=True),
        lax.all_gather(attention_gain, ("stream", "seq"), axis=0, tiled=True),
        lax.all_gather(feedforward_gain, ("stream", "seq"), axis=0, tiled=True),
    )
    (
        full_query,
        full_key,
        full_value,
        full_out,
        full_gate,
        full_up,
        full_down,
        full_gain_first,
        full_gain_second,
    ) = gathered
    grad_output = cotangent.reshape(flat_rows, model_width)
    grad_down = contract_rows(mixed_hidden, grad_output)
    grad_mixed = contract_cols(grad_output, full_down)
    grad_gate_low = (
        grad_mixed * up_proj * sigmoid_gate * (1.0 + gate_proj * (1.0 - sigmoid_gate))
    ).astype(jnp.bfloat16)
    grad_up_low = (grad_mixed * silu_gate).astype(jnp.bfloat16)
    grad_gate_w = contract_rows(normed_ffn, grad_gate_low)
    grad_up_w = contract_rows(normed_ffn, grad_up_low)
    grad_normed_ffn = lax.psum(
        contract_cols(grad_gate_low, full_gate) + contract_cols(grad_up_low, full_up), "head"
    )
    grad_residual_norm, grad_gain_second = norm_backward(
        grad_normed_ffn, residual, scale_second, gain_second
    )
    grad_residual = grad_output.astype(jnp.float32) + grad_residual_norm
    grad_branch = grad_residual.astype(jnp.bfloat16)
    grad_out_w = contract_rows(heads_out, grad_branch)
    grad_heads = contract_cols(grad_branch, full_out).astype(jnp.bfloat16)
    grad_heads_major = jnp.transpose(
        grad_heads.reshape(streams, shard_rows, local_heads, HEAD_DIM), (2, 0, 1, 3)
    )

    def head_backward(operands):
        query_one, key_one, value_one, grad_one, log_one = operands
        scores = jnp.einsum("sqe,ske->sqk", query_one, key_one, preferred_element_type=jnp.float32)
        scores = jnp.where(allowed, scores, masked_score)
        probability = jnp.exp(scores - log_one[..., None])
        grad_prob = jnp.einsum(
            "sqe,ske->sqk", grad_one, value_one, preferred_element_type=jnp.float32
        )
        centre = jnp.sum(probability * grad_prob, axis=-1, keepdims=True)
        grad_scores = (probability * (grad_prob - centre)).astype(jnp.bfloat16)
        grad_query_one = jnp.einsum(
            "sqk,ske->sqe", grad_scores, key_one, preferred_element_type=jnp.float32
        )
        grad_key_one = jnp.einsum(
            "sqk,sqe->ske", grad_scores, query_one, preferred_element_type=jnp.float32
        )
        grad_value_one = jnp.einsum(
            "sqk,sqe->ske",
            probability.astype(jnp.bfloat16),
            grad_one,
            preferred_element_type=jnp.float32,
        )
        return (grad_query_one, grad_key_one, grad_value_one)

    grad_query_heads, grad_key_heads, grad_value_heads = lax.map(
        head_backward, (query_heads, key_heads, value_heads, grad_heads_major, log_totals)
    )
    grad_window = jnp.transpose(
        jnp.stack([grad_key_heads, grad_value_heads]), (0, 2, 3, 1, 4)
    ).reshape(2, streams, window_rows, head_width)
    grad_paired = grad_window[:, :, halo_shards * shard_rows :]
    for distance in range(halo_shards, 0, -1):
        index_piece = halo_shards - distance
        grad_paired = grad_paired + from_behind(
            grad_window[:, :, index_piece * shard_rows : (index_piece + 1) * shard_rows],
            "seq",
            -distance,
        )
    grad_key_rot = grad_paired[0].reshape(streams, shard_rows, local_heads, HEAD_DIM)
    grad_query_rot = jnp.transpose(grad_query_heads, (1, 2, 0, 3))
    grad_query_low = (
        (unrotate_pairs(grad_query_rot, cosine, sine_table) * HEAD_DIM ** (-0.5))
        .reshape(flat_rows, head_width)
        .astype(jnp.bfloat16)
    )
    grad_key_low = (
        unrotate_pairs(grad_key_rot, cosine, sine_table)
        .reshape(flat_rows, head_width)
        .astype(jnp.bfloat16)
    )
    grad_value_low = grad_paired[1].reshape(flat_rows, head_width).astype(jnp.bfloat16)
    grad_query_w = contract_rows(normed, grad_query_low)
    grad_key_w = contract_rows(normed, grad_key_low)
    grad_value_w = contract_rows(normed, grad_value_low)
    grad_normed = lax.psum(
        contract_cols(grad_query_low, full_query)
        + contract_cols(grad_key_low, full_key)
        + contract_cols(grad_value_low, full_value),
        "head",
    )
    grad_inputs_norm, grad_gain_first = norm_backward(grad_normed, inputs, scale_first, gain_first)
    grad_tokens = (grad_residual + grad_inputs_norm).reshape(streams, shard_rows, model_width)
    reduced = (
        lax.psum_scatter(grad_query_w, ("stream", "seq"), scatter_dimension=0, tiled=True),
        lax.psum_scatter(grad_key_w, ("stream", "seq"), scatter_dimension=0, tiled=True),
        lax.psum_scatter(grad_value_w, ("stream", "seq"), scatter_dimension=0, tiled=True),
        lax.psum_scatter(grad_out_w, ("stream", "seq"), scatter_dimension=1, tiled=True),
        lax.psum_scatter(grad_gate_w, ("stream", "seq"), scatter_dimension=0, tiled=True),
        lax.psum_scatter(grad_up_w, ("stream", "seq"), scatter_dimension=0, tiled=True),
        lax.psum_scatter(grad_down, ("stream", "seq"), scatter_dimension=1, tiled=True),
        lax.psum_scatter(grad_gain_first, ("stream", "seq"), scatter_dimension=0, tiled=True),
        lax.psum_scatter(grad_gain_second, ("stream", "seq"), scatter_dimension=0, tiled=True),
    )
    return (
        output,
        grad_tokens,
        reduced[0],
        reduced[1],
        reduced[2],
        reduced[3],
        reduced[4],
        reduced[5],
        reduced[6],
        reduced[7],
        reduced[8],
    )


GROUP = ("zl", "y", "c")
SQUARE = ("zl", "y")
MEMBERS = 8
QUARTERS = 4
MESH = pl.DeviceIdType.MESH


def swap(value, axis):
    return lax.ppermute(value, axis, [(0, 1), (1, 0)])


def remote_copy(source, target, sent, landed, peer):
    return pltpu.make_async_remote_copy(
        source, target, sent, landed, device_id=peer, device_id_type=MESH
    )


def lanes(index, size):
    return pl.ds(pl.multiple_of(index * size, size), size)


class FarGather:
    def __init__(self, square, step):
        self.height, self.width = square.shape
        self.inputs = [(square, square.shape)]
        self.cuts = list(range(0, self.height, step)) + [self.height]
        self.pieces = len(self.cuts) - 1
        self.outputs = [(jax.ShapeDtypeStruct((self.height, 4 * self.width), square.dtype), None)]
        dma = pltpu.SemaphoreType.DMA
        self.scratch = [dma((3 * self.pieces,)), dma((3 * self.pieces,)), dma(())]
        self.peers = ("x", "zh")

    def bind(self, inputs, outputs, scratch, to_peer):
        (square,), (units,), (sent, landed, local) = inputs, outputs, scratch
        self.hops = []
        for piece in range(self.pieces):
            at = pl.ds(self.cuts[piece], self.cuts[piece + 1] - self.cuts[piece])

            def hop(index, source, target, axis, rows_at=at, first=3 * piece):
                place = units.at[rows_at, pl.ds(target * self.width, self.width)]
                return remote_copy(
                    source, place, sent.at[first + index], landed.at[first + index], to_peer[axis]
                )

            passed = units.at[at, pl.ds(self.width, self.width)]
            self.hops.append(
                (
                    hop(0, square.at[at], 1, "zh"),
                    hop(1, square.at[at], 2, "x"),
                    hop(2, passed, 3, "x"),
                )
            )
        self.here = pltpu.make_async_copy(square, units.at[:, pl.ds(0, self.width)], local)
        self.done = 0

    def begin(self):
        self.here.start()
        for hops in self.hops[:2]:
            hops[0].start()
        for hops in self.hops:
            hops[1].start()

    def advance(self, count):
        for piece in range(self.done, self.done + count):
            self.hops[piece][0].wait_recv()
            if piece + 2 < self.pieces:
                self.hops[piece + 2][0].start()
            self.hops[piece][2].start()
        self.done += count

    def end(self):
        self.advance(self.pieces - self.done)
        for hops in self.hops:
            hops[1].wait_recv()
            hops[2].wait_recv()
            for copy in hops:
                copy.wait_send()
        self.here.wait()


class FarReduce:
    def __init__(self, grads, near=False, stop=False):
        height, width = grads.shape
        self.height, self.near, self.stop = height, near, stop
        self.half = width if near else width // 2
        self.quarter = self.half // 2
        bf16 = jnp.bfloat16
        dma = pltpu.SemaphoreType.DMA
        self.inputs = [(grads, None)]
        self.outputs = [
            (
                jax.ShapeDtypeStruct((height, self.half if stop else self.quarter), bf16),
                (height, self.half if stop else self.quarter),
            )
        ]
        self.scratch = [dma((3,)), dma((2,)), pltpu.VMEM((height, self.half), bf16)]
        if not near:
            self.scratch.append(pltpu.VMEM((height, self.half), bf16))
        if not stop:
            self.scratch.append(pltpu.VMEM((height, self.quarter), bf16))
        self.peers = ("x", "zh")

    def bind(self, inputs, outputs, scratch, to_peer):
        (grads,), (self.result,) = inputs, outputs
        scratch = list(scratch)
        sent, landed, self.mine = scratch[:3]
        rest = scratch[3:]
        self.load = pltpu.make_async_copy(grads.at[:, pl.ds(0, self.half)], self.mine, sent.at[2])
        if not self.near:
            self.got = rest.pop(0)
            self.first = remote_copy(
                grads.at[:, pl.ds(self.half, self.half)],
                self.got,
                sent.at[0],
                landed.at[0],
                to_peer["x"],
            )
        if not self.stop:
            self.passed = rest.pop(0)
            self.second = remote_copy(
                (grads if self.near else self.mine).at[:, pl.ds(self.quarter, self.quarter)],
                self.passed,
                sent.at[1],
                landed.at[1],
                to_peer["zh"],
            )

    def add(self, target, source, width):
        step = 16
        columns = pl.ds(0, width)

        @pl.loop(0, self.height // step)
        def _(index):
            at = pl.ds(pl.multiple_of(index * step, step), step)
            total = self.mine[at, columns].astype(jnp.float32) + source[at, :].astype(jnp.float32)
            target[at, :] = total.astype(jnp.bfloat16)

    def begin(self):
        self.load.start()
        if self.near:
            self.second.start()
        else:
            self.first.start()

    def advance(self):
        self.load.wait()
        self.first.wait_recv()
        self.add(self.result if self.stop else self.mine, self.got, self.half)
        if not self.stop:
            self.second.start()

    def end(self):
        if self.near:
            self.load.wait()
        else:
            self.first.wait_send()
        if not self.stop:
            self.second.wait_recv()
            self.add(self.result, self.passed, self.quarter)
            self.second.wait_send()


def exchange(name, collective_id, jobs, extra, hosted, plan):
    bf16, f32 = jnp.bfloat16, jnp.float32
    length, model_width = jobs[0]["lefts"][0].shape[0], jobs[0]["rights"][0][0].shape[1]
    rows = length // (2 * MEMBERS)
    strip = 512
    gathers = jobs[-1]["gathers"]

    def block(shape, index):
        return pl.BlockSpec(shape, lambda step: index, pipeline_mode=pl.Buffered(1))

    def whole(shape):
        return block(shape, (0,) * len(shape))

    anywhere = pl.BlockSpec(memory_space=pl.ANY)
    arrays, in_specs, out_shape, out_specs = [], [], [], []
    for job in jobs:
        for left in job["lefts"]:
            arrays.append(left)
            in_specs.append(whole(left.shape))
        for array, height, at in job["rights"]:
            arrays.append(array)
            in_specs.append(block((height, model_width), (at, 0)))
        for array, height, at in job["states"]:
            arrays.append(array)
            in_specs.append(
                whole(array.shape) if height is None else block((height, model_width), (at, 0))
            )
        out_shape.append(jax.ShapeDtypeStruct((2, rows, model_width), job["kept"]))
        out_specs.append(whole((2, rows, model_width)))
    if gathers:
        out_shape.append(jax.ShapeDtypeStruct((2, MEMBERS, rows, model_width), bf16))
        out_specs.append(anywhere)
    handing = [job for job in jobs if job.get("hands")]
    for job in handing:
        out_shape.append(jax.ShapeDtypeStruct((rows, model_width), job["kept"]))
        out_specs.append(anywhere)
    for guest in hosted:
        for array, kind in guest.inputs:
            arrays.append(array)
            in_specs.append(anywhere if kind is None else whole(kind))
        for shape, kind in guest.outputs:
            out_shape.append(shape)
            out_specs.append(anywhere if kind is None else whole(kind))
    dma = pltpu.SemaphoreType.DMA
    count = len(jobs)
    scratch = [
        pltpu.VMEM((4, 2, rows, model_width), bf16),
        pltpu.VMEM((4, 2, rows, model_width), bf16),
        pltpu.VMEM((4, 2, rows, model_width), f32),
        pltpu.VMEM((6, rows, model_width), bf16),
        pltpu.VMEM((6, rows, model_width), bf16),
        pltpu.VMEM((2, rows, model_width), bf16),
        dma((4 * count,)),
        dma((4 * count,)),
        dma((6 * count,)),
        dma((6 * count,)),
        dma((12,)),
        dma((12,)),
        dma(()),
        dma((2,)),
        pltpu.SemaphoreType.REGULAR((3,)),
    ]
    own_scratch = len(scratch)
    for guest in hosted:
        scratch += guest.scratch

    def kernel(*refs):
        refs = list(refs)

        def take(number):
            taken = refs[:number]
            del refs[:number]
            return taken

        job_refs = [
            (take(len(job["lefts"])), take(len(job["rights"])), take(len(job["states"])))
            for job in jobs
        ]
        guest_inputs = [take(len(guest.inputs)) for guest in hosted]
        kept_refs = take(count)
        full = take(1)[0] if gathers else None
        handed = take(len(handing))
        guest_outputs = [take(len(guest.outputs)) for guest in hosted]
        (core_send, core_got, sums, link_send, link_got, own) = take(6)
        (core_out, core_in, link_out, link_in, full_out, full_in, local, hand, ready) = take(
            own_scratch - 6
        )
        to_peer = {axis: {axis: 1 - lax.axis_index(axis)} for axis in ("x", "zh", "zl", "y", "c")}
        zl, y, core = (lax.axis_index(axis) for axis in GROUP)

        peers = list(GROUP) + sorted({axis for guest in hosted for axis in guest.peers})
        barrier = pltpu.get_barrier_semaphore()
        for axis in peers:
            pl.semaphore_signal(barrier, inc=1, device_id=to_peer[axis], device_id_type=MESH)
        pl.semaphore_wait(barrier, len(peers))
        for guest, inputs, outputs in zip(hosted, guest_inputs, guest_outputs):
            guest.bind(inputs, outputs, take(len(guest.scratch)), to_peer)
        plan("begin")

        chips = ((1 - zl, 1 - y), (1 - zl, y), (zl, 1 - y), (zl, y))

        def run(number):
            left_refs, right_refs, state_refs = job_refs[number]
            finish, kept = jobs[number]["finish"], kept_refs[number]

            def produce(chip, mine):
                member = 4 * chips[chip][0] + 2 * chips[chip][1] + (core if mine else 1 - core)
                at = [
                    pl.ds(pl.multiple_of((half * MEMBERS + member) * rows, rows), rows)
                    for half in range(2)
                ]
                blocks = [
                    jnp.concatenate([ref[at[0], :], ref[at[1], :]], axis=0) for ref in left_refs
                ]

                @pl.loop(0, model_width // strip)
                def _(step):
                    columns = lanes(step, strip)
                    product = matmul(blocks[0], right_refs[0][:, columns])
                    for part, ref in zip(blocks[1:], right_refs[1:]):
                        product = product + matmul(part, ref[:, columns])
                    for half in range(2):
                        piece = product[half * rows : (half + 1) * rows]
                        if mine:
                            sums[chip, half, :, columns] = piece
                        else:
                            core_send[chip, half, :, columns] = piece.astype(bf16)

            core_copies = [
                remote_copy(
                    core_send.at[chip],
                    core_got.at[chip],
                    core_out.at[4 * number + chip],
                    core_in.at[4 * number + chip],
                    to_peer["c"],
                )
                for chip in range(4)
            ]

            axes = [extra[index % 2] for index in range(4)]
            axes += ["zl" if extra[half] == "y" else "y" for half in range(2)]
            chip_on = {"zl": 1, "y": 2}
            links = [
                remote_copy(
                    link_send.at[index],
                    link_got.at[index],
                    link_out.at[6 * number + index],
                    link_in.at[6 * number + index],
                    to_peer[axes[index]],
                )
                for index in range(6)
            ]

            def send(index):
                half = index % 2
                chip = 0 if index < 2 else chip_on[axes[index]]
                link_send[index] = sums[chip, half].astype(bf16)
                links[index].start()

            def settle(chip):
                core_copies[chip].wait_recv()
                for half in range(2):
                    sums[chip, half] += core_got[chip, half].astype(f32)

            if number > 0:
                for copy in previous:
                    copy.wait_send()
                for index, axis in enumerate(GROUP):
                    pl.semaphore_signal(
                        ready.at[index], inc=1, device_id=to_peer[axis], device_id_type=MESH
                    )
            produce(0, False)
            if number > 0:
                pl.semaphore_wait(ready.at[2], 1)
            core_copies[0].start()
            produce(0, True)
            produce(1, False)
            core_copies[1].start()
            settle(0)
            if number > 0:
                pl.semaphore_wait(ready.at[0], 1)
                pl.semaphore_wait(ready.at[1], 1)
            send(0)
            send(1)
            produce(1, True)
            produce(2, False)
            core_copies[2].start()
            settle(1)
            for index in (2, 3):
                if axes[index] == "zl":
                    send(index)
            produce(2, True)
            produce(3, False)
            core_copies[3].start()
            settle(2)
            for index in (2, 3):
                if axes[index] == "y":
                    send(index)
            for half in range(2):
                links[half].wait_recv()
                sums[chip_on[axes[4 + half]], half] += link_got[half].astype(f32)
                send(4 + half)
                if half == 0:
                    produce(3, True)
                    settle(3)
            plan("sent", number)

            def close(half):
                links[2 + half].wait_recv()
                links[4 + half].wait_recv()

                @pl.loop(0, rows // 32)
                def _(step):
                    at = pl.ds(pl.multiple_of(step * 32, 32), 32)
                    total = sums[3, half, at, :] + link_got[2 + half, at, :].astype(f32)
                    total = total + link_got[4 + half, at, :].astype(f32)
                    finish(total, half, at, state_refs, kept, own)

            if not jobs[number]["gathers"]:
                close(0)
                close(1)
                if jobs[number].get("hands"):
                    handovers.append(
                        remote_copy(
                            kept.at[1 - lax.axis_index("zh")],
                            handed[0],
                            hand.at[0],
                            hand.at[1],
                            to_peer["zh"],
                        )
                    )
                    handovers[0].start()
                plan("closed", number)
                return core_copies + links

            me = 4 * zl + 2 * y + core
            place = {
                "y": 4 * zl + 2 * (1 - y) + core,
                "zl": 4 * (1 - zl) + 2 * y + core,
            }
            opposite = 4 * (1 - zl) + 2 * (1 - y) + core

            def full_copy(index, source, half, member, axis):
                return remote_copy(
                    source,
                    full.at[half, member],
                    full_out.at[index],
                    full_in.at[index],
                    to_peer[axis],
                )

            def onward(index, half, member, axis):
                return full_copy(index, full.at[half, member], half, member, axis)

            other = ["zl" if extra[half] == "y" else "y" for half in range(2)]
            by_axis = {
                (axis, half): full_copy(2 * number_of + half, own.at[half], half, me, axis)
                for number_of, axis in enumerate(("y", "zl"))
                for half in range(2)
            }
            diagonal = [onward(4 + half, half, place[other[half]], extra[half]) for half in range(2)]
            shared = [full_copy(6 + half, own.at[half], half, me, "c") for half in range(2)]
            both = {
                axis: remote_copy(
                    full.at[:, place[axis]],
                    full.at[:, place[axis]],
                    full_out.at[8 + index],
                    full_in.at[8 + index],
                    to_peer["c"],
                )
                for index, axis in enumerate(("y", "zl"))
            }
            last = [onward(10 + half, half, opposite, "c") for half in range(2)]
            here = pltpu.make_async_copy(own, full.at[:, me], local)
            for half in range(2):
                close(half)
                by_axis[other[half], half].start()
                by_axis[extra[half], half].start()
                shared[half].start()
            here.start()
            plan("closed", number)
            for half in range(2):
                by_axis[other[half], half].wait_recv()
                diagonal[half].start()
            plan("passed", number)
            for half in range(2):
                by_axis[extra[half], half].wait_recv()
            both["y"].start()
            both["zl"].start()
            plan("spread", number)
            for half in range(2):
                diagonal[half].wait_recv()
                last[half].start()
            for copy in shared + list(both.values()) + last:
                copy.wait_recv()
            for copy in list(by_axis.values()) + diagonal + shared + list(both.values()) + last:
                copy.wait_send()
            here.wait()
            return core_copies + links

        previous, handovers = [], []
        for number in range(count):
            previous = run(number)
        plan("end")
        for copy in handovers:
            copy.wait()
        for copy in previous:
            copy.wait_send()

    depth = sum(height for job in jobs for _, height, _ in job["rights"])
    results = list(
        pl.pallas_call(
            kernel,
            grid=(1,),
            in_specs=in_specs,
            out_specs=out_specs,
            out_shape=out_shape,
            scratch_shapes=scratch,
            compiler_params=pltpu.CompilerParams(
                collective_id=collective_id,
                has_side_effects=True,
                vmem_limit_bytes=60 * 1024 * 1024,
            ),
            cost_estimate=pl.CostEstimate(
                flops=2 * length * depth * model_width,
                bytes_accessed=200 * 1024 * 1024,
                transcendentals=0,
            ),
            name=name,
        )(*arrays)
    )
    if gathers:
        results[count] = results[count].reshape(length, model_width)
    return results


class SquareSpread:
    def __init__(self, parts):
        _, self.height, self.width = parts.shape
        dma = pltpu.SemaphoreType.DMA
        self.inputs = [(parts, parts.shape)]
        self.outputs = [
            (jax.ShapeDtypeStruct((self.height, QUARTERS * self.width), parts.dtype), None)
        ]
        self.scratch = [dma((3,)), dma((3,)), dma(())]

    def bind(self, inputs, outputs, scratch):
        (parts,), (square,), (sent, landed, local) = inputs, outputs, scratch
        zl, y = lax.axis_index("zl"), lax.axis_index("y")
        chip = 2 * zl + y
        place = square.at[:, lanes(chip, self.width)]
        self.copies = [
            remote_copy(parts.at[other], place, sent.at[index], landed.at[index], peer)
            for index, (peer, other) in enumerate(
                (
                    ({"y": 1 - y}, chip + 1 - 2 * y),
                    ({"zl": 1 - zl}, chip + 2 - 4 * zl),
                    ({"zl": 1 - zl, "y": 1 - y}, 3 - chip),
                )
            )
        ]
        self.here = pltpu.make_async_copy(parts.at[chip], place, local)

    def begin(self):
        for copy in self.copies:
            copy.start()
        self.here.start()

    def end(self):
        for copy in self.copies:
            copy.wait()
        self.here.wait()


class SquareReturn:
    def __init__(self, grads):
        height, width = grads.shape
        self.width = width // QUARTERS
        dma = pltpu.SemaphoreType.DMA
        self.inputs = [(grads, grads.shape)]
        self.outputs = [(jax.ShapeDtypeStruct((QUARTERS, height, self.width), grads.dtype), None)]
        self.scratch = [dma((3,)), dma((3,)), dma(())]

    def bind(self, inputs, outputs, scratch, to_peer):
        (grads,), (got,), (sent, landed, local) = inputs, outputs, scratch
        zl, y = lax.axis_index("zl"), lax.axis_index("y")
        chip = 2 * zl + y
        others = (chip + 1 - 2 * y, chip + 2 - 4 * zl, 3 - chip)
        self.copies = [
            remote_copy(
                grads.at[:, lanes(other, self.width)],
                got.at[chip],
                sent.at[index],
                landed.at[index],
                peer,
            )
            for index, (peer, other) in enumerate(zip(square_peers(), others))
        ]
        self.here = pltpu.make_async_copy(
            grads.at[:, lanes(chip, self.width)], got.at[chip], local
        )

    def begin(self):
        for copy in self.copies:
            copy.start()
        self.here.start()

    def end(self):
        for copy in self.copies:
            copy.wait()
        self.here.wait()


def square_peers():
    zl, y = lax.axis_index("zl"), lax.axis_index("y")
    return [{"y": 1 - y}, {"zl": 1 - zl}, {"zl": 1 - zl, "y": 1 - y}]


def closing(grads, output_keep, output_give, tokens_keep, tokens_give):
    bf16, f32 = jnp.bfloat16, jnp.float32
    rows, model_width = output_keep.shape
    count = len(grads)
    width = grads[0].shape[1] // QUARTERS

    def kernel(*refs):
        grad_refs = refs[:count]
        out_keep, out_give, tok_keep, tok_give = refs[count : count + 4]
        got_refs = refs[count + 4 : 2 * count + 4]
        output, tokens = refs[2 * count + 4 : 2 * count + 6]
        sent, landed, local, out_sem, in_sem, here_sem, low, wide = refs[2 * count + 6 :]
        zh, zl, y, core = (lax.axis_index(axis) for axis in ("zh", "zl", "y", "c"))
        to_zh, to_core = {"zh": 1 - zh}, {"c": 1 - core}
        chip = 2 * zl + y
        peers = square_peers()
        barrier = pltpu.get_barrier_semaphore()
        for peer in peers + [to_zh, to_core]:
            pl.semaphore_signal(barrier, inc=1, device_id=peer, device_id_type=MESH)
        pl.semaphore_wait(barrier, 5)
        at = pl.ds(pl.multiple_of(core * rows, rows), rows)

        def link(index, source, target, peer):
            return remote_copy(source, target, out_sem.at[index], in_sem.at[index], peer)

        give = [link(0, tok_give, low, to_zh), link(4, out_give, output.at[zh, at], to_zh)]
        keep = [
            pltpu.make_async_copy(tok_keep, tokens.at[zh, at], here_sem.at[0]),
            pltpu.make_async_copy(out_keep, output.at[zh, at], here_sem.at[1]),
        ]
        for copy in give + keep:
            copy.start()
        across = [
            link(1, out_keep, output.at[zh, at], to_core),
            link(2, tok_keep, tokens.at[zh, at], to_core),
        ]
        for copy in across:
            copy.start()
        others = (chip + 1 - 2 * y, chip + 2 - 4 * zl, 3 - chip)
        spread, stay = [], []
        for number in range(count):
            for index in range(3):
                slot = 3 * number + index
                spread.append(
                    remote_copy(
                        grad_refs[number].at[:, lanes(others[index], width)],
                        got_refs[number].at[chip],
                        sent.at[slot],
                        landed.at[slot],
                        peers[index],
                    )
                )
            stay.append(
                pltpu.make_async_copy(
                    grad_refs[number].at[:, lanes(chip, width)],
                    got_refs[number].at[chip],
                    local.at[number],
                )
            )
        for copy in spread + stay:
            copy.start()
        give[0].wait_recv()
        wide[...] = low[...].astype(f32)
        across.append(link(3, wide, tokens.at[1 - zh, at], to_core))
        across[2].start()
        keep.append(pltpu.make_async_copy(wide, tokens.at[1 - zh, at], here_sem.at[2]))
        keep[2].start()
        give[1].wait_recv()
        across.append(link(5, output.at[1 - zh, at], output.at[1 - zh, at], to_core))
        across[3].start()
        for copy in give:
            copy.wait_send()
        for copy in spread + across + stay + keep:
            copy.wait()

    anywhere = pl.BlockSpec(memory_space=pl.ANY)
    inside = pl.BlockSpec(memory_space=pltpu.VMEM)
    shape = jax.ShapeDtypeStruct
    dma = pltpu.SemaphoreType.DMA
    return pl.pallas_call(
        kernel,
        in_specs=[inside] * (count + 4),
        out_specs=[anywhere] * (count + 2),
        out_shape=[shape((QUARTERS, grad.shape[0], width), bf16) for grad in grads]
        + [
            shape((2, 2 * rows, model_width), bf16),
            shape((2, 2 * rows, model_width), f32),
        ],
        scratch_shapes=[
            dma((3 * count,)),
            dma((3 * count,)),
            dma((count,)),
            dma((6,)),
            dma((6,)),
            dma((3,)),
            pltpu.VMEM((rows, model_width), bf16),
            pltpu.VMEM((rows, model_width), f32),
        ],
        compiler_params=pltpu.CompilerParams(collective_id=5, has_side_effects=True),
        cost_estimate=pl.CostEstimate(
            flops=0, bytes_accessed=100 * 1024 * 1024, transcendentals=0
        ),
        name="closing",
    )(*grads, output_keep, output_give, tokens_keep, tokens_give)


def attention_forward_kernel(query, key, value, first, attended, heads_out, log_total):
    tile = pl.program_id(1)
    rows = query.shape[0]
    query_tile = query[...]
    first_key = first[...]
    row_index = lax.broadcasted_iota(jnp.int32, (rows, rows), 0)
    column_index = lax.broadcasted_iota(jnp.int32, (rows, rows), 1)

    def block(index, carry, diagonal):
        largest, total, summed = carry
        at = pl.ds(pl.multiple_of(index * rows, rows), rows)
        scores = contract_cols(query_tile, key[at, :])
        visible = column_index + index * rows >= first_key
        if diagonal:
            visible = visible & (column_index <= row_index)
        scores = jnp.where(visible, scores, masked_score)
        new_largest = jnp.maximum(largest, jnp.max(scores, axis=1, keepdims=True))
        weights = jnp.where(visible, jnp.exp(scores - new_largest), 0.0)
        scaling = jnp.exp(largest - new_largest)
        total = total * scaling + jnp.sum(weights, axis=1, keepdims=True)
        summed = summed * scaling + matmul(weights.astype(jnp.bfloat16), value[at, :])
        return (new_largest, total, summed)

    carry = (
        jnp.full((rows, 1), masked_score, jnp.float32),
        jnp.zeros((rows, 1), jnp.float32),
        jnp.zeros((rows, HEAD_DIM), jnp.float32),
    )
    carry = lax.fori_loop(0, tile, lambda index, kept: block(index, kept, False), carry)
    largest, total, summed = block(tile, carry, True)
    summed = summed / total
    attended[...] = summed
    heads_out[...] = summed.astype(jnp.bfloat16)
    log_total[0, :, :] = jnp.broadcast_to(
        jnp.transpose(largest + jnp.log(total)), log_total.shape[1:]
    )


def attention_forward(query, key, value, first_key, tile_rows):
    length, width = query.shape
    heads = width // HEAD_DIM
    whole = pl.BlockSpec((length, HEAD_DIM), lambda head, tile: (0, head))
    part = pl.BlockSpec((tile_rows, HEAD_DIM), lambda head, tile: (tile, head))
    return pl.pallas_call(
        attention_forward_kernel,
        grid=(heads, length // tile_rows),
        in_specs=[
            part,
            whole,
            whole,
            pl.BlockSpec((tile_rows, 1), lambda head, tile: (tile, 0)),
        ],
        out_specs=[
            part,
            part,
            pl.BlockSpec((1, 8, tile_rows), lambda head, tile: (head, 0, tile)),
        ],
        out_shape=[
            jax.ShapeDtypeStruct((length, width), jnp.float32),
            jax.ShapeDtypeStruct((length, width), jnp.bfloat16),
            jax.ShapeDtypeStruct((heads, 8, length), jnp.float32),
        ],
        compiler_params=pltpu.CompilerParams(vmem_limit_bytes=48 * 1024 * 1024),
        cost_estimate=pl.CostEstimate(
            flops=2 * length * length * width,
            bytes_accessed=10 * length * width,
            transcendentals=length * length * heads // 2,
        ),
        name="attention_forward",
    )(query, key, value, first_key)


def project(all_tokens, units, head_width, cosine, sine_table, parts, give):
    guest = SquareSpread(parts)
    bf16, f32 = jnp.bfloat16, jnp.float32
    length, model_width = all_tokens.shape
    rows = 256

    def kernel(
        tokens, weight, gains, cos, sin, parts, give, normed, query, key, value, square, got, *scratch
    ):
        guest.bind((parts,), (square,), scratch[:3])
        to_zh = {"zh": 1 - lax.axis_index("zh")}
        swapped = remote_copy(give, got, scratch[3], scratch[4], to_zh)

        @pl.when(pl.program_id(0) == 0)
        def _():
            barrier = pltpu.get_barrier_semaphore()
            for peer in square_peers() + [to_zh]:
                pl.semaphore_signal(barrier, inc=1, device_id=peer, device_id_type=MESH)
            pl.semaphore_wait(barrier, 4)
            guest.begin()
            swapped.start()

        values = tokens[...].astype(f32)
        gain = gains[0:1, :].astype(f32)
        low = (values * rms_scale(values) * gain).astype(bf16)
        normed[...] = low

        def turn(part):
            return part * cos[...] + pltpu.roll(part, HEAD_DIM // 2, 1) * sin[...]

        for head in range(head_width // HEAD_DIM):
            at = slice(head * HEAD_DIM, (head + 1) * HEAD_DIM)

            def projection(start):
                begin = start + head * HEAD_DIM
                return contract_cols(low, weight[begin : begin + HEAD_DIM, :])

            query[:, at] = (turn(projection(0)) * HEAD_DIM ** (-0.5)).astype(bf16)
            key[:, at] = turn(projection(head_width)).astype(bf16)
            value[:, at] = projection(2 * head_width).astype(bf16)

        @pl.when(pl.program_id(0) == pl.num_programs(0) - 1)
        def _():
            guest.end()
            swapped.wait()

    def tile(width):
        return pl.BlockSpec((rows, width), lambda step: (step, 0))

    gain_block = units.shape[0] // 16 - 1
    shape = jax.ShapeDtypeStruct
    anywhere = pl.BlockSpec(memory_space=pl.ANY)
    return pl.pallas_call(
        kernel,
        grid=(length // rows,),
        in_specs=[
            tile(model_width),
            pl.BlockSpec((3 * head_width, model_width), lambda step: (0, 0)),
            pl.BlockSpec((16, model_width), lambda step: (gain_block, 0)),
            tile(HEAD_DIM),
            tile(HEAD_DIM),
            pl.BlockSpec(parts.shape, lambda step: (0, 0, 0), pipeline_mode=pl.Buffered(1)),
            anywhere,
        ],
        out_specs=[tile(model_width)] + [tile(head_width)] * 3 + [anywhere] * 2,
        out_shape=[shape((length, model_width), bf16)]
        + [shape((length, head_width), bf16)] * 3
        + [guest.outputs[0][0], shape(give.shape, bf16)],
        scratch_shapes=guest.scratch + [pltpu.SemaphoreType.DMA(())] * 2,
        compiler_params=pltpu.CompilerParams(
            collective_id=4, has_side_effects=True, vmem_limit_bytes=48 * 1024 * 1024
        ),
        cost_estimate=pl.CostEstimate(
            flops=6 * length * head_width * model_width,
            bytes_accessed=4 * length * model_width,
            transcendentals=0,
        ),
        name="project",
    )(all_tokens, units, units, cosine, sine_table, parts, give)


def feedforward(normed_ffn, all_cotangent, units, hidden):
    bf16 = jnp.bfloat16
    length, model_width = normed_ffn.shape
    rows = 256

    def kernel(normed, cotangent, weights, mixed, grad_gate, grad_up, partial):
        low = normed[...]
        gate = contract_cols(low, weights[:hidden, :])
        up = contract_cols(low, weights[hidden : 2 * hidden, :])
        grad_mixed = contract_cols(cotangent[...], weights[2 * hidden :, :])
        sigmoid = 1.0 / (1.0 + jnp.exp(-gate))
        silu = gate * sigmoid
        mixed_low = (silu * up).astype(bf16)
        mixed[...] = mixed_low
        partial[...] = matmul(mixed_low, weights[2 * hidden :, :]).astype(bf16)
        grad_up[...] = (grad_mixed * silu).astype(bf16)
        grad_gate[...] = (grad_mixed * up * sigmoid * (1.0 + gate * (1.0 - sigmoid))).astype(bf16)

    def tile(width):
        return pl.BlockSpec((rows, width), lambda step: (step, 0))

    shape = jax.ShapeDtypeStruct
    return pl.pallas_call(
        kernel,
        grid=(length // rows,),
        in_specs=[
            tile(model_width),
            tile(model_width),
            pl.BlockSpec((3 * hidden, model_width), lambda step: (0, 0)),
        ],
        out_specs=[tile(hidden)] * 3 + [tile(model_width)],
        out_shape=[shape((length, hidden), bf16)] * 3 + [shape((length, model_width), bf16)],
        compiler_params=pltpu.CompilerParams(vmem_limit_bytes=56 * 1024 * 1024),
        cost_estimate=pl.CostEstimate(
            flops=8 * length * hidden * model_width,
            bytes_accessed=6 * length * model_width,
            transcendentals=length * hidden,
        ),
        name="feedforward",
    )(normed_ffn, all_cotangent, units)


def attention_backward_kernel(guests, plan, *refs):
    refs = list(refs)

    def take(number):
        taken = refs[:number]
        del refs[:number]
        return taken

    query, key, value, branch, weight, attended, log_total, first, cos, sin = take(10)
    guest_inputs = [take(len(guest.inputs)) for guest in guests]
    grad_query, grad_key, grad_value = take(3)
    guest_outputs = [take(len(guest.outputs)) for guest in guests]
    key_sum, value_sum = take(2)
    to_peer = {axis: {axis: 1 - lax.axis_index(axis)} for axis in ("x", "zh")}
    for guest, inputs, outputs in zip(guests, guest_inputs, guest_outputs):
        guest.bind(inputs, outputs, take(len(guest.scratch)), to_peer)
    turn = pl.program_id(0) * pl.num_programs(1) + pl.program_id(1)

    @pl.when(turn == 0)
    def _():
        barrier = pltpu.get_barrier_semaphore()
        for peer in square_peers() + [to_peer["x"], to_peer["zh"]]:
            pl.semaphore_signal(barrier, inc=1, device_id=peer, device_id_type=MESH)
        pl.semaphore_wait(barrier, 5)
        plan("begin")

    @pl.when(turn == pl.num_programs(1))
    def _():
        plan("middle")

    tile = pl.program_id(1)
    rows = query.shape[0]
    query_tile = query[...]
    grad_tile = contract_cols(branch[...], weight[...]).astype(jnp.bfloat16)
    centre_row = jnp.transpose(
        jnp.sum(grad_tile.astype(jnp.float32) * attended[...], axis=1, keepdims=True)
    )
    log_row = log_total[0, :1, :]
    first_row = first[:1, :]
    key_index = lax.broadcasted_iota(jnp.int32, (rows, rows), 0)
    query_index = lax.broadcasted_iota(jnp.int32, (rows, rows), 1)

    def block(index, summed, diagonal):
        at = pl.ds(pl.multiple_of(index * rows, rows), rows)
        key_block = key[at, :]
        scores = contract_cols(key_block, query_tile)
        visible = key_index + index * rows >= first_row
        if diagonal:
            visible = visible & (key_index <= query_index)
        probability = jnp.where(visible, jnp.exp(scores - log_row), 0.0)
        grad_prob = contract_cols(value[at, :], grad_tile)
        grad_scores = (probability * (grad_prob - centre_row)).astype(jnp.bfloat16)
        key_part = matmul(grad_scores, query_tile)
        value_part = matmul(probability.astype(jnp.bfloat16), grad_tile)
        if diagonal:
            key_sum[at, :] = key_part
            value_sum[at, :] = value_part
        else:
            key_sum[at, :] += key_part
            value_sum[at, :] += value_part
        return summed + contract_rows(grad_scores, key_block)

    def turn_back(part, at):
        return part * cos[at, :] - pltpu.roll(part, HEAD_DIM // 2, 1) * sin[at, :]

    summed = lax.fori_loop(
        0,
        tile,
        lambda index, kept: block(index, kept, False),
        jnp.zeros((rows, HEAD_DIM), jnp.float32),
    )
    summed = block(tile, summed, True)
    here = pl.ds(pl.multiple_of(tile * rows, rows), rows)
    grad_query[...] = (turn_back(summed, here) * HEAD_DIM ** (-0.5)).astype(jnp.bfloat16)

    @pl.when(tile == pl.num_programs(1) - 1)
    def _():
        @pl.loop(0, pl.num_programs(1))
        def _(index):
            at = pl.ds(pl.multiple_of(index * rows, rows), rows)
            grad_key[at, :] = turn_back(key_sum[at, :], at).astype(jnp.bfloat16)
            grad_value[at, :] = value_sum[at, :].astype(jnp.bfloat16)

    @pl.when(turn == pl.num_programs(0) * pl.num_programs(1) - 1)
    def _():
        plan("end")


def attention_backward(
    query,
    key,
    value,
    grad_branch,
    units,
    attended,
    log_total,
    first_key,
    cosine,
    sine_table,
    tile_rows,
    guests,
    plan,
):
    length, width = query.shape
    model_width = grad_branch.shape[1]
    heads = width // HEAD_DIM
    whole = pl.BlockSpec((length, HEAD_DIM), lambda head, tile: (0, head))
    part = pl.BlockSpec((tile_rows, HEAD_DIM), lambda head, tile: (tile, head))
    table = pl.BlockSpec((length, HEAD_DIM), lambda head, tile: (0, 0))
    shape = jax.ShapeDtypeStruct((length, width), jnp.bfloat16)
    anywhere = pl.BlockSpec(memory_space=pl.ANY)
    arrays = [array for guest in guests for array, _ in guest.inputs]

    def place(kind):
        if kind is None:
            return anywhere
        return pl.BlockSpec(
            kind, lambda head, tile: (0,) * len(kind), pipeline_mode=pl.Buffered(1)
        )

    outputs = [output for guest in guests for output in guest.outputs]
    return pl.pallas_call(
        functools.partial(attention_backward_kernel, guests, plan),
        grid=(heads, length // tile_rows),
        in_specs=[
            part,
            whole,
            whole,
            pl.BlockSpec((tile_rows, model_width), lambda head, tile: (tile, 0)),
            pl.BlockSpec((HEAD_DIM, model_width), lambda head, tile: (3 * heads + head, 0)),
            part,
            pl.BlockSpec((1, 8, tile_rows), lambda head, tile: (head, 0, tile)),
            pl.BlockSpec((8, tile_rows), lambda head, tile: (0, tile)),
            table,
            table,
        ]
        + [place(kind) for guest in guests for _, kind in guest.inputs],
        out_specs=[part, whole, whole] + [place(kind) for _, kind in outputs],
        out_shape=[shape, shape, shape] + [output for output, _ in outputs],
        scratch_shapes=[
            pltpu.VMEM((length, HEAD_DIM), jnp.float32),
            pltpu.VMEM((length, HEAD_DIM), jnp.float32),
        ]
        + [shape for guest in guests for shape in guest.scratch],
        compiler_params=pltpu.CompilerParams(
            collective_id=6, has_side_effects=True, vmem_limit_bytes=56 * 1024 * 1024
        ),
        cost_estimate=pl.CostEstimate(
            flops=5 * length * length * width + 2 * length * width * model_width,
            bytes_accessed=24 * length * width,
            transcendentals=length * length * heads // 2,
        ),
        name="attention_backward",
    )(
        query,
        key,
        value,
        grad_branch,
        units,
        attended,
        log_total,
        first_key,
        cosine,
        sine_table,
        *arrays,
    )


def opening(keep, give, attention_parts):
    bf16 = jnp.bfloat16
    rows, model_width = keep.shape
    _, first_units, width = attention_parts.shape
    block_width = QUARTERS * width
    piece_rows = first_units // 64 * 16
    cuts = (0, piece_rows, 2 * piece_rows, 3 * piece_rows, first_units)
    pieces = len(cuts) - 1

    def kernel(
        keep_ref,
        give_ref,
        first_ref,
        own,
        full,
        units,
        tok_out,
        tok_in,
        full_out,
        full_in,
        first_out,
        first_in,
        far_out,
        far_in,
        local,
    ):
        x, zh, zl, y, core = (lax.axis_index(axis) for axis in ("x", "zh", "zl", "y", "c"))
        to_x, to_zh, to_zl = {"x": 1 - x}, {"zh": 1 - zh}, {"zl": 1 - zl}
        to_y, to_core, to_both = {"y": 1 - y}, {"c": 1 - core}, {"zl": 1 - zl, "y": 1 - y}
        chip = 2 * zl + y
        member = 2 * chip + core
        along_y, along_zl = member + 2 - 4 * y, member + 4 - 8 * zl
        opposite = along_y + 4 - 8 * zl

        barrier = pltpu.get_barrier_semaphore()
        for peer in (to_x, to_zh, to_zl, to_y, to_core, to_both):
            pl.semaphore_signal(barrier, inc=1, device_id=peer, device_id_type=MESH)
        pl.semaphore_wait(barrier, 6)

        def remote(source, target, sent, landed, peer):
            return pltpu.make_async_remote_copy(
                source, target, sent, landed, device_id=peer, device_id_type=MESH
            )

        def columns(index, size):
            return pl.ds(pl.multiple_of(index * size, size), size)

        swap_tokens = remote(give_ref, own.at[zh], tok_out, tok_in, to_zh)
        swap_tokens.start()
        keep_own = pltpu.make_async_copy(keep_ref, own.at[zh], local.at[0])
        keep_full = pltpu.make_async_copy(keep_ref, full.at[zh, member], local.at[1])
        keep_own.start()
        keep_full.start()

        peers = ((to_y, chip + 1 - 2 * y), (to_zl, chip + 2 - 4 * zl), (to_both, 3 - chip))
        spread = []
        for piece in range(pieces):
            at = pl.ds(cuts[piece], cuts[piece + 1] - cuts[piece])
            group = []
            for index, (peer, other) in enumerate(peers):
                slot = 3 * piece + index
                group.append(
                    remote(
                        first_ref.at[other, at],
                        units.at[at, columns(chip, width)],
                        first_out.at[slot],
                        first_in.at[slot],
                        peer,
                    )
                )
            here = pltpu.make_async_copy(
                first_ref.at[chip, at], units.at[at, columns(chip, width)], local.at[2 + piece]
            )
            spread.append((group, here))

        def start_spread(piece):
            group, here = spread[piece]
            for copy in group:
                copy.start()
            here.start()

        start_spread(0)

        def gather(index, source, half, place, peer):
            return remote(
                source, full.at[half, place], full_out.at[index], full_in.at[index], peer
            )

        def onward(index, half, place, peer):
            return gather(index, full.at[half, place], half, place, peer)

        late = 1 - zh
        copies = [
            gather(0, keep_ref, zh, member, to_y),
            gather(1, own.at[late], late, member, to_y),
            gather(2, own.at[late], late, member, to_zl),
            gather(3, keep_ref, zh, member, to_zl),
            gather(4, keep_ref, zh, member, to_core),
            onward(5, zh, along_zl, to_y),
            onward(6, late, along_zl, to_y),
            onward(7, zh, along_y, to_core),
            onward(8, late, along_y, to_core),
            onward(9, zh, along_zl, to_core),
            onward(10, late, along_zl, to_core),
            onward(11, zh, opposite, to_core),
            onward(12, late, opposite, to_core),
            gather(13, own.at[late], late, member, to_core),
        ]
        far = []
        for piece in range(pieces):
            at = pl.ds(cuts[piece], cuts[piece + 1] - cuts[piece])

            def block(index, rows_at=at):
                return units.at[rows_at, pl.ds(index * block_width, block_width)]

            def hop(slot, source, target, peer):
                return remote(block(source), block(target), far_out.at[slot], far_in.at[slot], peer)

            far.append(
                (
                    hop(3 * piece, 0, 1, to_zh),
                    hop(3 * piece + 1, 0, 2, to_x),
                    hop(3 * piece + 2, 1, 3, to_x),
                )
            )

        for piece, (group, here) in enumerate(spread):
            for copy in group:
                copy.wait_recv()
            here.wait()
            if piece == 0:
                far[0][0].start()
                for index in (0, 3, 4):
                    copies[index].start()
                for following in range(1, pieces):
                    start_spread(following)
            far[piece][1].start()

        def pass_on(piece):
            far[piece][0].wait_recv()
            if piece + 1 < pieces:
                far[piece + 1][0].start()
            far[piece][2].start()

        copies[3].wait_recv()
        copies[5].start()
        copies[9].start()
        copies[0].wait_recv()
        copies[7].start()
        pass_on(0)
        swap_tokens.wait_recv()
        for index in (2, 1, 13):
            copies[index].start()
        late_full = pltpu.make_async_copy(
            own.at[late], full.at[late, member], local.at[2 + pieces]
        )
        late_full.start()
        pass_on(1)
        copies[2].wait_recv()
        copies[6].start()
        copies[10].start()
        copies[1].wait_recv()
        copies[8].start()
        pass_on(2)
        copies[5].wait_recv()
        copies[11].start()
        copies[6].wait_recv()
        copies[12].start()
        pass_on(3)
        for index in (4, 7, 8, 9, 10, 11, 12, 13):
            copies[index].wait_recv()
        for group in far:
            group[1].wait_recv()
            group[2].wait_recv()
        swap_tokens.wait_send()
        for group, _ in spread:
            for copy in group:
                copy.wait_send()
        for copy in copies:
            copy.wait_send()
        for group in far:
            for copy in group:
                copy.wait_send()
        for copy in (keep_own, keep_full, late_full):
            copy.wait()

    dma = pltpu.SemaphoreType.DMA
    anywhere = pl.BlockSpec(memory_space=pl.ANY)
    inside = pl.BlockSpec(memory_space=pltpu.VMEM)
    shape = jax.ShapeDtypeStruct
    own, full, units = pl.pallas_call(
        kernel,
        in_specs=[inside] * 3,
        out_specs=[inside, anywhere, anywhere],
        out_shape=[
            shape((2, rows, model_width), bf16),
            shape((2, MEMBERS, rows, model_width), bf16),
            shape((first_units, model_width), bf16),
        ],
        scratch_shapes=[
            dma(()),
            dma(()),
            dma((14,)),
            dma((14,)),
            dma((3 * pieces,)),
            dma((3 * pieces,)),
            dma((3 * pieces,)),
            dma((3 * pieces,)),
            dma((3 + pieces,)),
        ],
        compiler_params=pltpu.CompilerParams(collective_id=0, has_side_effects=True),
        cost_estimate=pl.CostEstimate(
            flops=0, bytes_accessed=200 * 1024 * 1024, transcendentals=0
        ),
        name="opening",
    )(keep, give, attention_parts)
    return own, full.reshape(2 * MEMBERS * rows, model_width), units


def group_device(
    tokens,
    doc_starts,
    query_weight,
    key_weight,
    value_weight,
    out_weight,
    gate_weight,
    up_weight,
    down_weight,
    attention_gain,
    feedforward_gain,
    cotangent,
):
    bf16, f32 = jnp.bfloat16, jnp.float32
    x_at, zh_at, core = (lax.axis_index(name) for name in ("x", "zh", "c"))
    streams, shard_rows, model_width = tokens.shape
    slice_width = query_weight.shape[0]
    half_rows = shard_rows // 2
    own_rows = 2 * half_rows
    length = MEMBERS * own_rows
    block_width = QUARTERS * slice_width
    head_width = query_weight.shape[1] // QUARTERS
    hidden = gate_weight.shape[1] // QUARTERS
    local_heads = head_width // HEAD_DIM

    def reorder(values, x_from, zh_from):
        quarters = [values[..., i * block_width : (i + 1) * block_width] for i in range(4)]
        pairs = [jnp.where(zh_from == 0, quarters[i], quarters[i ^ 1]) for i in range(4)]
        return jnp.concatenate(
            [jnp.where(x_from == 0, pairs[i], pairs[i ^ 2]) for i in range(4)], axis=-1
        )

    def for_group(values):
        mine = lax.dynamic_slice_in_dim(values, core * half_rows, half_rows, 1)
        keep = lax.dynamic_index_in_dim(mine, zh_at, 0, keepdims=False)
        give = lax.dynamic_index_in_dim(mine, 1 - zh_at, 0, keepdims=False)
        return reorder(keep, x_at, zh_at), reorder(give, x_at, 1 - zh_at)

    def units_of(weight):
        return weight.reshape(QUARTERS, -1, slice_width)

    gains = jnp.concatenate(
        [attention_gain[None], feedforward_gain[None], jnp.zeros((14, slice_width), bf16)]
    )
    gains = jnp.broadcast_to(gains[None], (QUARTERS, 16, slice_width))
    token_keep, token_give = for_group(tokens)
    own_tokens, all_tokens, attention_units = opening(
        token_keep,
        token_give,
        jnp.concatenate(
            [
                units_of(query_weight.T),
                units_of(key_weight.T),
                units_of(value_weight.T),
                units_of(out_weight),
                gains,
            ],
            axis=1,
        ),
    )
    feedforward_parts = jnp.concatenate(
        [units_of(gate_weight.T), units_of(up_weight.T), units_of(down_weight)], axis=1
    )

    positions = jnp.arange(length, dtype=jnp.int32)
    cosine, sine_table = rotary_tables(positions)
    cosine = jnp.concatenate([cosine, cosine], axis=1)
    sine_table = jnp.concatenate([-sine_table, sine_table], axis=1)
    starts = lax.dynamic_index_in_dim(doc_starts, zh_at, 0, keepdims=False)
    first_key = jnp.max(
        jnp.where(starts[None, :] <= positions[:, None], starts[None, :], 0), axis=1
    )
    cotangent_keep, cotangent_give = for_group(cotangent)
    normed, query_rot, key_rot, value_low, square_units, cotangent_got = project(
        all_tokens,
        attention_units,
        head_width,
        cosine,
        sine_table,
        feedforward_parts,
        cotangent_give,
    )
    own_cotangent = jnp.stack(
        [
            jnp.where(zh_at == 0, cotangent_keep, cotangent_got),
            jnp.where(zh_at == 0, cotangent_got, cotangent_keep),
        ]
    )
    all_cotangent = lax.all_gather(own_cotangent, GROUP, axis=1, tiled=True).reshape(
        length, model_width
    )
    tile_rows = min(512, length)
    attended, heads_out, log_total = attention_forward(
        query_rot, key_rot, value_low, first_key[:, None], tile_rows
    )
    gains_at = (attention_units, 16, attention_units.shape[0] // 16 - 1)

    def after_attention(total, half, at, states, kept, own):
        token_ref, gain_ref = states
        residual = token_ref[half, at, :].astype(f32) + total
        kept[half, at, :] = residual
        gain = gain_ref[1:2, :].astype(f32)
        own[half, at, :] = (residual * rms_scale(residual) * gain).astype(bf16)

    far_gather = FarGather(square_units, hidden // 2)

    def plan_branch(stage, number=0):
        if stage == "begin":
            far_gather.begin()
        elif stage == "end":
            far_gather.end()
        else:
            far_gather.advance({"sent": 2, "closed": 2, "passed": 0, "spread": 0}[stage])

    residual, normed_ffn, feedforward_units = exchange(
        "branch_exchange",
        1,
        [
            dict(
                lefts=[heads_out],
                rights=[(attention_units, head_width, 3)],
                states=[(own_tokens, None, 0), gains_at],
                finish=after_attention,
                kept=f32,
                gathers=True,
            )
        ],
        ("zl", "y"),
        [far_gather],
        plan_branch,
    )
    mixed_hidden, grad_gate_low, grad_up_low, partial = feedforward(
        normed_ffn, all_cotangent, feedforward_units, hidden
    )
    grad_down = contract_rows(mixed_hidden, all_cotangent).astype(bf16)
    grad_gate = contract_rows(grad_gate_low, normed_ffn).astype(bf16)
    grad_up = contract_rows(grad_up_low, normed_ffn).astype(bf16)

    def after_feedforward(total, half, at, states, kept, own):
        residual_ref, cotangent_ref, gain_ref = states
        rows = residual_ref[half, at, :]
        scale = rms_scale(rows)
        weighted = total * gain_ref[1:2, :].astype(f32)
        mean = jnp.mean(weighted * rows, axis=-1, keepdims=True)
        grad = cotangent_ref[half, at, :].astype(f32) + scale * weighted - rows * scale**3 * mean
        kept[half, at, :] = grad
        own[half, at, :] = grad.astype(bf16)

    far_grads = [FarReduce(grad_down), FarReduce(grad_gate), FarReduce(grad_up, stop=True)]

    def plan_feedforward(stage, number=0):
        if stage == "begin":
            far_grads[0].begin()
        elif stage == "sent":
            far_grads[1].begin()
            far_grads[0].advance()
        elif stage == "closed":
            far_grads[2].begin()
            far_grads[1].advance()
        elif stage == "end":
            far_grads[2].advance()
            for guest in far_grads:
                guest.end()

    grad_residual, grad_branch, grad_down, grad_gate, grad_up = exchange(
        "feedforward_exchange",
        2,
        [
            dict(
                lefts=[grad_gate_low, grad_up_low],
                rights=[(feedforward_units, hidden, 0), (feedforward_units, hidden, 1)],
                states=[(residual, None, 0), (own_cotangent, None, 0), gains_at],
                finish=after_feedforward,
                kept=f32,
                gathers=True,
            )
        ],
        ("zl", "y"),
        far_grads,
        plan_feedforward,
    )
    partial, _ = lax.optimization_barrier((partial, grad_branch))
    hidden_sum = lax.psum_scatter(
        partial.reshape(2, length // 2, model_width), GROUP, scatter_dimension=1, tiled=True
    )
    grad_out = contract_rows(heads_out, grad_branch).astype(bf16)
    side_grads = [
        FarReduce(grad_up, near=True),
        FarReduce(grad_out),
        SquareReturn(grad_down),
        SquareReturn(grad_gate),
    ]

    def plan_attention(stage):
        if stage == "begin":
            for guest in side_grads:
                guest.begin()
        elif stage == "middle":
            side_grads[1].advance()
        else:
            for guest in side_grads:
                guest.end()

    *grad_heads_in, grad_up, grad_out, spread_down, spread_gate = attention_backward(
        query_rot,
        key_rot,
        value_low,
        grad_branch,
        attention_units,
        attended,
        log_total,
        jnp.broadcast_to(first_key[None], (8, length)),
        cosine,
        sine_table,
        tile_rows,
        side_grads,
        plan_attention,
    )
    grad_projections = [contract_rows(grad, normed).astype(bf16) for grad in grad_heads_in]

    def after_all(total, half, at, states, kept, own):
        token_ref, grad_ref, gain_ref = states
        rows = token_ref[half, at, :].astype(f32)
        scale = rms_scale(rows)
        weighted = total * gain_ref[0:1, :].astype(f32)
        mean = jnp.mean(weighted * rows, axis=-1, keepdims=True)
        kept[half, at, :] = grad_ref[half, at, :] + scale * weighted - rows * scale**3 * mean

    late_grads = [FarReduce(grad) for grad in grad_projections]

    def plan_tokens(stage, number=0):
        if stage == "begin":
            late_grads[0].begin()
        elif stage == "sent":
            late_grads[1].begin()
            late_grads[2].begin()
            late_grads[0].advance()
        elif stage == "closed":
            late_grads[1].advance()
            late_grads[2].advance()
        elif stage == "end":
            for guest in late_grads:
                guest.end()

    grad_own, *late_grads_own = exchange(
        "token_exchange",
        3,
        [
            dict(
                lefts=list(grad_heads_in),
                rights=[(attention_units, head_width, at) for at in range(3)],
                states=[(own_tokens, None, 0), (grad_residual, None, 0), gains_at],
                finish=after_all,
                kept=f32,
                gathers=False,
            ),
        ],
        ("zl", "y"),
        late_grads,
        plan_tokens,
    )

    grad_own = reorder(grad_own, x_at, zh_at)
    own_output = reorder((residual + hidden_sum.astype(f32)).astype(bf16), x_at, zh_at)
    *spread_grads, output, grad_tokens = closing(
        [grad_up, grad_out] + late_grads_own,
        lax.dynamic_index_in_dim(own_output, zh_at, 0, keepdims=False),
        lax.dynamic_index_in_dim(own_output, 1 - zh_at, 0, keepdims=False),
        lax.dynamic_index_in_dim(grad_own, zh_at, 0, keepdims=False),
        lax.dynamic_index_in_dim(grad_own, 1 - zh_at, 0, keepdims=False).astype(bf16),
    )
    spread_grads = [spread_down, spread_gate] + spread_grads

    def columns(grads):
        return grads.reshape(-1, slice_width).astype(f32)

    grad_down_w, grad_gate_w, grad_up_w, grad_out_w, *projection_grads = (
        columns(grads) for grads in spread_grads
    )
    grad_gate_w, grad_up_w = grad_gate_w.T, grad_up_w.T
    grad_query_w, grad_key_w, grad_value_w = (grads.T for grads in projection_grads)

    def gain_sum(*pairs):
        return sum(jnp.sum(weight.astype(f32) * grad, axis=1) for weight, grad in pairs)

    sums = jnp.stack(
        [
            gain_sum(
                (query_weight, grad_query_w), (key_weight, grad_key_w), (value_weight, grad_value_w)
            ),
            gain_sum((gate_weight, grad_gate_w), (up_weight, grad_up_w)),
        ]
    )
    sums = sums + swap(sums, "c")
    return (
        output,
        grad_tokens,
        grad_query_w,
        grad_key_w,
        grad_value_w,
        grad_out_w,
        grad_gate_w,
        grad_up_w,
        grad_down_w,
        sums[0] / attention_gain.astype(f32),
        sums[1] / feedforward_gain.astype(f32),
    )


def placements(stream, seq, head):
    both = (stream + seq) if isinstance(stream, tuple) else (stream, seq)
    in_specs = (
        P(stream, seq, None),
        P(stream, None),
        P(both, head),
        P(both, head),
        P(both, head),
        P(head, both),
        P(both, head),
        P(both, head),
        P(head, both),
        P(both),
        P(both),
        P(stream, seq, None),
    )
    out_specs = (
        P(stream, seq, None),
        P(stream, seq, None),
        P(both, head),
        P(both, head),
        P(both, head),
        P(head, both),
        P(both, head),
        P(both, head),
        P(head, both),
        P(both),
        P(both),
    )
    return in_specs, out_specs


def solution(mesh):
    def run(*arguments):
        tokens, doc_starts = arguments[:2]
        sizes = dict(mesh.shape)
        grouped = (
            (sizes["stream"], sizes["seq"], sizes["head"]) == (2, 8, 2)
            and tokens.shape[0] == 4
            and tokens.shape[1] <= WIN
        )
        if grouped:
            split = Mesh(mesh.devices.reshape(2, 2, 2, 2, 2), ("x", "zh", "zl", "y", "c"))
            in_specs, out_specs = placements(("x",), ("zh", "zl", "y"), "c")
            step = group_device
        else:
            split = mesh
            in_specs, out_specs = placements("stream", "seq", "head")
            step = per_device
        return jax.shard_map(
            step, mesh=split, in_specs=in_specs, out_specs=out_specs, check_vma=False
        )(*arguments)

    return run
```

```python
import functools
import math

import jax
import jax.numpy as jnp
import numpy as np
from jax import lax
from jax.experimental import pallas as pl
from jax.experimental.pallas import tpu as pltpu
from jax.sharding import Mesh
from jax.sharding import PartitionSpec as P

HEAD_DIM = 128
WIN = 2048


epsilon = 1e-06
masked_score = -1e30


def from_behind(value, axis, steps):
    count = lax.axis_size(axis)
    initial, last = (max(0, -steps), min(count, count - steps))
    return lax.ppermute(value, axis, [(source, source + steps) for source in range(initial, last)])


def matmul(left, right):
    return jnp.dot(left, right, preferred_element_type=jnp.float32)


def contract_rows(left, right):
    return lax.dot_general(
        left, right, (((0,), (0,)), ((), ())), preferred_element_type=jnp.float32
    )


def contract_cols(left, right):
    return lax.dot_general(
        left, right, (((1,), (1,)), ((), ())), preferred_element_type=jnp.float32
    )


def rotary_tables(positions):
    half_dim = HEAD_DIM // 2
    frequency = jnp.exp(
        jnp.arange(half_dim).astype(jnp.float32) * (-2.0 * math.log(10000.0) / HEAD_DIM)
    )
    angles = positions.astype(jnp.float32)[:, None] * frequency[None, :]
    return (jnp.cos(angles), jnp.sin(angles))


def rotate_pairs(values, cosine, sine_table):
    half_dim = values.shape[-1] // 2
    first_half = values[..., :half_dim]
    second_half = values[..., half_dim:]
    return jnp.concatenate(
        [
            first_half * cosine - second_half * sine_table,
            second_half * cosine + first_half * sine_table,
        ],
        axis=-1,
    )


def unrotate_pairs(values, cosine, sine_table):
    half_dim = values.shape[-1] // 2
    first_half = values[..., :half_dim]
    second_half = values[..., half_dim:]
    return jnp.concatenate(
        [
            first_half * cosine + second_half * sine_table,
            second_half * cosine - first_half * sine_table,
        ],
        axis=-1,
    )


def document_number(starts, positions):
    return jnp.sum((starts[:, None, :] <= positions[None, :, None]).astype(jnp.int32), axis=2)


def rms_scale(values):
    return lax.rsqrt(jnp.mean(values * values, axis=-1, keepdims=True) + epsilon)


def norm_backward(grad_normed, inputs, row_scale, gain_vector):
    gain_grad = jnp.sum(grad_normed * inputs * row_scale, axis=0)
    weighted = grad_normed * gain_vector
    grad_inputs = row_scale * weighted - inputs * row_scale**3 * jnp.mean(
        weighted * inputs, axis=-1, keepdims=True
    )
    return (grad_inputs, gain_grad)


def per_device(
    tokens,
    doc_starts,
    query_weight,
    key_weight,
    value_weight,
    out_weight,
    gate_weight,
    up_weight,
    down_weight,
    attention_gain,
    feedforward_gain,
    cotangent,
):
    gathered = (
        lax.all_gather(query_weight, ("stream", "seq"), axis=0, tiled=True),
        lax.all_gather(key_weight, ("stream", "seq"), axis=0, tiled=True),
        lax.all_gather(value_weight, ("stream", "seq"), axis=0, tiled=True),
        lax.all_gather(out_weight, ("stream", "seq"), axis=1, tiled=True),
        lax.all_gather(gate_weight, ("stream", "seq"), axis=0, tiled=True),
        lax.all_gather(up_weight, ("stream", "seq"), axis=0, tiled=True),
        lax.all_gather(down_weight, ("stream", "seq"), axis=1, tiled=True),
        lax.all_gather(attention_gain, ("stream", "seq"), axis=0, tiled=True),
        lax.all_gather(feedforward_gain, ("stream", "seq"), axis=0, tiled=True),
    )
    (
        full_query,
        full_key,
        full_value,
        full_out,
        full_gate,
        full_up,
        full_down,
        full_gain_first,
        full_gain_second,
    ) = gathered
    streams, shard_rows, model_width = tokens.shape
    head_width = full_query.shape[1]
    local_heads = head_width // HEAD_DIM
    flat_rows = streams * shard_rows
    seq_index = lax.axis_index("seq")
    halo_shards = min(WIN // shard_rows, lax.axis_size("seq") - 1)
    window_rows = (halo_shards + 1) * shard_rows
    inputs = tokens.reshape(flat_rows, model_width).astype(jnp.float32)
    scale_first = rms_scale(inputs)
    gain_first = full_gain_first.astype(jnp.float32)
    normed = (inputs * scale_first * gain_first).astype(jnp.bfloat16)
    query_proj = matmul(normed, full_query).reshape(streams, shard_rows, local_heads, HEAD_DIM)
    key_proj = matmul(normed, full_key).reshape(streams, shard_rows, local_heads, HEAD_DIM)
    value_low = (
        matmul(normed, full_value).astype(jnp.bfloat16).reshape(streams, shard_rows, head_width)
    )
    positions = seq_index * shard_rows + jnp.arange(shard_rows, dtype=jnp.int32)
    cosine, sine_table = rotary_tables(positions)
    cosine = cosine[None, :, None, :]
    sine_table = sine_table[None, :, None, :]
    query_rot = (rotate_pairs(query_proj, cosine, sine_table) * HEAD_DIM ** (-0.5)).astype(
        jnp.bfloat16
    )
    key_rot = rotate_pairs(key_proj, cosine, sine_table).astype(jnp.bfloat16)
    paired = jnp.stack([key_rot.reshape(streams, shard_rows, head_width), value_low])
    pieces = []
    for distance in range(halo_shards, 0, -1):
        pieces.append(from_behind(paired, "seq", distance))
    window = jnp.concatenate(pieces + [paired], axis=2)
    key_positions = (seq_index - halo_shards) * shard_rows + jnp.arange(
        window_rows, dtype=jnp.int32
    )
    query_docs = document_number(doc_starts, positions)
    key_docs = document_number(doc_starts, key_positions)
    offsets = positions[:, None] - key_positions[None, :]
    allowed = ((offsets >= 0) & (offsets < WIN))[None] & (
        query_docs[:, :, None] == key_docs[:, None, :]
    )
    query_heads = jnp.transpose(query_rot, (2, 0, 1, 3))
    key_heads = jnp.transpose(
        window[0].reshape(streams, window_rows, local_heads, HEAD_DIM), (2, 0, 1, 3)
    )
    value_heads = jnp.transpose(
        window[1].reshape(streams, window_rows, local_heads, HEAD_DIM), (2, 0, 1, 3)
    )

    def head_forward(operands):
        query_one, key_one, value_one = operands
        scores = jnp.einsum("sqe,ske->sqk", query_one, key_one, preferred_element_type=jnp.float32)
        scores = jnp.where(allowed, scores, masked_score)
        largest = jnp.max(scores, axis=-1, keepdims=True)
        weights = jnp.exp(scores - largest)
        totals = jnp.sum(weights, axis=-1, keepdims=True)
        probability = (weights / totals).astype(jnp.bfloat16)
        attended = jnp.einsum(
            "sqk,ske->sqe", probability, value_one, preferred_element_type=jnp.float32
        )
        return (attended, (largest + jnp.log(totals))[..., 0])

    attended, log_totals = lax.map(head_forward, (query_heads, key_heads, value_heads))
    heads_out = (
        jnp.transpose(attended, (1, 2, 0, 3)).reshape(flat_rows, head_width).astype(jnp.bfloat16)
    )
    attention_sum = lax.psum(matmul(heads_out, full_out), "head")
    residual = inputs + attention_sum
    scale_second = rms_scale(residual)
    gain_second = full_gain_second.astype(jnp.float32)
    normed_ffn = (residual * scale_second * gain_second).astype(jnp.bfloat16)
    gate_proj = matmul(normed_ffn, full_gate)
    up_proj = matmul(normed_ffn, full_up)
    sigmoid_gate = jax.nn.sigmoid(gate_proj)
    silu_gate = gate_proj * sigmoid_gate
    mixed_hidden = (silu_gate * up_proj).astype(jnp.bfloat16)
    feedforward_sum = lax.psum(matmul(mixed_hidden, full_down).astype(jnp.bfloat16), "head").astype(
        jnp.float32
    )
    output = (
        (residual + feedforward_sum).astype(jnp.bfloat16).reshape(streams, shard_rows, model_width)
    )
    gathered = (
        lax.all_gather(query_weight, ("stream", "seq"), axis=0, tiled=True),
        lax.all_gather(key_weight, ("stream", "seq"), axis=0, tiled=True),
        lax.all_gather(value_weight, ("stream", "seq"), axis=0, tiled=True),
        lax.all_gather(out_weight, ("stream", "seq"), axis=1, tiled=True),
        lax.all_gather(gate_weight, ("stream", "seq"), axis=0, tiled=True),
        lax.all_gather(up_weight, ("stream", "seq"), axis=0, tiled=True),
        lax.all_gather(down_weight, ("stream", "seq"), axis=1, tiled=True),
        lax.all_gather(attention_gain, ("stream", "seq"), axis=0, tiled=True),
        lax.all_gather(feedforward_gain, ("stream", "seq"), axis=0, tiled=True),
    )
    (
        full_query,
        full_key,
        full_value,
        full_out,
        full_gate,
        full_up,
        full_down,
        full_gain_first,
        full_gain_second,
    ) = gathered
    grad_output = cotangent.reshape(flat_rows, model_width)
    grad_down = contract_rows(mixed_hidden, grad_output)
    grad_mixed = contract_cols(grad_output, full_down)
    grad_gate_low = (
        grad_mixed * up_proj * sigmoid_gate * (1.0 + gate_proj * (1.0 - sigmoid_gate))
    ).astype(jnp.bfloat16)
    grad_up_low = (grad_mixed * silu_gate).astype(jnp.bfloat16)
    grad_gate_w = contract_rows(normed_ffn, grad_gate_low)
    grad_up_w = contract_rows(normed_ffn, grad_up_low)
    grad_normed_ffn = lax.psum(
        contract_cols(grad_gate_low, full_gate) + contract_cols(grad_up_low, full_up), "head"
    )
    grad_residual_norm, grad_gain_second = norm_backward(
        grad_normed_ffn, residual, scale_second, gain_second
    )
    grad_residual = grad_output.astype(jnp.float32) + grad_residual_norm
    grad_branch = grad_residual.astype(jnp.bfloat16)
    grad_out_w = contract_rows(heads_out, grad_branch)
    grad_heads = contract_cols(grad_branch, full_out).astype(jnp.bfloat16)
    grad_heads_major = jnp.transpose(
        grad_heads.reshape(streams, shard_rows, local_heads, HEAD_DIM), (2, 0, 1, 3)
    )

    def head_backward(operands):
        query_one, key_one, value_one, grad_one, log_one = operands
        scores = jnp.einsum("sqe,ske->sqk", query_one, key_one, preferred_element_type=jnp.float32)
        scores = jnp.where(allowed, scores, masked_score)
        probability = jnp.exp(scores - log_one[..., None])
        grad_prob = jnp.einsum(
            "sqe,ske->sqk", grad_one, value_one, preferred_element_type=jnp.float32
        )
        centre = jnp.sum(probability * grad_prob, axis=-1, keepdims=True)
        grad_scores = (probability * (grad_prob - centre)).astype(jnp.bfloat16)
        grad_query_one = jnp.einsum(
            "sqk,ske->sqe", grad_scores, key_one, preferred_element_type=jnp.float32
        )
        grad_key_one = jnp.einsum(
            "sqk,sqe->ske", grad_scores, query_one, preferred_element_type=jnp.float32
        )
        grad_value_one = jnp.einsum(
            "sqk,sqe->ske",
            probability.astype(jnp.bfloat16),
            grad_one,
            preferred_element_type=jnp.float32,
        )
        return (grad_query_one, grad_key_one, grad_value_one)

    grad_query_heads, grad_key_heads, grad_value_heads = lax.map(
        head_backward, (query_heads, key_heads, value_heads, grad_heads_major, log_totals)
    )
    grad_window = jnp.transpose(
        jnp.stack([grad_key_heads, grad_value_heads]), (0, 2, 3, 1, 4)
    ).reshape(2, streams, window_rows, head_width)
    grad_paired = grad_window[:, :, halo_shards * shard_rows :]
    for distance in range(halo_shards, 0, -1):
        index_piece = halo_shards - distance
        grad_paired = grad_paired + from_behind(
            grad_window[:, :, index_piece * shard_rows : (index_piece + 1) * shard_rows],
            "seq",
            -distance,
        )
    grad_key_rot = grad_paired[0].reshape(streams, shard_rows, local_heads, HEAD_DIM)
    grad_query_rot = jnp.transpose(grad_query_heads, (1, 2, 0, 3))
    grad_query_low = (
        (unrotate_pairs(grad_query_rot, cosine, sine_table) * HEAD_DIM ** (-0.5))
        .reshape(flat_rows, head_width)
        .astype(jnp.bfloat16)
    )
    grad_key_low = (
        unrotate_pairs(grad_key_rot, cosine, sine_table)
        .reshape(flat_rows, head_width)
        .astype(jnp.bfloat16)
    )
    grad_value_low = grad_paired[1].reshape(flat_rows, head_width).astype(jnp.bfloat16)
    grad_query_w = contract_rows(normed, grad_query_low)
    grad_key_w = contract_rows(normed, grad_key_low)
    grad_value_w = contract_rows(normed, grad_value_low)
    grad_normed = lax.psum(
        contract_cols(grad_query_low, full_query)
        + contract_cols(grad_key_low, full_key)
        + contract_cols(grad_value_low, full_value),
        "head",
    )
    grad_inputs_norm, grad_gain_first = norm_backward(grad_normed, inputs, scale_first, gain_first)
    grad_tokens = (grad_residual + grad_inputs_norm).reshape(streams, shard_rows, model_width)
    reduced = (
        lax.psum_scatter(grad_query_w, ("stream", "seq"), scatter_dimension=0, tiled=True),
        lax.psum_scatter(grad_key_w, ("stream", "seq"), scatter_dimension=0, tiled=True),
        lax.psum_scatter(grad_value_w, ("stream", "seq"), scatter_dimension=0, tiled=True),
        lax.psum_scatter(grad_out_w, ("stream", "seq"), scatter_dimension=1, tiled=True),
        lax.psum_scatter(grad_gate_w, ("stream", "seq"), scatter_dimension=0, tiled=True),
        lax.psum_scatter(grad_up_w, ("stream", "seq"), scatter_dimension=0, tiled=True),
        lax.psum_scatter(grad_down, ("stream", "seq"), scatter_dimension=1, tiled=True),
        lax.psum_scatter(grad_gain_first, ("stream", "seq"), scatter_dimension=0, tiled=True),
        lax.psum_scatter(grad_gain_second, ("stream", "seq"), scatter_dimension=0, tiled=True),
    )
    return (
        output,
        grad_tokens,
        reduced[0],
        reduced[1],
        reduced[2],
        reduced[3],
        reduced[4],
        reduced[5],
        reduced[6],
        reduced[7],
        reduced[8],
    )


GROUP = ("x", "y", "c")
MEMBERS = 8
QUARTERS = 4
MESH = pl.DeviceIdType.MESH


def turning_tables(length):
    half_dim = HEAD_DIM // 2
    frequency = np.exp(
        np.arange(half_dim).astype(np.float32) * np.float32(-2.0 * math.log(10000.0) / HEAD_DIM)
    )
    angles = np.arange(length).astype(np.float32)[:, None] * frequency[None, :]
    cosine, sine = np.cos(angles), np.sin(angles)
    return (
        jnp.asarray(np.concatenate([cosine, cosine], axis=1)),
        jnp.asarray(np.concatenate([-sine, sine], axis=1)),
    )


def swap(value, axis):
    return lax.ppermute(value, axis, [(0, 1), (1, 0)])


def remote_copy(source, target, sent, landed, peer):
    return pltpu.make_async_remote_copy(
        source, target, sent, landed, device_id=peer, device_id_type=MESH
    )


def lanes(index, size):
    return pl.ds(pl.multiple_of(index * size, size), size)


def plane_x(plane):
    return (plane + plane // 2) % 2


def plane_of(x, index):
    return x * (1 + index) + (1 - x) * 3 * index


def keeper_x(plane, core):
    return (1 - plane_x(plane) + core) % 2


def source_plane(half, x, core):
    side = (x + core) % 2
    return 2 * half + (side if half else 1 - side)


def slot_of(half, x, y, core):
    side = (x + core) % 2
    return 4 * (side if half else 1 - side) + 2 * y + core


def square_peers():
    x, y = lax.axis_index("x"), lax.axis_index("y")
    return [{"y": 1 - y}, {"x": 1 - x}, {"x": 1 - x, "y": 1 - y}]


def signal_and_wait(peers, others=()):
    barrier = pltpu.get_barrier_semaphore()
    number = len(peers)
    for peer in peers:
        pl.semaphore_signal(barrier, inc=1, device_id=peer, device_id_type=MESH)
    for peer, own in others:
        number = number + jnp.where(own, 0, 1)

        @pl.when(jnp.logical_not(own))
        def _(peer=peer):
            pl.semaphore_signal(barrier, inc=1, device_id=peer, device_id_type=MESH)

    pl.semaphore_wait(barrier, number)


class HandBack:
    def __init__(self, kept, got, out_sems, in_sems, local):
        x, z, core = (lax.axis_index(axis) for axis in ("x", "z", "c"))
        self.stays = (core == 1) & (plane_x(z) == x)
        self.home = z // 2
        targets = [{"x": plane_x(z), "z": source_plane(half, x, core)} for half in range(2)]
        senders = [{"x": keeper_x(z, core), "z": plane_of(x, index)} for index in range(2)]
        self.others = [
            (peer, self.stays & (self.home == number))
            for group in (targets, senders)
            for number, peer in enumerate(group)
        ]
        self.kept, self.got, self.sems = kept, got, (out_sems, in_sems)
        self.targets, self.senders, self.local = targets, senders, local

    def here(self, half):
        return pltpu.make_async_copy(self.kept.at[half], self.got(self.home), self.local)

    def away(self, half):
        out_sems, in_sems = self.sems
        return remote_copy(
            self.kept.at[half],
            self.got(self.home),
            out_sems.at[half],
            in_sems.at[self.home],
            self.targets[half],
        )

    def start(self, half):
        own = self.stays & (self.home == half)

        @pl.when(own)
        def _():
            self.here(half).start()

        @pl.when(jnp.logical_not(own))
        def _():
            self.away(half).start()

    def wait_recv(self, index):
        own = self.stays & (self.home == index)
        out_sems, in_sems = self.sems
        place = self.got(index)

        @pl.when(own)
        def _():
            self.here(index).wait()

        @pl.when(jnp.logical_not(own))
        def _():
            remote_copy(
                place, place, out_sems.at[index], in_sems.at[index], self.senders[index]
            ).wait_recv()

    def wait_send(self):
        for half in range(2):
            own = self.stays & (self.home == half)

            @pl.when(jnp.logical_not(own))
            def _(half=half):
                self.away(half).wait_send()


def in_spec(shape):
    return pl.BlockSpec(shape, lambda *step: (0,) * len(shape), pipeline_mode=pl.Buffered(1))


class SquareSpread:
    def __init__(self, parts):
        _, self.height, self.width = parts.shape
        dma = pltpu.SemaphoreType.DMA
        self.shape = jax.ShapeDtypeStruct((self.height, QUARTERS * self.width), parts.dtype)
        self.scratch = [dma((3,)), dma((3,)), dma(())]

    def bind(self, parts, square, sent, landed, local):
        x, y = lax.axis_index("x"), lax.axis_index("y")
        chip = 2 * x + y
        place = square.at[:, lanes(chip, self.width)]
        others = (chip + 1 - 2 * y, chip + 2 - 4 * x, 3 - chip)
        self.copies = [
            remote_copy(parts.at[other], place, sent.at[index], landed.at[index], peer)
            for index, (peer, other) in enumerate(zip(square_peers(), others))
        ]
        self.copies.append(pltpu.make_async_copy(parts.at[chip], place, local))

    def begin(self):
        for copy in self.copies:
            copy.start()

    def end(self):
        for copy in self.copies:
            copy.wait()


class SquareReturn:
    def __init__(self, grads):
        self.height, width = grads.shape
        self.width = width // QUARTERS
        dma = pltpu.SemaphoreType.DMA
        self.shape = jax.ShapeDtypeStruct((QUARTERS, self.height, self.width), grads.dtype)
        self.scratch = [dma((3,)), dma((3,)), dma(())]

    def bind(self, grads, got, sent, landed, local):
        x, y = lax.axis_index("x"), lax.axis_index("y")
        chip = 2 * x + y
        others = (chip + 1 - 2 * y, chip + 2 - 4 * x, 3 - chip)
        self.copies = [
            remote_copy(
                grads.at[:, lanes(other, self.width)],
                got.at[chip],
                sent.at[index],
                landed.at[index],
                peer,
            )
            for index, (peer, other) in enumerate(zip(square_peers(), others))
        ]
        here = grads.at[:, lanes(chip, self.width)]
        self.copies.append(pltpu.make_async_copy(here, got.at[chip], local))

    def begin(self):
        for copy in self.copies:
            copy.start()

    def end(self):
        for copy in self.copies:
            copy.wait()


class GroupGather:
    scratch_sizes = (14, 14, 2)

    def __init__(self, own, full, sent, landed, local, to_peer, extra):
        x, y, core = (lax.axis_index(axis) for axis in GROUP)
        self.extra = extra
        self.other = ["x" if axis == "y" else "y" for axis in extra]

        def copy(index, source, half, slot, axis):
            return remote_copy(
                source, full.at[half, slot], sent.at[index], landed.at[index], to_peer[axis]
            )

        def place(half, axis):
            return slot_of(half, 1 - x if axis in ("x", "xy") else x, 1 - y if "y" in axis else y, core)

        def onward(index, half, near, axis):
            slot = place(half, near)
            return copy(index, full.at[half, slot], half, slot, axis)

        halves = range(2)
        me = [slot_of(half, x, y, core) for half in halves]
        self.direct = {
            (axis, half): copy(2 * number + half, own.at[half], half, me[half], axis)
            for number, axis in enumerate(("y", "x"))
            for half in halves
        }
        self.diagonal = [onward(4 + half, half, self.other[half], extra[half]) for half in halves]
        self.shared = [copy(6 + half, own.at[half], half, me[half], "c") for half in halves]
        self.across = [
            onward(8 + 2 * number + half, half, axis, "c")
            for number, axis in enumerate(("y", "x"))
            for half in halves
        ]
        self.last = [onward(12 + half, half, "xy", "c") for half in halves]
        self.here = [
            pltpu.make_async_copy(own.at[half], full.at[half, me[half]], local.at[half])
            for half in halves
        ]

    def start(self, half):
        self.direct[self.other[half], half].start()
        self.direct[self.extra[half], half].start()
        self.shared[half].start()
        self.here[half].start()

    def turn(self, half):
        self.direct[self.other[half], half].wait_recv()
        self.diagonal[half].start()

    def cross(self):
        for half in range(2):
            self.direct[self.extra[half], half].wait_recv()
        for copy in self.across:
            copy.start()

    def end(self):
        for half in range(2):
            self.diagonal[half].wait_recv()
            self.last[half].start()
        for copy in self.shared + self.across + self.last:
            copy.wait_recv()
        for copy in list(self.direct.values()) + self.diagonal + self.shared:
            copy.wait_send()
        for copy in self.across + self.last:
            copy.wait_send()
        for copy in self.here:
            copy.wait()


def deal(tokens, cotangent, parts, docs):
    bf16 = jnp.bfloat16
    _, shard_rows, model_width = tokens.shape
    rows = shard_rows // 2
    guests = [SquareSpread(part) for part in parts]
    part = QUARTERS * parts[0].shape[2] // 2
    planes = model_width // part // 2

    count = len(parts)

    def kernel(tokens_ref, cotangent_ref, docs_ref, *refs):
        part_refs = refs[:count]
        own_first, own_second, other_docs = refs[count : count + 3]
        square_refs = refs[count + 3 : 2 * count + 3]
        row_out, row_in, doc_out, doc_in, staged, here_sems, *scratch = refs[2 * count + 3 :]
        x, z, core = (lax.axis_index(axis) for axis in ("x", "z", "c"))
        home, stays = z // 2, (core == 1) & (plane_x(z) == x)
        targets = [{"x": keeper_x(z, core), "z": plane_of(x, index)} for index in range(2)]
        sources = [{"x": plane_x(z), "z": source_plane(half, x, core)} for half in range(2)]
        square = square_peers()
        others = [
            (peer, stays & (home == number))
            for group in (targets, sources)
            for number, peer in enumerate(group)
        ]
        signal_and_wait(square, others)
        for number, guest in enumerate(guests):
            guest.bind(
                part_refs[number], square_refs[number], *scratch[3 * number : 3 * number + 3]
            )
        guests[0].begin()
        swapped = remote_copy(docs_ref, other_docs, doc_out, doc_in, square[1])
        swapped.start()
        at = pl.ds(pl.multiple_of(core * rows, rows), rows)
        def when_own(number, index, local, away):
            source, own = staged.at[number, index], (own_first, own_second)[number]
            here = pltpu.make_async_copy(source, own.at[home], here_sems.at[number])
            sent = remote_copy(
                source,
                own.at[home],
                row_out.at[2 * number + index],
                row_in.at[2 * number + home],
                targets[index],
            )

            @pl.when(stays & (home == index))
            def _():
                local(here)

            @pl.when(jnp.logical_not(stays & (home == index)))
            def _():
                away(sent)

        for number, source in enumerate((tokens_ref, cotangent_ref)):
            for index in range(2):
                for x_part in range(2):
                    for plane in range(planes):
                        place = (2 * plane + x_part) * part
                        start = (planes * x_part + plane) * part
                        staged[number, index, :, place : place + part] = source[
                            index, at, start : start + part
                        ]
                when_own(number, index, lambda copy: copy.start(), lambda copy: copy.start())
        for guest in guests[1:]:
            guest.begin()
        for guest in guests:
            guest.end()
        swapped.wait()
        for number, own in enumerate((own_first, own_second)):
            for half in range(2):
                slot = 2 * number + half

                @pl.when(jnp.logical_not(stays & (home == half)))
                def _():
                    remote_copy(
                        own.at[half], own.at[half], row_out.at[slot], row_in.at[slot], sources[half]
                    ).wait_recv()

        for number in range(2):
            for index in range(2):
                when_own(number, index, lambda copy: copy.wait(), lambda copy: copy.wait_send())

    inside = pl.BlockSpec(memory_space=pltpu.VMEM)
    anywhere = pl.BlockSpec(memory_space=pl.ANY)
    dma = pltpu.SemaphoreType.DMA
    shape = jax.ShapeDtypeStruct
    return pl.pallas_call(
        kernel,
        in_specs=[inside] * (3 + count),
        out_specs=[inside] * 3 + [anywhere] * count,
        out_shape=[shape((2, rows, model_width), bf16)] * 2
        + [shape(docs.shape, docs.dtype)]
        + [guest.shape for guest in guests],
        scratch_shapes=[
            dma((4,)),
            dma((4,)),
            dma(()),
            dma(()),
            pltpu.VMEM((2, 2, rows, model_width), bf16),
            dma((2,)),
        ]
        + [sems for guest in guests for sems in guest.scratch],
        compiler_params=pltpu.CompilerParams(
            collective_id=0, has_side_effects=True, vmem_limit_bytes=32 * 1024 * 1024
        ),
        cost_estimate=pl.CostEstimate(flops=0, bytes_accessed=2**27, transcendentals=0),
        name="deal",
    )(tokens, cotangent, docs, *parts)


def gather_rows(first, second):
    bf16 = jnp.bfloat16
    _, rows, model_width = first.shape

    def kernel(own_first, own_second, full_first, full_second, *scratch):
        x, y, core = (lax.axis_index(axis) for axis in GROUP)
        to_peer = {"x": {"x": 1 - x}, "y": {"y": 1 - y}, "c": {"c": 1 - core}}
        signal_and_wait([to_peer[axis] for axis in GROUP])
        gathers = [
            GroupGather(own, full, *scratch[3 * number : 3 * number + 3], to_peer, ("x", "y"))
            for number, (own, full) in enumerate(
                ((own_first, full_first), (own_second, full_second))
            )
        ]
        for gather in gathers:
            for half in range(2):
                gather.start(half)
        for gather in gathers:
            for half in range(2):
                gather.turn(half)
            gather.cross()
        for gather in gathers:
            gather.end()

    dma = pltpu.SemaphoreType.DMA
    anywhere = pl.BlockSpec(memory_space=pl.ANY)
    inside = pl.BlockSpec(memory_space=pltpu.VMEM)
    full = jax.ShapeDtypeStruct((2, MEMBERS, rows, model_width), bf16)
    results = pl.pallas_call(
        kernel,
        in_specs=[inside] * 2,
        out_specs=[anywhere] * 2,
        out_shape=[full, full],
        scratch_shapes=[dma((size,)) for size in GroupGather.scratch_sizes] * 2,
        compiler_params=pltpu.CompilerParams(collective_id=1, has_side_effects=True),
        cost_estimate=pl.CostEstimate(flops=0, bytes_accessed=2**28, transcendentals=0),
        name="gather_rows",
    )(first, second)
    return [result.reshape(2 * MEMBERS * rows, model_width) for result in results]


def exchange(name, collective_id, jobs, extra):
    bf16, f32 = jnp.bfloat16, jnp.float32
    planes, _, strip = jobs[0]["rights"][0][0].shape
    model_width = planes * strip
    first = jobs[0]["lefts"][0]
    length = first[0].shape[1] if isinstance(first, tuple) else first.shape[0]
    rows = length // (2 * MEMBERS)
    gathers = jobs[-1]["gathers"]
    handing = [job for job in jobs if job.get("hands")]

    def block(shape, index):
        return pl.BlockSpec(shape, lambda step: index, pipeline_mode=pl.Buffered(1))

    def whole(shape):
        return block(shape, (0,) * len(shape))

    anywhere = pl.BlockSpec(memory_space=pl.ANY)
    arrays, in_specs, out_shape, out_specs = [], [], [], []
    for job in jobs:
        for left in job["lefts"]:
            if isinstance(left, tuple):
                left, at = left
                in_specs.append(block((None,) + left.shape[1:], (at, 0, 0)))
            else:
                in_specs.append(whole(left.shape))
            arrays.append(left)
        for array, height, at in job["rights"]:
            arrays.append(array)
            in_specs.append(block((planes, height, strip), (0, at, 0)))
        for array, height, at in job["states"]:
            arrays.append(array)
            in_specs.append(
                whole(array.shape) if height is None else block((planes, height, strip), (0, at, 0))
            )
        out_shape.append(jax.ShapeDtypeStruct((2, rows, model_width), job["kept"]))
        out_specs.append(whole((2, rows, model_width)))
    if gathers:
        out_shape.append(jax.ShapeDtypeStruct((2, MEMBERS, rows, model_width), bf16))
        out_specs.append(anywhere)
    for job in handing:
        out_shape.append(jax.ShapeDtypeStruct((2, rows, model_width), job["kept"]))
        out_specs.append(anywhere)
    dma = pltpu.SemaphoreType.DMA
    count = len(jobs)
    scratch = [
        pltpu.VMEM((4, 2, rows, model_width), bf16),
        pltpu.VMEM((4, 2, rows, model_width), bf16),
        pltpu.VMEM((4, 2, rows, model_width), f32),
        pltpu.VMEM((6, rows, model_width), bf16),
        pltpu.VMEM((6, rows, model_width), bf16),
        pltpu.VMEM((2, rows, model_width), bf16),
        dma((4 * count,)),
        dma((4 * count,)),
        dma((6 * count,)),
        dma((6 * count,)),
        dma((2,)),
        dma((2,)),
        dma(()),
        pltpu.SemaphoreType.REGULAR((3,)),
    ] + [dma((size,)) for size in GroupGather.scratch_sizes]

    def kernel(*refs):
        refs = list(refs)

        def take(number):
            taken = refs[:number]
            del refs[:number]
            return taken

        job_refs = [
            (take(len(job["lefts"])), take(len(job["rights"])), take(len(job["states"])))
            for job in jobs
        ]
        kept_refs = take(count)
        full = take(1)[0] if gathers else None
        handed = take(len(handing))
        (core_send, core_got, sums, link_send, link_got, own) = take(6)
        (core_out, core_in, link_out, link_in, hand_out, hand_in, hand_here, ready) = take(8)
        x, y, core = (lax.axis_index(axis) for axis in GROUP)
        to_peer = {"x": {"x": 1 - x}, "y": {"y": 1 - y}, "c": {"c": 1 - core}}
        peers = [to_peer[axis] for axis in GROUP]
        hands = []
        for number, job in enumerate(jobs):
            if job.get("hands"):
                hands.append(
                    HandBack(
                        kept_refs[number],
                        lambda index: handed[0].at[index],
                        hand_out,
                        hand_in,
                        hand_here,
                    )
                )
        signal_and_wait(peers, hands[0].others if hands else ())
        gather = GroupGather(own, full, *refs, to_peer, extra) if gathers else None

        chips = ((1 - x, 1 - y), (1 - x, y), (x, 1 - y), (x, y))

        def run(number, previous):
            left_refs, right_refs, state_refs = job_refs[number]
            finish, kept = jobs[number]["finish"], kept_refs[number]

            def produce(chip, mine):
                at = [
                    half * MEMBERS + slot_of(half, *chips[chip], core if mine else 1 - core)
                    for half in range(2)
                ]
                at = [pl.ds(pl.multiple_of(index * rows, rows), rows) for index in at]
                blocks = [
                    jnp.concatenate([ref[at[0], :], ref[at[1], :]], axis=0) for ref in left_refs
                ]

                @pl.loop(0, planes)
                def _(step):
                    columns = lanes(step, strip)
                    product = matmul(blocks[0], right_refs[0][step])
                    for part, ref in zip(blocks[1:], right_refs[1:]):
                        product = product + matmul(part, ref[step])
                    for half in range(2):
                        piece = product[half * rows : (half + 1) * rows]
                        if mine:
                            sums[chip, half, :, columns] = piece
                        else:
                            core_send[chip, half, :, columns] = piece.astype(bf16)

            core_copies = [
                remote_copy(
                    core_send.at[chip],
                    core_got.at[chip],
                    core_out.at[4 * number + chip],
                    core_in.at[4 * number + chip],
                    to_peer["c"],
                )
                for chip in range(4)
            ]

            axes = [extra[index % 2] for index in range(4)]
            axes += ["x" if extra[half] == "y" else "y" for half in range(2)]
            chip_on = {"x": 1, "y": 2}
            links = [
                remote_copy(
                    link_send.at[index],
                    link_got.at[index],
                    link_out.at[6 * number + index],
                    link_in.at[6 * number + index],
                    to_peer[axes[index]],
                )
                for index in range(6)
            ]

            def send(index):
                half = index % 2
                chip = 0 if index < 2 else chip_on[axes[index]]
                link_send[index] = sums[chip, half].astype(bf16)
                links[index].start()

            def settle(chip):
                core_copies[chip].wait_recv()
                for half in range(2):
                    sums[chip, half] += core_got[chip, half].astype(f32)

            if number > 0:
                for copy in previous:
                    copy.wait_send()
                for index, peer in enumerate(peers):
                    pl.semaphore_signal(
                        ready.at[index], inc=1, device_id=peer, device_id_type=MESH
                    )
            produce(0, False)
            if number > 0:
                pl.semaphore_wait(ready.at[2], 1)
            core_copies[0].start()
            produce(0, True)
            produce(1, False)
            core_copies[1].start()
            settle(0)
            if number > 0:
                pl.semaphore_wait(ready.at[0], 1)
                pl.semaphore_wait(ready.at[1], 1)
            send(0)
            send(1)
            produce(1, True)
            produce(2, False)
            core_copies[2].start()
            settle(1)
            for index in (2, 3):
                if axes[index] == "x":
                    send(index)
            produce(2, True)
            produce(3, False)
            core_copies[3].start()
            settle(2)
            for index in (2, 3):
                if axes[index] == "y":
                    send(index)
            for half in range(2):
                links[half].wait_recv()
                sums[chip_on[axes[4 + half]], half] += link_got[half].astype(f32)
                send(4 + half)
                if half == 0:
                    produce(3, True)
                    settle(3)

            for half in range(2):
                links[2 + half].wait_recv()
                links[4 + half].wait_recv()

                @pl.loop(0, rows // 32)
                def _(step):
                    at = pl.ds(pl.multiple_of(step * 32, 32), 32)
                    total = sums[3, half, at, :] + link_got[2 + half, at, :].astype(f32)
                    total = total + link_got[4 + half, at, :].astype(f32)
                    finish(total, half, at, state_refs, kept, own)

                if jobs[number]["gathers"]:
                    gather.start(half)
                if jobs[number].get("hands"):
                    hands[0].start(half)
            if jobs[number]["gathers"]:
                for half in range(2):
                    gather.turn(half)
                gather.cross()
                gather.end()
            return core_copies + links

        previous = []
        for number in range(count):
            previous = run(number, previous)
        for hand in hands:
            for index in range(2):
                hand.wait_recv(index)
            hand.wait_send()
        for copy in previous:
            copy.wait_send()

    depth = sum(height for job in jobs for _, height, _ in job["rights"])
    results = list(
        pl.pallas_call(
            kernel,
            grid=(1,),
            in_specs=in_specs,
            out_specs=out_specs,
            out_shape=out_shape,
            scratch_shapes=scratch,
            compiler_params=pltpu.CompilerParams(
                collective_id=collective_id,
                has_side_effects=True,
                vmem_limit_bytes=60 * 1024 * 1024,
            ),
            cost_estimate=pl.CostEstimate(
                flops=2 * length * depth * model_width,
                bytes_accessed=200 * 1024 * 1024,
                transcendentals=0,
            ),
            name=name,
        )(*arrays)
    )
    if gathers:
        results[count] = results[count].reshape(length, model_width)
    return results


def closing(grads, own_output, got_tokens):
    bf16, f32 = jnp.bfloat16, jnp.float32
    _, rows, model_width = own_output.shape
    count = len(grads)
    guests = [SquareReturn(grad) for grad in grads]

    def kernel(*refs):
        grad_refs = refs[:count]
        out_ref, tokens_ref = refs[count : count + 2]
        got_refs = refs[count + 2 : 2 * count + 2]
        output, tokens = refs[2 * count + 2 : 2 * count + 4]
        wide, hand_out, hand_in, core_out, core_in, local = refs[2 * count + 4 : 2 * count + 10]
        guest_scratch = refs[2 * count + 10 :]
        core = lax.axis_index("c")
        to_core = {"c": 1 - core}
        at = pl.ds(pl.multiple_of(core * rows, rows), rows)
        hand = HandBack(
            out_ref, lambda index: output.at[index, at], hand_out, hand_in, local.at[2]
        )
        signal_and_wait(square_peers() + [to_core], hand.others)
        for half in range(2):
            hand.start(half)
        for number, guest in enumerate(guests):
            guest.bind(
                grad_refs[number], got_refs[number], *guest_scratch[3 * number : 3 * number + 3]
            )
            guest.begin()
        copies = []
        for index in range(2):
            wide[index] = tokens_ref[index].astype(f32)
            copies += [
                remote_copy(
                    wide.at[index],
                    tokens.at[index, at],
                    core_out.at[index],
                    core_in.at[index],
                    to_core,
                ),
                pltpu.make_async_copy(wide.at[index], tokens.at[index, at], local.at[index]),
            ]
        for copy in copies:
            copy.start()
        for index in range(2):
            place = output.at[index, at]
            hand.wait_recv(index)
            copies.append(
                remote_copy(
                    place, place, core_out.at[2 + index], core_in.at[2 + index], to_core
                )
            )
            copies[-1].start()
        hand.wait_send()
        for copy in copies:
            copy.wait()
        for guest in guests:
            guest.end()

    anywhere = pl.BlockSpec(memory_space=pl.ANY)
    shape = jax.ShapeDtypeStruct
    dma = pltpu.SemaphoreType.DMA
    operands = (*grads, own_output, got_tokens)
    return pl.pallas_call(
        kernel,
        grid=(1,),
        in_specs=[in_spec(array.shape) for array in operands],
        out_specs=[anywhere] * (count + 2),
        out_shape=[guest.shape for guest in guests]
        + [shape((2, 2 * rows, model_width), bf16), shape((2, 2 * rows, model_width), f32)],
        scratch_shapes=[
            pltpu.VMEM((2, rows, model_width), f32),
            dma((2,)),
            dma((2,)),
            dma((4,)),
            dma((4,)),
            dma((3,)),
        ]
        + [sems for guest in guests for sems in guest.scratch],
        compiler_params=pltpu.CompilerParams(
            collective_id=5, has_side_effects=True, vmem_limit_bytes=60 * 1024 * 1024
        ),
        cost_estimate=pl.CostEstimate(flops=0, bytes_accessed=2**27, transcendentals=0),
        name="closing",
    )(*operands)


def attention_forward_kernel(query, key, value, first, attended, heads_out, log_total):
    tile = pl.program_id(1)
    rows = query.shape[0]
    query_tile = query[...]
    first_key = first[...]
    row_index = lax.broadcasted_iota(jnp.int32, (rows, rows), 0)
    column_index = lax.broadcasted_iota(jnp.int32, (rows, rows), 1)

    def block(index, carry, diagonal):
        largest, total, summed = carry
        at = pl.ds(pl.multiple_of(index * rows, rows), rows)
        scores = contract_cols(query_tile, key[at, :])
        visible = column_index + index * rows >= first_key
        if diagonal:
            visible = visible & (column_index <= row_index)
        scores = jnp.where(visible, scores, masked_score)
        new_largest = jnp.maximum(largest, jnp.max(scores, axis=1, keepdims=True))
        weights = jnp.where(visible, jnp.exp(scores - new_largest), 0.0)
        scaling = jnp.exp(largest - new_largest)
        total = total * scaling + jnp.sum(weights, axis=1, keepdims=True)
        summed = summed * scaling + matmul(weights.astype(jnp.bfloat16), value[at, :])
        return (new_largest, total, summed)

    carry = (
        jnp.full((rows, 1), masked_score, jnp.float32),
        jnp.zeros((rows, 1), jnp.float32),
        jnp.zeros((rows, HEAD_DIM), jnp.float32),
    )
    carry = lax.fori_loop(0, tile, lambda index, kept: block(index, kept, False), carry)
    largest, total, summed = block(tile, carry, True)
    summed = summed / total
    attended[...] = summed
    heads_out[...] = summed.astype(jnp.bfloat16)
    log_total[0, :, :] = jnp.broadcast_to(
        jnp.transpose(largest + jnp.log(total)), log_total.shape[1:]
    )


def attention_forward(query, key, value, first_key, tile_rows):
    length, width = query.shape
    heads = width // HEAD_DIM
    whole = pl.BlockSpec((length, HEAD_DIM), lambda head, tile: (0, head))
    part = pl.BlockSpec((tile_rows, HEAD_DIM), lambda head, tile: (tile, head))
    return pl.pallas_call(
        attention_forward_kernel,
        grid=(heads, length // tile_rows),
        in_specs=[
            part,
            whole,
            whole,
            pl.BlockSpec((tile_rows, 1), lambda head, tile: (tile, 0)),
        ],
        out_specs=[
            part,
            part,
            pl.BlockSpec((1, 8, tile_rows), lambda head, tile: (head, 0, tile)),
        ],
        out_shape=[
            jax.ShapeDtypeStruct((length, width), jnp.float32),
            jax.ShapeDtypeStruct((length, width), jnp.bfloat16),
            jax.ShapeDtypeStruct((heads, 8, length), jnp.float32),
        ],
        compiler_params=pltpu.CompilerParams(vmem_limit_bytes=60 * 1024 * 1024),
        cost_estimate=pl.CostEstimate(
            flops=2 * length * length * width,
            bytes_accessed=10 * length * width,
            transcendentals=length * length * heads // 2,
        ),
        name="attention_forward",
    )(query, key, value, first_key)


def project(all_tokens, units, head_width, cosine, sine_table):
    bf16, f32 = jnp.bfloat16, jnp.float32
    length, model_width = all_tokens.shape
    planes, height, strip = units.shape
    rows = 256

    def kernel(tokens, weight, gains, cos, sin, normed, query, key, value):
        values = tokens[...].astype(f32)
        low = (values * rms_scale(values) * gain_row(gains, 0)).astype(bf16)
        normed[...] = low

        def turn(part):
            return part * cos[...] + pltpu.roll(part, HEAD_DIM // 2, 1) * sin[...]

        def projection(start):
            return by_planes(low, weight, start, head_width)

        query_proj = projection(0)
        key_proj = projection(head_width)
        for head in range(head_width // HEAD_DIM):
            at = slice(head * HEAD_DIM, (head + 1) * HEAD_DIM)
            query[:, at] = (turn(query_proj[:, at]) * HEAD_DIM ** (-0.5)).astype(bf16)
            key[:, at] = turn(key_proj[:, at]).astype(bf16)
        value[...] = projection(2 * head_width).astype(bf16)

    def tile(width):
        return pl.BlockSpec((rows, width), lambda step: (step, 0))

    gain_block = height // 16 - 1
    shape = jax.ShapeDtypeStruct
    return pl.pallas_call(
        kernel,
        grid=(length // rows,),
        in_specs=[
            tile(model_width),
            pl.BlockSpec((planes, 3 * head_width, strip), lambda step: (0, 0, 0)),
            pl.BlockSpec((planes, 16, strip), lambda step: (0, gain_block, 0)),
            tile(HEAD_DIM),
            tile(HEAD_DIM),
        ],
        out_specs=[tile(model_width)] + [tile(head_width)] * 3,
        out_shape=[shape((length, model_width), bf16)] + [shape((length, head_width), bf16)] * 3,
        compiler_params=pltpu.CompilerParams(vmem_limit_bytes=60 * 1024 * 1024),
        cost_estimate=pl.CostEstimate(
            flops=6 * length * head_width * model_width,
            bytes_accessed=4 * length * model_width,
            transcendentals=0,
        ),
        name="project",
    )(all_tokens, units, units, cosine, sine_table)


def gain_row(gains, index):
    return jnp.concatenate(
        [gains[plane, index : index + 1, :] for plane in range(gains.shape[0])], axis=1
    ).astype(jnp.float32)


def by_planes(rows, units, start, height):
    strip = units.shape[2]
    total = contract_cols(rows[:, :strip], units[0, start : start + height, :])
    for plane in range(1, units.shape[0]):
        total = total + contract_cols(
            rows[:, plane * strip : (plane + 1) * strip], units[plane, start : start + height, :]
        )
    return total


def hidden_forward(normed_ffn, units, hidden):
    bf16, f32 = jnp.bfloat16, jnp.float32
    length, model_width = normed_ffn.shape
    rows = 256

    def kernel(normed, weights, mixed, gate, up):
        low = normed[...]
        gate_proj = by_planes(low, weights, 0, hidden)
        up_proj = by_planes(low, weights, hidden, hidden)
        gate[...] = gate_proj
        up[...] = up_proj
        mixed[...] = (gate_proj / (1.0 + jnp.exp(-gate_proj)) * up_proj).astype(bf16)

    def tile(width):
        return pl.BlockSpec((rows, width), lambda step: (step, 0))

    shape = jax.ShapeDtypeStruct
    return pl.pallas_call(
        kernel,
        grid=(length // rows,),
        in_specs=[tile(model_width), in_spec(units.shape)],
        out_specs=[tile(hidden)] * 3,
        out_shape=[shape((length, hidden), bf16)] + [shape((length, hidden), f32)] * 2,
        compiler_params=pltpu.CompilerParams(vmem_limit_bytes=60 * 1024 * 1024),
        cost_estimate=pl.CostEstimate(
            flops=4 * length * hidden * model_width,
            bytes_accessed=4 * length * model_width,
            transcendentals=length * hidden,
        ),
        name="hidden_forward",
    )(normed_ffn, units)


def hidden_backward(gate_proj, up_proj, all_cotangent, units, hidden):
    bf16 = jnp.bfloat16
    length, model_width = all_cotangent.shape
    rows = 256

    def kernel(gate_ref, up_ref, cotangent, weights, grad_pair):
        gate, up = gate_ref[...], up_ref[...]
        grad_mixed = by_planes(cotangent[...], weights, 0, hidden)
        sigmoid = 1.0 / (1.0 + jnp.exp(-gate))
        grad_gate = grad_mixed * up * sigmoid * (1.0 + gate * (1.0 - sigmoid))
        grad_up = grad_mixed * gate * sigmoid
        grad_pair[...] = jnp.concatenate([grad_gate, grad_up], axis=1).astype(bf16)

    def tile(width):
        return pl.BlockSpec((rows, width), lambda step: (step, 0))

    shape = jax.ShapeDtypeStruct
    return pl.pallas_call(
        kernel,
        grid=(length // rows,),
        in_specs=[tile(hidden), tile(hidden), tile(model_width), in_spec(units.shape)],
        out_specs=tile(2 * hidden),
        out_shape=shape((length, 2 * hidden), bf16),
        compiler_params=pltpu.CompilerParams(vmem_limit_bytes=60 * 1024 * 1024),
        cost_estimate=pl.CostEstimate(
            flops=2 * length * hidden * model_width,
            bytes_accessed=4 * length * model_width,
            transcendentals=length * hidden,
        ),
        name="hidden_backward",
    )(gate_proj, up_proj, all_cotangent, units)


def attention_backward_kernel(guests, *refs):
    count = len(guests)
    query, key, value, branch, weight, attended, log_total, first, cos, sin = refs[:10]
    grads, key_sum, value_sum = refs[10 + count], refs[11 + 2 * count], refs[12 + 2 * count]
    guest_scratch = refs[13 + 2 * count :]
    for number, guest in enumerate(guests):
        guest.bind(
            refs[10 + number], refs[11 + count + number], *guest_scratch[3 * number : 3 * number + 3]
        )
    turn = pl.program_id(0) * pl.num_programs(1) + pl.program_id(1)

    @pl.when(turn == 0)
    def _():
        signal_and_wait(square_peers())
        for guest in guests:
            guest.begin()

    tile = pl.program_id(1)
    rows = query.shape[0]
    query_tile = query[...]
    grad_tile = by_planes(branch[...], weight, 0, HEAD_DIM).astype(jnp.bfloat16)
    centre_row = jnp.transpose(
        jnp.sum(grad_tile.astype(jnp.float32) * attended[...], axis=1, keepdims=True)
    )
    log_row = log_total[0, :1, :]
    first_row = first[:1, :]
    key_index = lax.broadcasted_iota(jnp.int32, (rows, rows), 0)
    query_index = lax.broadcasted_iota(jnp.int32, (rows, rows), 1)

    def block(index, summed, diagonal):
        at = pl.ds(pl.multiple_of(index * rows, rows), rows)
        key_block = key[at, :]
        scores = contract_cols(key_block, query_tile)
        visible = key_index + index * rows >= first_row
        if diagonal:
            visible = visible & (key_index <= query_index)
        probability = jnp.where(visible, jnp.exp(scores - log_row), 0.0)
        grad_prob = contract_cols(value[at, :], grad_tile)
        grad_scores = (probability * (grad_prob - centre_row)).astype(jnp.bfloat16)
        key_part = matmul(grad_scores, query_tile)
        value_part = matmul(probability.astype(jnp.bfloat16), grad_tile)
        if diagonal:
            key_sum[at, :] = key_part
            value_sum[at, :] = value_part
        else:
            key_sum[at, :] += key_part
            value_sum[at, :] += value_part
        return summed + contract_rows(grad_scores, key_block)

    def turn_back(part, at):
        return part * cos[at, :] - pltpu.roll(part, HEAD_DIM // 2, 1) * sin[at, :]

    summed = lax.fori_loop(
        0,
        tile,
        lambda index, kept: block(index, kept, False),
        jnp.zeros((rows, HEAD_DIM), jnp.float32),
    )
    summed = block(tile, summed, True)
    here = pl.ds(pl.multiple_of(tile * rows, rows), rows)
    grads[0, here, :] = (turn_back(summed, here) * HEAD_DIM ** (-0.5)).astype(jnp.bfloat16)

    @pl.when(tile == pl.num_programs(1) - 1)
    def _():
        @pl.loop(0, pl.num_programs(1))
        def _(index):
            at = pl.ds(pl.multiple_of(index * rows, rows), rows)
            grads[1, at, :] = turn_back(key_sum[at, :], at).astype(jnp.bfloat16)
            grads[2, at, :] = value_sum[at, :].astype(jnp.bfloat16)

    @pl.when(turn == pl.num_programs(0) * pl.num_programs(1) - 1)
    def _():
        for guest in guests:
            guest.end()


def attention_backward(
    query,
    key,
    value,
    grad_branch,
    units,
    attended,
    log_total,
    first_key,
    cosine,
    sine_table,
    tile_rows,
    summed,
):
    guests = [SquareReturn(grad) for grad in summed]
    length, width = query.shape
    model_width = grad_branch.shape[1]
    heads = width // HEAD_DIM
    whole = pl.BlockSpec((length, HEAD_DIM), lambda head, tile: (0, head))
    part = pl.BlockSpec((tile_rows, HEAD_DIM), lambda head, tile: (tile, head))
    table = pl.BlockSpec((length, HEAD_DIM), lambda head, tile: (0, 0))
    shape = jax.ShapeDtypeStruct((3, length, width), jnp.bfloat16)
    all_three = pl.BlockSpec((3, length, HEAD_DIM), lambda head, tile: (0, 0, head))
    return pl.pallas_call(
        functools.partial(attention_backward_kernel, guests),
        grid=(heads, length // tile_rows),
        in_specs=[
            part,
            whole,
            whole,
            pl.BlockSpec((tile_rows, model_width), lambda head, tile: (tile, 0)),
            pl.BlockSpec(
                (units.shape[0], HEAD_DIM, units.shape[2]),
                lambda head, tile: (0, 3 * heads + head, 0),
            ),
            part,
            pl.BlockSpec((1, 8, tile_rows), lambda head, tile: (head, 0, tile)),
            pl.BlockSpec((8, tile_rows), lambda head, tile: (0, tile)),
            table,
            table,
        ]
        + [in_spec(grad.shape) for grad in summed],
        out_specs=[all_three] + [pl.BlockSpec(memory_space=pl.ANY)] * len(guests),
        out_shape=[shape] + [guest.shape for guest in guests],
        scratch_shapes=[
            pltpu.VMEM((length, HEAD_DIM), jnp.float32),
            pltpu.VMEM((length, HEAD_DIM), jnp.float32),
        ]
        + [sems for guest in guests for sems in guest.scratch],
        compiler_params=pltpu.CompilerParams(
            collective_id=6, has_side_effects=True, vmem_limit_bytes=60 * 1024 * 1024
        ),
        cost_estimate=pl.CostEstimate(
            flops=5 * length * length * width + 2 * length * width * model_width,
            bytes_accessed=24 * length * width,
            transcendentals=length * length * heads // 2,
        ),
        name="attention_backward",
    )(
        query,
        key,
        value,
        grad_branch,
        units,
        attended,
        log_total,
        first_key,
        cosine,
        sine_table,
        *summed,
    )


def group_device(
    tokens,
    doc_starts,
    query_weight,
    key_weight,
    value_weight,
    out_weight,
    gate_weight,
    up_weight,
    down_weight,
    attention_gain,
    feedforward_gain,
    cotangent,
):
    bf16, f32 = jnp.bfloat16, jnp.float32
    x_at, z_at, core = (lax.axis_index(name) for name in ("x", "z", "c"))
    _, shard_rows, model_width = tokens.shape
    slice_width = query_weight.shape[0]
    half_rows = shard_rows // 2
    length = 2 * MEMBERS * half_rows
    planes = lax.axis_size("z")
    strip = model_width // planes
    head_width = query_weight.shape[1] // QUARTERS
    hidden = gate_weight.shape[1] // QUARTERS

    def keep_naturally(kept, half, at, values):
        part = strip // 2
        for x in range(2):
            for plane in range(planes):
                start = plane * strip + x * part
                place = x * planes * part + plane * part
                kept[half, at, place : place + part] = values[:, start : start + part]

    def units_of(weight):
        return weight.reshape(QUARTERS, -1, slice_width)

    def far_sum(grads):
        return lax.psum_scatter(grads.astype(bf16), "z", scatter_dimension=1, tiled=True)

    gains = jnp.concatenate(
        [attention_gain[None], feedforward_gain[None], jnp.zeros((14, slice_width), bf16)]
    )
    gains = jnp.broadcast_to(gains[None], (QUARTERS, 16, slice_width))
    docs = jnp.zeros((8, 128), jnp.int32).at[:2, : doc_starts.shape[1]].set(doc_starts)
    own_tokens, own_cotangent, other_docs, attention_square, pair_square, down_square = deal(
        tokens,
        cotangent,
        [
            jnp.concatenate(
                [
                    units_of(query_weight.T),
                    units_of(key_weight.T),
                    units_of(value_weight.T),
                    units_of(out_weight),
                    gains,
                ],
                axis=1,
            ),
            jnp.concatenate([units_of(gate_weight.T), units_of(up_weight.T)], axis=1),
            units_of(down_weight),
        ],
        docs,
    )
    attention_units = lax.all_gather(attention_square, "z")
    all_tokens, all_cotangent = gather_rows(own_tokens, own_cotangent)
    pair_square, _ = lax.optimization_barrier((pair_square, all_tokens))
    pair_units = lax.all_gather(pair_square, "z")

    positions = jnp.arange(length, dtype=jnp.int32)
    cosine, sine_table = turning_tables(length)
    docs = jnp.where(plane_x(z_at) == x_at, docs, other_docs)
    starts = lax.dynamic_index_in_dim(docs, z_at // 2, 0, keepdims=False)[: doc_starts.shape[1]]
    first_key = jnp.max(
        jnp.where(starts[None, :] <= positions[:, None], starts[None, :], 0), axis=1
    )
    normed, query_rot, key_rot, value_low = project(
        all_tokens, attention_units, head_width, cosine, sine_table
    )
    down_square, _ = lax.optimization_barrier((down_square, query_rot))
    down_units = lax.all_gather(down_square, "z")
    tile_rows = min(512, length)
    attended, heads_out, log_total = attention_forward(
        query_rot, key_rot, value_low, first_key[:, None], tile_rows
    )
    gains_at = (attention_units, 16, attention_units.shape[1] // 16 - 1)

    def after_attention(total, half, at, states, kept, own):
        token_ref, gain_ref = states
        residual = token_ref[half, at, :].astype(f32) + total
        kept[half, at, :] = residual
        own[half, at, :] = (residual * rms_scale(residual) * gain_row(gain_ref, 1)).astype(bf16)

    residual, normed_ffn = exchange(
        "branch_exchange",
        2,
        [
            dict(
                lefts=[heads_out],
                rights=[(attention_units, head_width, 3)],
                states=[(own_tokens, None, 0), gains_at],
                finish=after_attention,
                kept=f32,
                gathers=True,
            )
        ],
        ("x", "y"),
    )
    mixed_hidden, gate_proj, up_proj = hidden_forward(normed_ffn, pair_units, hidden)
    grad_down_all = contract_rows(mixed_hidden, all_cotangent)
    grad_pair_low = hidden_backward(
        gate_proj, up_proj, all_cotangent, down_units, hidden
    )
    grad_down = far_sum(grad_down_all)
    grad_pair_all = contract_rows(grad_pair_low, normed_ffn).astype(bf16)
    grad_pair_low, grad_pair_all = lax.optimization_barrier((grad_pair_low, grad_pair_all))
    grad_pair = far_sum(grad_pair_all)

    def after_feedforward(total, half, at, states, kept, own):
        residual_ref, cotangent_ref, gain_ref = states
        rows = residual_ref[half, at, :]
        scale = rms_scale(rows)
        weighted = total * gain_row(gain_ref, 1)
        mean = jnp.mean(weighted * rows, axis=-1, keepdims=True)
        grad = cotangent_ref[half, at, :].astype(f32) + scale * weighted - rows * scale**3 * mean
        kept[half, at, :] = grad
        own[half, at, :] = grad.astype(bf16)

    grad_residual, grad_branch = exchange(
        "feedforward_exchange",
        3,
        [
            dict(
                lefts=[grad_pair_low],
                rights=[(pair_units, 2 * hidden, 0)],
                states=[(residual, None, 0), (own_cotangent, None, 0), gains_at],
                finish=after_feedforward,
                kept=f32,
                gathers=True,
            )
        ],
        ("x", "y"),
    )
    grad_out = contract_rows(heads_out, grad_branch).astype(bf16)
    grad_qkv, spread_down = attention_backward(
        query_rot,
        key_rot,
        value_low,
        grad_branch,
        attention_units,
        attended,
        log_total,
        jnp.broadcast_to(first_key[None], (8, length)),
        cosine,
        sine_table,
        tile_rows,
        [grad_down],
    )
    grad_projections = lax.dot_general(
        grad_qkv, normed, (((1,), (0,)), ((), ())), preferred_element_type=f32
    ).reshape(3 * head_width, model_width)
    grad_attention = jnp.concatenate([grad_projections.astype(bf16), grad_out])
    grad_attention, grad_pair = lax.optimization_barrier((grad_attention, grad_pair))
    grad_attention = far_sum(grad_attention)

    def after_hidden(total, half, at, states, kept, own):
        keep_naturally(kept, half, at, (states[0][half, at, :] + total).astype(bf16))

    def after_all(total, half, at, states, kept, own):
        token_ref, grad_ref, gain_ref = states
        rows = token_ref[half, at, :].astype(f32)
        scale = rms_scale(rows)
        weighted = total * gain_row(gain_ref, 0)
        mean = jnp.mean(weighted * rows, axis=-1, keepdims=True)
        grad = grad_ref[half, at, :] + scale * weighted - rows * scale**3 * mean
        keep_naturally(kept, half, at, grad.astype(bf16))

    _, own_output, got_tokens = exchange(
        "token_exchange",
        4,
        [
            dict(
                lefts=[(grad_qkv, at) for at in range(3)],
                rights=[(attention_units, head_width, at) for at in range(3)],
                states=[(own_tokens, None, 0), (grad_residual, None, 0), gains_at],
                finish=after_all,
                kept=bf16,
                gathers=False,
                hands=True,
            ),
            dict(
                lefts=[mixed_hidden],
                rights=[(down_units, hidden, 0)],
                states=[(residual, None, 0)],
                finish=after_hidden,
                kept=bf16,
                gathers=False,
            ),
        ],
        ("x", "y"),
    )
    spread_pair, spread_attention, output, grad_tokens = closing(
        [grad_pair, grad_attention], own_output, got_tokens
    )

    def columns(grads):
        return grads.reshape(-1, slice_width).astype(f32)

    grad_down_w, grad_gate_w, grad_up_w = (
        columns(grads)
        for grads in (spread_down, spread_pair[:, :hidden], spread_pair[:, hidden:])
    )
    grad_gate_w, grad_up_w = grad_gate_w.T, grad_up_w.T
    grad_query_w, grad_key_w, grad_value_w, grad_out_w = (
        columns(spread_attention[:, at * head_width : (at + 1) * head_width]) for at in range(4)
    )
    grad_query_w, grad_key_w, grad_value_w = grad_query_w.T, grad_key_w.T, grad_value_w.T

    def gain_sum(*pairs):
        return sum(jnp.sum(weight.astype(f32) * grad, axis=1) for weight, grad in pairs)

    sums = jnp.stack(
        [
            gain_sum(
                (query_weight, grad_query_w), (key_weight, grad_key_w), (value_weight, grad_value_w)
            ),
            gain_sum((gate_weight, grad_gate_w), (up_weight, grad_up_w)),
        ]
    )
    sums = sums + swap(sums, "c")
    return (
        output,
        grad_tokens,
        grad_query_w,
        grad_key_w,
        grad_value_w,
        grad_out_w,
        grad_gate_w,
        grad_up_w,
        grad_down_w,
        sums[0] / attention_gain.astype(f32),
        sums[1] / feedforward_gain.astype(f32),
    )


def placements(stream, seq, head):
    both = (stream + seq) if isinstance(stream, tuple) else (stream, seq)
    in_specs = (
        P(stream, seq, None),
        P(stream, None),
        P(both, head),
        P(both, head),
        P(both, head),
        P(head, both),
        P(both, head),
        P(both, head),
        P(head, both),
        P(both),
        P(both),
        P(stream, seq, None),
    )
    out_specs = (
        P(stream, seq, None),
        P(stream, seq, None),
        P(both, head),
        P(both, head),
        P(both, head),
        P(head, both),
        P(both, head),
        P(both, head),
        P(head, both),
        P(both),
        P(both),
    )
    return in_specs, out_specs


def solution(mesh):
    def run(*arguments):
        tokens, doc_starts = arguments[:2]
        sizes = dict(mesh.shape)
        grouped = (
            (sizes["stream"], sizes["seq"], sizes["head"]) == (2, 8, 2)
            and tokens.shape[0] == 4
            and tokens.shape[1] <= WIN
        )
        if grouped:
            split = Mesh(mesh.devices.reshape(2, 4, 2, 2), ("x", "z", "y", "c"))
            in_specs, out_specs = placements(("x",), ("z", "y"), "c")
            step = group_device
        else:
            split = mesh
            in_specs, out_specs = placements("stream", "seq", "head")
            step = per_device
        return jax.shard_map(
            step, mesh=split, in_specs=in_specs, out_specs=out_specs, check_vma=False
        )(*arguments)

    return run
```

```python
import functools
import math

import jax
import jax.numpy as jnp
import numpy as np
from jax import lax
from jax.experimental import pallas as pl
from jax.experimental.pallas import tpu as pltpu
from jax.sharding import Mesh
from jax.sharding import PartitionSpec as P

HEAD_DIM = 128
WIN = 2048


epsilon = 1e-06
masked_score = -1e30


def from_behind(value, axis, steps):
    count = lax.axis_size(axis)
    initial, last = (max(0, -steps), min(count, count - steps))
    return lax.ppermute(value, axis, [(source, source + steps) for source in range(initial, last)])


def matmul(left, right):
    return jnp.dot(left, right, preferred_element_type=jnp.float32)


def contract_rows(left, right):
    return lax.dot_general(
        left, right, (((0,), (0,)), ((), ())), preferred_element_type=jnp.float32
    )


def contract_cols(left, right):
    return lax.dot_general(
        left, right, (((1,), (1,)), ((), ())), preferred_element_type=jnp.float32
    )


def rotary_tables(positions):
    half_dim = HEAD_DIM // 2
    frequency = jnp.exp(
        jnp.arange(half_dim).astype(jnp.float32) * (-2.0 * math.log(10000.0) / HEAD_DIM)
    )
    angles = positions.astype(jnp.float32)[:, None] * frequency[None, :]
    return (jnp.cos(angles), jnp.sin(angles))


def rotate_pairs(values, cosine, sine_table):
    half_dim = values.shape[-1] // 2
    first_half = values[..., :half_dim]
    second_half = values[..., half_dim:]
    return jnp.concatenate(
        [
            first_half * cosine - second_half * sine_table,
            second_half * cosine + first_half * sine_table,
        ],
        axis=-1,
    )


def unrotate_pairs(values, cosine, sine_table):
    half_dim = values.shape[-1] // 2
    first_half = values[..., :half_dim]
    second_half = values[..., half_dim:]
    return jnp.concatenate(
        [
            first_half * cosine + second_half * sine_table,
            second_half * cosine - first_half * sine_table,
        ],
        axis=-1,
    )


def document_number(starts, positions):
    return jnp.sum((starts[:, None, :] <= positions[None, :, None]).astype(jnp.int32), axis=2)


def rms_scale(values):
    return lax.rsqrt(jnp.mean(values * values, axis=-1, keepdims=True) + epsilon)


def norm_backward(grad_normed, inputs, row_scale, gain_vector):
    gain_grad = jnp.sum(grad_normed * inputs * row_scale, axis=0)
    weighted = grad_normed * gain_vector
    grad_inputs = row_scale * weighted - inputs * row_scale**3 * jnp.mean(
        weighted * inputs, axis=-1, keepdims=True
    )
    return (grad_inputs, gain_grad)


def per_device(
    tokens,
    doc_starts,
    query_weight,
    key_weight,
    value_weight,
    out_weight,
    gate_weight,
    up_weight,
    down_weight,
    attention_gain,
    feedforward_gain,
    cotangent,
):
    gathered = (
        lax.all_gather(query_weight, ("stream", "seq"), axis=0, tiled=True),
        lax.all_gather(key_weight, ("stream", "seq"), axis=0, tiled=True),
        lax.all_gather(value_weight, ("stream", "seq"), axis=0, tiled=True),
        lax.all_gather(out_weight, ("stream", "seq"), axis=1, tiled=True),
        lax.all_gather(gate_weight, ("stream", "seq"), axis=0, tiled=True),
        lax.all_gather(up_weight, ("stream", "seq"), axis=0, tiled=True),
        lax.all_gather(down_weight, ("stream", "seq"), axis=1, tiled=True),
        lax.all_gather(attention_gain, ("stream", "seq"), axis=0, tiled=True),
        lax.all_gather(feedforward_gain, ("stream", "seq"), axis=0, tiled=True),
    )
    (
        full_query,
        full_key,
        full_value,
        full_out,
        full_gate,
        full_up,
        full_down,
        full_gain_first,
        full_gain_second,
    ) = gathered
    streams, shard_rows, model_width = tokens.shape
    head_width = full_query.shape[1]
    local_heads = head_width // HEAD_DIM
    flat_rows = streams * shard_rows
    seq_index = lax.axis_index("seq")
    halo_shards = min(WIN // shard_rows, lax.axis_size("seq") - 1)
    window_rows = (halo_shards + 1) * shard_rows
    inputs = tokens.reshape(flat_rows, model_width).astype(jnp.float32)
    scale_first = rms_scale(inputs)
    gain_first = full_gain_first.astype(jnp.float32)
    normed = (inputs * scale_first * gain_first).astype(jnp.bfloat16)
    query_proj = matmul(normed, full_query).reshape(streams, shard_rows, local_heads, HEAD_DIM)
    key_proj = matmul(normed, full_key).reshape(streams, shard_rows, local_heads, HEAD_DIM)
    value_low = (
        matmul(normed, full_value).astype(jnp.bfloat16).reshape(streams, shard_rows, head_width)
    )
    positions = seq_index * shard_rows + jnp.arange(shard_rows, dtype=jnp.int32)
    cosine, sine_table = rotary_tables(positions)
    cosine = cosine[None, :, None, :]
    sine_table = sine_table[None, :, None, :]
    query_rot = (rotate_pairs(query_proj, cosine, sine_table) * HEAD_DIM ** (-0.5)).astype(
        jnp.bfloat16
    )
    key_rot = rotate_pairs(key_proj, cosine, sine_table).astype(jnp.bfloat16)
    paired = jnp.stack([key_rot.reshape(streams, shard_rows, head_width), value_low])
    pieces = []
    for distance in range(halo_shards, 0, -1):
        pieces.append(from_behind(paired, "seq", distance))
    window = jnp.concatenate(pieces + [paired], axis=2)
    key_positions = (seq_index - halo_shards) * shard_rows + jnp.arange(
        window_rows, dtype=jnp.int32
    )
    query_docs = document_number(doc_starts, positions)
    key_docs = document_number(doc_starts, key_positions)
    offsets = positions[:, None] - key_positions[None, :]
    allowed = ((offsets >= 0) & (offsets < WIN))[None] & (
        query_docs[:, :, None] == key_docs[:, None, :]
    )
    query_heads = jnp.transpose(query_rot, (2, 0, 1, 3))
    key_heads = jnp.transpose(
        window[0].reshape(streams, window_rows, local_heads, HEAD_DIM), (2, 0, 1, 3)
    )
    value_heads = jnp.transpose(
        window[1].reshape(streams, window_rows, local_heads, HEAD_DIM), (2, 0, 1, 3)
    )

    def head_forward(operands):
        query_one, key_one, value_one = operands
        scores = jnp.einsum("sqe,ske->sqk", query_one, key_one, preferred_element_type=jnp.float32)
        scores = jnp.where(allowed, scores, masked_score)
        largest = jnp.max(scores, axis=-1, keepdims=True)
        weights = jnp.exp(scores - largest)
        totals = jnp.sum(weights, axis=-1, keepdims=True)
        probability = (weights / totals).astype(jnp.bfloat16)
        attended = jnp.einsum(
            "sqk,ske->sqe", probability, value_one, preferred_element_type=jnp.float32
        )
        return (attended, (largest + jnp.log(totals))[..., 0])

    attended, log_totals = lax.map(head_forward, (query_heads, key_heads, value_heads))
    heads_out = (
        jnp.transpose(attended, (1, 2, 0, 3)).reshape(flat_rows, head_width).astype(jnp.bfloat16)
    )
    attention_sum = lax.psum(matmul(heads_out, full_out), "head")
    residual = inputs + attention_sum
    scale_second = rms_scale(residual)
    gain_second = full_gain_second.astype(jnp.float32)
    normed_ffn = (residual * scale_second * gain_second).astype(jnp.bfloat16)
    gate_proj = matmul(normed_ffn, full_gate)
    up_proj = matmul(normed_ffn, full_up)
    sigmoid_gate = jax.nn.sigmoid(gate_proj)
    silu_gate = gate_proj * sigmoid_gate
    mixed_hidden = (silu_gate * up_proj).astype(jnp.bfloat16)
    feedforward_sum = lax.psum(matmul(mixed_hidden, full_down).astype(jnp.bfloat16), "head").astype(
        jnp.float32
    )
    output = (
        (residual + feedforward_sum).astype(jnp.bfloat16).reshape(streams, shard_rows, model_width)
    )
    gathered = (
        lax.all_gather(query_weight, ("stream", "seq"), axis=0, tiled=True),
        lax.all_gather(key_weight, ("stream", "seq"), axis=0, tiled=True),
        lax.all_gather(value_weight, ("stream", "seq"), axis=0, tiled=True),
        lax.all_gather(out_weight, ("stream", "seq"), axis=1, tiled=True),
        lax.all_gather(gate_weight, ("stream", "seq"), axis=0, tiled=True),
        lax.all_gather(up_weight, ("stream", "seq"), axis=0, tiled=True),
        lax.all_gather(down_weight, ("stream", "seq"), axis=1, tiled=True),
        lax.all_gather(attention_gain, ("stream", "seq"), axis=0, tiled=True),
        lax.all_gather(feedforward_gain, ("stream", "seq"), axis=0, tiled=True),
    )
    (
        full_query,
        full_key,
        full_value,
        full_out,
        full_gate,
        full_up,
        full_down,
        full_gain_first,
        full_gain_second,
    ) = gathered
    grad_output = cotangent.reshape(flat_rows, model_width)
    grad_down = contract_rows(mixed_hidden, grad_output)
    grad_mixed = contract_cols(grad_output, full_down)
    grad_gate_low = (
        grad_mixed * up_proj * sigmoid_gate * (1.0 + gate_proj * (1.0 - sigmoid_gate))
    ).astype(jnp.bfloat16)
    grad_up_low = (grad_mixed * silu_gate).astype(jnp.bfloat16)
    grad_gate_w = contract_rows(normed_ffn, grad_gate_low)
    grad_up_w = contract_rows(normed_ffn, grad_up_low)
    grad_normed_ffn = lax.psum(
        contract_cols(grad_gate_low, full_gate) + contract_cols(grad_up_low, full_up), "head"
    )
    grad_residual_norm, grad_gain_second = norm_backward(
        grad_normed_ffn, residual, scale_second, gain_second
    )
    grad_residual = grad_output.astype(jnp.float32) + grad_residual_norm
    grad_branch = grad_residual.astype(jnp.bfloat16)
    grad_out_w = contract_rows(heads_out, grad_branch)
    grad_heads = contract_cols(grad_branch, full_out).astype(jnp.bfloat16)
    grad_heads_major = jnp.transpose(
        grad_heads.reshape(streams, shard_rows, local_heads, HEAD_DIM), (2, 0, 1, 3)
    )

    def head_backward(operands):
        query_one, key_one, value_one, grad_one, log_one = operands
        scores = jnp.einsum("sqe,ske->sqk", query_one, key_one, preferred_element_type=jnp.float32)
        scores = jnp.where(allowed, scores, masked_score)
        probability = jnp.exp(scores - log_one[..., None])
        grad_prob = jnp.einsum(
            "sqe,ske->sqk", grad_one, value_one, preferred_element_type=jnp.float32
        )
        centre = jnp.sum(probability * grad_prob, axis=-1, keepdims=True)
        grad_scores = (probability * (grad_prob - centre)).astype(jnp.bfloat16)
        grad_query_one = jnp.einsum(
            "sqk,ske->sqe", grad_scores, key_one, preferred_element_type=jnp.float32
        )
        grad_key_one = jnp.einsum(
            "sqk,sqe->ske", grad_scores, query_one, preferred_element_type=jnp.float32
        )
        grad_value_one = jnp.einsum(
            "sqk,sqe->ske",
            probability.astype(jnp.bfloat16),
            grad_one,
            preferred_element_type=jnp.float32,
        )
        return (grad_query_one, grad_key_one, grad_value_one)

    grad_query_heads, grad_key_heads, grad_value_heads = lax.map(
        head_backward, (query_heads, key_heads, value_heads, grad_heads_major, log_totals)
    )
    grad_window = jnp.transpose(
        jnp.stack([grad_key_heads, grad_value_heads]), (0, 2, 3, 1, 4)
    ).reshape(2, streams, window_rows, head_width)
    grad_paired = grad_window[:, :, halo_shards * shard_rows :]
    for distance in range(halo_shards, 0, -1):
        index_piece = halo_shards - distance
        grad_paired = grad_paired + from_behind(
            grad_window[:, :, index_piece * shard_rows : (index_piece + 1) * shard_rows],
            "seq",
            -distance,
        )
    grad_key_rot = grad_paired[0].reshape(streams, shard_rows, local_heads, HEAD_DIM)
    grad_query_rot = jnp.transpose(grad_query_heads, (1, 2, 0, 3))
    grad_query_low = (
        (unrotate_pairs(grad_query_rot, cosine, sine_table) * HEAD_DIM ** (-0.5))
        .reshape(flat_rows, head_width)
        .astype(jnp.bfloat16)
    )
    grad_key_low = (
        unrotate_pairs(grad_key_rot, cosine, sine_table)
        .reshape(flat_rows, head_width)
        .astype(jnp.bfloat16)
    )
    grad_value_low = grad_paired[1].reshape(flat_rows, head_width).astype(jnp.bfloat16)
    grad_query_w = contract_rows(normed, grad_query_low)
    grad_key_w = contract_rows(normed, grad_key_low)
    grad_value_w = contract_rows(normed, grad_value_low)
    grad_normed = lax.psum(
        contract_cols(grad_query_low, full_query)
        + contract_cols(grad_key_low, full_key)
        + contract_cols(grad_value_low, full_value),
        "head",
    )
    grad_inputs_norm, grad_gain_first = norm_backward(grad_normed, inputs, scale_first, gain_first)
    grad_tokens = (grad_residual + grad_inputs_norm).reshape(streams, shard_rows, model_width)
    reduced = (
        lax.psum_scatter(grad_query_w, ("stream", "seq"), scatter_dimension=0, tiled=True),
        lax.psum_scatter(grad_key_w, ("stream", "seq"), scatter_dimension=0, tiled=True),
        lax.psum_scatter(grad_value_w, ("stream", "seq"), scatter_dimension=0, tiled=True),
        lax.psum_scatter(grad_out_w, ("stream", "seq"), scatter_dimension=1, tiled=True),
        lax.psum_scatter(grad_gate_w, ("stream", "seq"), scatter_dimension=0, tiled=True),
        lax.psum_scatter(grad_up_w, ("stream", "seq"), scatter_dimension=0, tiled=True),
        lax.psum_scatter(grad_down, ("stream", "seq"), scatter_dimension=1, tiled=True),
        lax.psum_scatter(grad_gain_first, ("stream", "seq"), scatter_dimension=0, tiled=True),
        lax.psum_scatter(grad_gain_second, ("stream", "seq"), scatter_dimension=0, tiled=True),
    )
    return (
        output,
        grad_tokens,
        reduced[0],
        reduced[1],
        reduced[2],
        reduced[3],
        reduced[4],
        reduced[5],
        reduced[6],
        reduced[7],
        reduced[8],
    )


GROUP = ("x", "y", "c")
MEMBERS = 8
QUARTERS = 4
MESH = pl.DeviceIdType.MESH


def turning_tables(length):
    half_dim = HEAD_DIM // 2
    frequency = np.exp(
        np.arange(half_dim).astype(np.float32) * np.float32(-2.0 * math.log(10000.0) / HEAD_DIM)
    )
    angles = np.arange(length).astype(np.float32)[:, None] * frequency[None, :]
    cosine, sine = np.cos(angles), np.sin(angles)
    return (
        jnp.asarray(np.concatenate([cosine, cosine], axis=1)),
        jnp.asarray(np.concatenate([-sine, sine], axis=1)),
    )


def swap(value, axis):
    return lax.ppermute(value, axis, [(0, 1), (1, 0)])


def remote_copy(source, target, sent, landed, peer):
    return pltpu.make_async_remote_copy(
        source, target, sent, landed, device_id=peer, device_id_type=MESH
    )


def lanes(index, size):
    return pl.ds(pl.multiple_of(index * size, size), size)


def plane_x(plane):
    return (plane + plane // 2) % 2


def plane_of(x, index):
    return x * (1 + index) + (1 - x) * 3 * index


def keeper_x(plane, core):
    return (1 - plane_x(plane) + core) % 2


def source_plane(half, x, core):
    side = (x + core) % 2
    return 2 * half + (side if half else 1 - side)


def slot_of(half, x, y, core):
    side = (x + core) % 2
    return 4 * (side if half else 1 - side) + 2 * y + core


def square_peers():
    x, y = lax.axis_index("x"), lax.axis_index("y")
    return [{"y": 1 - y}, {"x": 1 - x}, {"x": 1 - x, "y": 1 - y}]


def signal_and_wait(peers, others=()):
    barrier = pltpu.get_barrier_semaphore()
    number = len(peers)
    for peer in peers:
        pl.semaphore_signal(barrier, inc=1, device_id=peer, device_id_type=MESH)
    for peer, own in others:
        number = number + jnp.where(own, 0, 1)

        @pl.when(jnp.logical_not(own))
        def _(peer=peer):
            pl.semaphore_signal(barrier, inc=1, device_id=peer, device_id_type=MESH)

    pl.semaphore_wait(barrier, number)


class HandBack:
    def __init__(self, kept, got, out_sems, in_sems, local):
        x, z, core = (lax.axis_index(axis) for axis in ("x", "z", "c"))
        self.stays = (core == 1) & (plane_x(z) == x)
        self.home = z // 2
        targets = [{"x": plane_x(z), "z": source_plane(half, x, core)} for half in range(2)]
        senders = [{"x": keeper_x(z, core), "z": plane_of(x, index)} for index in range(2)]
        self.others = [
            (peer, self.stays & (self.home == number))
            for group in (targets, senders)
            for number, peer in enumerate(group)
        ]
        self.kept, self.got, self.sems = kept, got, (out_sems, in_sems)
        self.targets, self.senders, self.local = targets, senders, local

    def here(self, half):
        return pltpu.make_async_copy(self.kept.at[half], self.got(self.home), self.local)

    def away(self, half):
        out_sems, in_sems = self.sems
        return remote_copy(
            self.kept.at[half],
            self.got(self.home),
            out_sems.at[half],
            in_sems.at[self.home],
            self.targets[half],
        )

    def start(self, half):
        own = self.stays & (self.home == half)

        @pl.when(own)
        def _():
            self.here(half).start()

        @pl.when(jnp.logical_not(own))
        def _():
            self.away(half).start()

    def wait_recv(self, index):
        own = self.stays & (self.home == index)
        out_sems, in_sems = self.sems
        place = self.got(index)

        @pl.when(own)
        def _():
            self.here(index).wait()

        @pl.when(jnp.logical_not(own))
        def _():
            remote_copy(
                place, place, out_sems.at[index], in_sems.at[index], self.senders[index]
            ).wait_recv()

    def wait_send(self):
        for half in range(2):
            own = self.stays & (self.home == half)

            @pl.when(jnp.logical_not(own))
            def _(half=half):
                self.away(half).wait_send()


def in_spec(shape):
    return pl.BlockSpec(shape, lambda *step: (0,) * len(shape), pipeline_mode=pl.Buffered(1))


class SquareSpread:
    def __init__(self, parts):
        _, self.height, self.width = parts.shape
        dma = pltpu.SemaphoreType.DMA
        self.shape = jax.ShapeDtypeStruct((self.height, QUARTERS * self.width), parts.dtype)
        self.scratch = [dma((3,)), dma((3,)), dma(())]

    def bind(self, parts, square, sent, landed, local):
        x, y = lax.axis_index("x"), lax.axis_index("y")
        chip = 2 * x + y
        place = square.at[:, lanes(chip, self.width)]
        others = (chip + 1 - 2 * y, chip + 2 - 4 * x, 3 - chip)
        self.copies = [
            remote_copy(parts.at[other], place, sent.at[index], landed.at[index], peer)
            for index, (peer, other) in enumerate(zip(square_peers(), others))
        ]
        self.copies.append(pltpu.make_async_copy(parts.at[chip], place, local))

    def begin(self):
        for copy in self.copies:
            copy.start()

    def end(self):
        for copy in self.copies:
            copy.wait()


class SquareReturn:
    def __init__(self, grads):
        self.height, width = grads.shape
        self.width = width // QUARTERS
        dma = pltpu.SemaphoreType.DMA
        self.shape = jax.ShapeDtypeStruct((QUARTERS, self.height, self.width), grads.dtype)
        self.scratch = [dma((3,)), dma((3,)), dma(())]

    def bind(self, grads, got, sent, landed, local):
        x, y = lax.axis_index("x"), lax.axis_index("y")
        chip = 2 * x + y
        others = (chip + 1 - 2 * y, chip + 2 - 4 * x, 3 - chip)
        self.copies = [
            remote_copy(
                grads.at[:, lanes(other, self.width)],
                got.at[chip],
                sent.at[index],
                landed.at[index],
                peer,
            )
            for index, (peer, other) in enumerate(zip(square_peers(), others))
        ]
        here = grads.at[:, lanes(chip, self.width)]
        self.copies.append(pltpu.make_async_copy(here, got.at[chip], local))

    def begin(self):
        for copy in self.copies:
            copy.start()

    def end(self):
        for copy in self.copies:
            copy.wait()


class GroupGather:
    scratch_sizes = (14, 14, 2)

    def __init__(self, own, full, sent, landed, local, to_peer, extra):
        x, y, core = (lax.axis_index(axis) for axis in GROUP)
        self.extra = extra
        self.other = ["x" if axis == "y" else "y" for axis in extra]

        def copy(index, source, half, slot, axis):
            return remote_copy(
                source, full.at[half, slot], sent.at[index], landed.at[index], to_peer[axis]
            )

        def place(half, axis):
            return slot_of(half, 1 - x if axis in ("x", "xy") else x, 1 - y if "y" in axis else y, core)

        def onward(index, half, near, axis):
            slot = place(half, near)
            return copy(index, full.at[half, slot], half, slot, axis)

        halves = range(2)
        me = [slot_of(half, x, y, core) for half in halves]
        self.direct = {
            (axis, half): copy(2 * number + half, own.at[half], half, me[half], axis)
            for number, axis in enumerate(("y", "x"))
            for half in halves
        }
        self.diagonal = [onward(4 + half, half, self.other[half], extra[half]) for half in halves]
        self.shared = [copy(6 + half, own.at[half], half, me[half], "c") for half in halves]
        self.across = [
            onward(8 + 2 * number + half, half, axis, "c")
            for number, axis in enumerate(("y", "x"))
            for half in halves
        ]
        self.last = [onward(12 + half, half, "xy", "c") for half in halves]
        self.here = [
            pltpu.make_async_copy(own.at[half], full.at[half, me[half]], local.at[half])
            for half in halves
        ]

    def start(self, half):
        self.direct[self.other[half], half].start()
        self.direct[self.extra[half], half].start()
        self.shared[half].start()
        self.here[half].start()

    def turn(self, half):
        self.direct[self.other[half], half].wait_recv()
        self.diagonal[half].start()

    def cross(self):
        for half in range(2):
            self.direct[self.extra[half], half].wait_recv()
        for copy in self.across:
            copy.start()

    def end(self):
        for half in range(2):
            self.diagonal[half].wait_recv()
            self.last[half].start()
        for copy in self.shared + self.across + self.last:
            copy.wait_recv()
        for copy in list(self.direct.values()) + self.diagonal + self.shared:
            copy.wait_send()
        for copy in self.across + self.last:
            copy.wait_send()
        for copy in self.here:
            copy.wait()


def deal(tokens, cotangent, parts, docs):
    bf16 = jnp.bfloat16
    _, shard_rows, model_width = tokens.shape
    rows = shard_rows // 2
    guests = [SquareSpread(part) for part in parts]
    part = QUARTERS * parts[0].shape[2] // 2
    planes = model_width // part // 2

    count = len(parts)

    def kernel(tokens_ref, cotangent_ref, docs_ref, *refs):
        part_refs = refs[:count]
        own_first, own_second, other_docs = refs[count : count + 3]
        square_refs = refs[count + 3 : 2 * count + 3]
        row_out, row_in, doc_out, doc_in, staged, here_sems, *scratch = refs[2 * count + 3 :]
        x, z, core = (lax.axis_index(axis) for axis in ("x", "z", "c"))
        home, stays = z // 2, (core == 1) & (plane_x(z) == x)
        targets = [{"x": keeper_x(z, core), "z": plane_of(x, index)} for index in range(2)]
        sources = [{"x": plane_x(z), "z": source_plane(half, x, core)} for half in range(2)]
        square = square_peers()
        others = [
            (peer, stays & (home == number))
            for group in (targets, sources)
            for number, peer in enumerate(group)
        ]
        signal_and_wait(square, others)
        for number, guest in enumerate(guests):
            guest.bind(
                part_refs[number], square_refs[number], *scratch[3 * number : 3 * number + 3]
            )
        guests[0].begin()
        swapped = remote_copy(docs_ref, other_docs, doc_out, doc_in, square[1])
        swapped.start()
        at = pl.ds(pl.multiple_of(core * rows, rows), rows)
        def when_own(number, index, local, away):
            source, own = staged.at[number, index], (own_first, own_second)[number]
            here = pltpu.make_async_copy(source, own.at[home], here_sems.at[number])
            sent = remote_copy(
                source,
                own.at[home],
                row_out.at[2 * number + index],
                row_in.at[2 * number + home],
                targets[index],
            )

            @pl.when(stays & (home == index))
            def _():
                local(here)

            @pl.when(jnp.logical_not(stays & (home == index)))
            def _():
                away(sent)

        for number, source in enumerate((tokens_ref, cotangent_ref)):
            for index in range(2):
                for x_part in range(2):
                    for plane in range(planes):
                        place = (2 * plane + x_part) * part
                        start = (planes * x_part + plane) * part
                        staged[number, index, :, place : place + part] = source[
                            index, at, start : start + part
                        ]
                when_own(number, index, lambda copy: copy.start(), lambda copy: copy.start())
        for guest in guests[1:]:
            guest.begin()
        for guest in guests:
            guest.end()
        swapped.wait()
        for number, own in enumerate((own_first, own_second)):
            for half in range(2):
                slot = 2 * number + half

                @pl.when(jnp.logical_not(stays & (home == half)))
                def _():
                    remote_copy(
                        own.at[half], own.at[half], row_out.at[slot], row_in.at[slot], sources[half]
                    ).wait_recv()

        for number in range(2):
            for index in range(2):
                when_own(number, index, lambda copy: copy.wait(), lambda copy: copy.wait_send())

    inside = pl.BlockSpec(memory_space=pltpu.VMEM)
    anywhere = pl.BlockSpec(memory_space=pl.ANY)
    dma = pltpu.SemaphoreType.DMA
    shape = jax.ShapeDtypeStruct
    return pl.pallas_call(
        kernel,
        in_specs=[inside] * (3 + count),
        out_specs=[inside] * 3 + [anywhere] * count,
        out_shape=[shape((2, rows, model_width), bf16)] * 2
        + [shape(docs.shape, docs.dtype)]
        + [guest.shape for guest in guests],
        scratch_shapes=[
            dma((4,)),
            dma((4,)),
            dma(()),
            dma(()),
            pltpu.VMEM((2, 2, rows, model_width), bf16),
            dma((2,)),
        ]
        + [sems for guest in guests for sems in guest.scratch],
        compiler_params=pltpu.CompilerParams(
            collective_id=0, has_side_effects=True, vmem_limit_bytes=32 * 1024 * 1024
        ),
        cost_estimate=pl.CostEstimate(flops=0, bytes_accessed=2**27, transcendentals=0),
        name="deal",
    )(tokens, cotangent, docs, *parts)


def gather_rows(first, second):
    bf16 = jnp.bfloat16
    _, rows, model_width = first.shape

    def kernel(own_first, own_second, full_first, full_second, *scratch):
        x, y, core = (lax.axis_index(axis) for axis in GROUP)
        to_peer = {"x": {"x": 1 - x}, "y": {"y": 1 - y}, "c": {"c": 1 - core}}
        signal_and_wait([to_peer[axis] for axis in GROUP])
        gathers = [
            GroupGather(own, full, *scratch[3 * number : 3 * number + 3], to_peer, ("x", "y"))
            for number, (own, full) in enumerate(
                ((own_first, full_first), (own_second, full_second))
            )
        ]
        for gather in gathers:
            for half in range(2):
                gather.start(half)
        for gather in gathers:
            for half in range(2):
                gather.turn(half)
            gather.cross()
        for gather in gathers:
            gather.end()

    dma = pltpu.SemaphoreType.DMA
    anywhere = pl.BlockSpec(memory_space=pl.ANY)
    inside = pl.BlockSpec(memory_space=pltpu.VMEM)
    full = jax.ShapeDtypeStruct((2, MEMBERS, rows, model_width), bf16)
    results = pl.pallas_call(
        kernel,
        in_specs=[inside] * 2,
        out_specs=[anywhere] * 2,
        out_shape=[full, full],
        scratch_shapes=[dma((size,)) for size in GroupGather.scratch_sizes] * 2,
        compiler_params=pltpu.CompilerParams(collective_id=1, has_side_effects=True),
        cost_estimate=pl.CostEstimate(flops=0, bytes_accessed=2**28, transcendentals=0),
        name="gather_rows",
    )(first, second)
    return [result.reshape(2 * MEMBERS * rows, model_width) for result in results]


def exchange(name, collective_id, jobs, extra):
    bf16, f32 = jnp.bfloat16, jnp.float32
    planes, _, strip = jobs[0]["rights"][0][0].shape
    model_width = planes * strip
    first = jobs[0]["lefts"][0]
    length = first[0].shape[1] if isinstance(first, tuple) else first.shape[0]
    rows = length // (2 * MEMBERS)
    gathers = jobs[-1]["gathers"]
    handing = [job for job in jobs if job.get("hands")]

    def block(shape, index):
        return pl.BlockSpec(shape, lambda step: index, pipeline_mode=pl.Buffered(1))

    def whole(shape):
        return block(shape, (0,) * len(shape))

    anywhere = pl.BlockSpec(memory_space=pl.ANY)
    arrays, in_specs, out_shape, out_specs = [], [], [], []
    for job in jobs:
        for left in job["lefts"]:
            if isinstance(left, tuple):
                left, at = left
                in_specs.append(block((None,) + left.shape[1:], (at, 0, 0)))
            else:
                in_specs.append(whole(left.shape))
            arrays.append(left)
        for array, height, at in job["rights"]:
            arrays.append(array)
            in_specs.append(block((planes, height, strip), (0, at, 0)))
        for array, height, at in job["states"]:
            arrays.append(array)
            in_specs.append(
                whole(array.shape) if height is None else block((planes, height, strip), (0, at, 0))
            )
        out_shape.append(jax.ShapeDtypeStruct((2, rows, model_width), job["kept"]))
        out_specs.append(whole((2, rows, model_width)))
    if gathers:
        out_shape.append(jax.ShapeDtypeStruct((2, MEMBERS, rows, model_width), bf16))
        out_specs.append(anywhere)
    for job in handing:
        out_shape.append(jax.ShapeDtypeStruct((2, rows, model_width), job["kept"]))
        out_specs.append(anywhere)
    dma = pltpu.SemaphoreType.DMA
    count = len(jobs)
    scratch = [
        pltpu.VMEM((4, 2, rows, model_width), bf16),
        pltpu.VMEM((4, 2, rows, model_width), bf16),
        pltpu.VMEM((4, 2, rows, model_width), f32),
        pltpu.VMEM((6, rows, model_width), bf16),
        pltpu.VMEM((6, rows, model_width), bf16),
        pltpu.VMEM((2, rows, model_width), bf16),
        dma((4 * count,)),
        dma((4 * count,)),
        dma((6 * count,)),
        dma((6 * count,)),
        dma((2,)),
        dma((2,)),
        dma(()),
        pltpu.SemaphoreType.REGULAR((3,)),
    ] + [dma((size,)) for size in GroupGather.scratch_sizes]

    def kernel(*refs):
        refs = list(refs)

        def take(number):
            taken = refs[:number]
            del refs[:number]
            return taken

        job_refs = [
            (take(len(job["lefts"])), take(len(job["rights"])), take(len(job["states"])))
            for job in jobs
        ]
        kept_refs = take(count)
        full = take(1)[0] if gathers else None
        handed = take(len(handing))
        (core_send, core_got, sums, link_send, link_got, own) = take(6)
        (core_out, core_in, link_out, link_in, hand_out, hand_in, hand_here, ready) = take(8)
        x, y, core = (lax.axis_index(axis) for axis in GROUP)
        to_peer = {"x": {"x": 1 - x}, "y": {"y": 1 - y}, "c": {"c": 1 - core}}
        peers = [to_peer[axis] for axis in GROUP]
        hands = []
        for number, job in enumerate(jobs):
            if job.get("hands"):
                hands.append(
                    HandBack(
                        kept_refs[number],
                        lambda index: handed[0].at[index],
                        hand_out,
                        hand_in,
                        hand_here,
                    )
                )
        signal_and_wait(peers, hands[0].others if hands else ())
        gather = GroupGather(own, full, *refs, to_peer, extra) if gathers else None

        chips = ((1 - x, 1 - y), (1 - x, y), (x, 1 - y), (x, y))

        def phases(number):
            left_refs, right_refs, state_refs = job_refs[number]
            finish, kept = jobs[number]["finish"], kept_refs[number]

            def produce(chip, mine):
                at = [
                    half * MEMBERS + slot_of(half, *chips[chip], core if mine else 1 - core)
                    for half in range(2)
                ]
                at = [pl.ds(pl.multiple_of(index * rows, rows), rows) for index in at]
                blocks = [
                    jnp.concatenate([ref[at[0], :], ref[at[1], :]], axis=0) for ref in left_refs
                ]

                @pl.loop(0, planes)
                def _(step):
                    columns = lanes(step, strip)
                    product = matmul(blocks[0], right_refs[0][step])
                    for part, ref in zip(blocks[1:], right_refs[1:]):
                        product = product + matmul(part, ref[step])
                    for half in range(2):
                        piece = product[half * rows : (half + 1) * rows]
                        if mine:
                            sums[chip, half, :, columns] = piece
                        else:
                            core_send[chip, half, :, columns] = piece.astype(bf16)

            core_copies = [
                remote_copy(
                    core_send.at[chip],
                    core_got.at[chip],
                    core_out.at[4 * number + chip],
                    core_in.at[4 * number + chip],
                    to_peer["c"],
                )
                for chip in range(4)
            ]

            axes = [extra[index % 2] for index in range(4)]
            axes += ["x" if extra[half] == "y" else "y" for half in range(2)]
            chip_on = {"x": 1, "y": 2}
            links = [
                remote_copy(
                    link_send.at[index],
                    link_got.at[index],
                    link_out.at[6 * number + index],
                    link_in.at[6 * number + index],
                    to_peer[axes[index]],
                )
                for index in range(6)
            ]

            def send(index):
                half = index % 2
                chip = 0 if index < 2 else chip_on[axes[index]]
                link_send[index] = sums[chip, half].astype(bf16)
                links[index].start()

            def settle(chip):
                core_copies[chip].wait_recv()
                for half in range(2):
                    sums[chip, half] += core_got[chip, half].astype(f32)

            def begin(previous):
                if number > 0:
                    for copy in previous[0]:
                        copy.wait_send()
                    pl.semaphore_signal(
                        ready.at[2], inc=1, device_id=peers[2], device_id_type=MESH
                    )
                produce(0, False)
                if number > 0:
                    pl.semaphore_wait(ready.at[2], 1)
                core_copies[0].start()
                produce(0, True)

            def middle(previous):
                if number > 0:
                    for copy in previous[1]:
                        copy.wait_send()
                    for index in range(2):
                        pl.semaphore_signal(
                            ready.at[index], inc=1, device_id=peers[index], device_id_type=MESH
                        )
                settle(0)
                if number > 0:
                    pl.semaphore_wait(ready.at[0], 1)
                    pl.semaphore_wait(ready.at[1], 1)
                send(0)
                send(1)
                produce(1, False)
                core_copies[1].start()
                produce(1, True)
                produce(2, False)
                core_copies[2].start()
                settle(1)
                for index in (2, 3):
                    if axes[index] == "x":
                        send(index)
                produce(2, True)
                produce(3, False)
                core_copies[3].start()
                settle(2)
                for index in (2, 3):
                    if axes[index] == "y":
                        send(index)
                for half in range(2):
                    links[half].wait_recv()
                    sums[chip_on[axes[4 + half]], half] += link_got[half].astype(f32)
                    send(4 + half)
                    if half == 0:
                        produce(3, True)
                        settle(3)

            def close():
                for half in range(2):
                    links[2 + half].wait_recv()
                    links[4 + half].wait_recv()

                    @pl.loop(0, rows // 32)
                    def _(step):
                        at = pl.ds(pl.multiple_of(step * 32, 32), 32)
                        total = sums[3, half, at, :] + link_got[2 + half, at, :].astype(f32)
                        total = total + link_got[4 + half, at, :].astype(f32)
                        finish(total, half, at, state_refs, kept, own)

                    if jobs[number]["gathers"]:
                        gather.start(half)
                    if jobs[number].get("hands"):
                        hands[0].start(half)
                if jobs[number]["gathers"]:
                    for half in range(2):
                        gather.turn(half)
                    gather.cross()
                    gather.end()

            return begin, middle, close, (core_copies, links)

        steps = [phases(number) for number in range(count)]
        steps[0][0](None)
        for number, (_, middle, close, copies) in enumerate(steps):
            middle(steps[number - 1][3])
            if number + 1 < count:
                steps[number + 1][0](copies)
            close()
        for hand in hands:
            for index in range(2):
                hand.wait_recv(index)
            hand.wait_send()
        for copy in steps[-1][3][0] + steps[-1][3][1]:
            copy.wait_send()

    depth = sum(height for job in jobs for _, height, _ in job["rights"])
    results = list(
        pl.pallas_call(
            kernel,
            grid=(1,),
            in_specs=in_specs,
            out_specs=out_specs,
            out_shape=out_shape,
            scratch_shapes=scratch,
            compiler_params=pltpu.CompilerParams(
                collective_id=collective_id,
                has_side_effects=True,
                vmem_limit_bytes=60 * 1024 * 1024,
            ),
            cost_estimate=pl.CostEstimate(
                flops=2 * length * depth * model_width,
                bytes_accessed=200 * 1024 * 1024,
                transcendentals=0,
            ),
            name=name,
        )(*arrays)
    )
    if gathers:
        results[count] = results[count].reshape(length, model_width)
    return results


def closing(grads, own_output, got_tokens):
    bf16, f32 = jnp.bfloat16, jnp.float32
    _, rows, model_width = own_output.shape
    count = len(grads)
    guests = [SquareReturn(grad) for grad in grads]

    def kernel(*refs):
        grad_refs = refs[:count]
        out_ref, tokens_ref = refs[count : count + 2]
        got_refs = refs[count + 2 : 2 * count + 2]
        output, tokens = refs[2 * count + 2 : 2 * count + 4]
        wide, hand_out, hand_in, core_out, core_in, local = refs[2 * count + 4 : 2 * count + 10]
        guest_scratch = refs[2 * count + 10 :]
        core = lax.axis_index("c")
        to_core = {"c": 1 - core}
        at = pl.ds(pl.multiple_of(core * rows, rows), rows)
        hand = HandBack(
            out_ref, lambda index: output.at[index, at], hand_out, hand_in, local.at[2]
        )
        signal_and_wait(square_peers() + [to_core], hand.others)
        for half in range(2):
            hand.start(half)
        for number, guest in enumerate(guests):
            guest.bind(
                grad_refs[number], got_refs[number], *guest_scratch[3 * number : 3 * number + 3]
            )
            guest.begin()
        copies = []
        for index in range(2):
            wide[index] = tokens_ref[index].astype(f32)
            copies += [
                remote_copy(
                    wide.at[index],
                    tokens.at[index, at],
                    core_out.at[index],
                    core_in.at[index],
                    to_core,
                ),
                pltpu.make_async_copy(wide.at[index], tokens.at[index, at], local.at[index]),
            ]
        for copy in copies:
            copy.start()
        for index in range(2):
            place = output.at[index, at]
            hand.wait_recv(index)
            copies.append(
                remote_copy(
                    place, place, core_out.at[2 + index], core_in.at[2 + index], to_core
                )
            )
            copies[-1].start()
        hand.wait_send()
        for copy in copies:
            copy.wait()
        for guest in guests:
            guest.end()

    anywhere = pl.BlockSpec(memory_space=pl.ANY)
    shape = jax.ShapeDtypeStruct
    dma = pltpu.SemaphoreType.DMA
    operands = (*grads, own_output, got_tokens)
    return pl.pallas_call(
        kernel,
        grid=(1,),
        in_specs=[in_spec(array.shape) for array in operands],
        out_specs=[anywhere] * (count + 2),
        out_shape=[guest.shape for guest in guests]
        + [shape((2, 2 * rows, model_width), bf16), shape((2, 2 * rows, model_width), f32)],
        scratch_shapes=[
            pltpu.VMEM((2, rows, model_width), f32),
            dma((2,)),
            dma((2,)),
            dma((4,)),
            dma((4,)),
            dma((3,)),
        ]
        + [sems for guest in guests for sems in guest.scratch],
        compiler_params=pltpu.CompilerParams(
            collective_id=5, has_side_effects=True, vmem_limit_bytes=60 * 1024 * 1024
        ),
        cost_estimate=pl.CostEstimate(flops=0, bytes_accessed=2**27, transcendentals=0),
        name="closing",
    )(*operands)


def head_lanes(head):
    return slice(head * HEAD_DIM, (head + 1) * HEAD_DIM)


def attention_forward_kernel(query, key, value, first, attended, heads_out, log_total):
    tile = pl.program_id(0)
    rows, width = query.shape
    heads = range(width // HEAD_DIM)
    first_key = first[...]
    row_index = lax.broadcasted_iota(jnp.int32, (rows, rows), 0)
    column_index = lax.broadcasted_iota(jnp.int32, (rows, rows), 1)

    def block(index, carry, diagonal):
        at = pl.ds(pl.multiple_of(index * rows, rows), rows)
        visible = column_index + index * rows >= first_key
        if diagonal:
            visible = visible & (column_index <= row_index)
        result = []
        for head in heads:
            lane = head_lanes(head)
            largest, total, summed = carry[head]
            scores = contract_cols(query[:, lane], key[at, lane])
            scores = jnp.where(visible, scores, masked_score)
            new_largest = jnp.maximum(largest, jnp.max(scores, axis=1, keepdims=True))
            weights = jnp.where(visible, jnp.exp(scores - new_largest), 0.0)
            scaling = jnp.exp(largest - new_largest)
            total = total * scaling + jnp.sum(weights, axis=1, keepdims=True)
            summed = summed * scaling + matmul(weights.astype(jnp.bfloat16), value[at, lane])
            result.append((new_largest, total, summed))
        return tuple(result)

    carry = tuple(
        (
            jnp.full((rows, 1), masked_score, jnp.float32),
            jnp.zeros((rows, 1), jnp.float32),
            jnp.zeros((rows, HEAD_DIM), jnp.float32),
        )
        for _ in heads
    )
    carry = lax.fori_loop(0, tile, lambda index, kept: block(index, kept, False), carry)
    carry = block(tile, carry, True)
    for head in heads:
        largest, total, summed = carry[head]
        summed = summed / total
        attended[:, head_lanes(head)] = summed
        heads_out[:, head_lanes(head)] = summed.astype(jnp.bfloat16)
        log_total[head, :, :] = jnp.broadcast_to(
            jnp.transpose(largest + jnp.log(total)), log_total.shape[1:]
        )


def attention_forward(query, key, value, first_key, tile_rows):
    length, width = query.shape
    heads = width // HEAD_DIM
    part = pl.BlockSpec((tile_rows, width), lambda tile: (tile, 0))
    return pl.pallas_call(
        attention_forward_kernel,
        grid=(length // tile_rows,),
        in_specs=[
            part,
            in_spec(key.shape),
            in_spec(value.shape),
            pl.BlockSpec((tile_rows, 1), lambda tile: (tile, 0)),
        ],
        out_specs=[
            part,
            part,
            pl.BlockSpec((heads, 8, tile_rows), lambda tile: (0, 0, tile)),
        ],
        out_shape=[
            jax.ShapeDtypeStruct((length, width), jnp.float32),
            jax.ShapeDtypeStruct((length, width), jnp.bfloat16),
            jax.ShapeDtypeStruct((heads, 8, length), jnp.float32),
        ],
        compiler_params=pltpu.CompilerParams(vmem_limit_bytes=60 * 1024 * 1024),
        cost_estimate=pl.CostEstimate(
            flops=2 * length * length * width,
            bytes_accessed=10 * length * width,
            transcendentals=length * length * heads // 2,
        ),
        name="attention_forward",
    )(query, key, value, first_key)


def project(all_tokens, units, head_width, cosine, sine_table):
    bf16, f32 = jnp.bfloat16, jnp.float32
    length, model_width = all_tokens.shape
    planes, height, strip = units.shape
    rows = 256

    def kernel(tokens, weight, gains, cos, sin, normed, query, key, value):
        values = tokens[...].astype(f32)
        low = (values * rms_scale(values) * gain_row(gains, 0)).astype(bf16)
        normed[...] = low

        def turn(part):
            return part * cos[...] + pltpu.roll(part, HEAD_DIM // 2, 1) * sin[...]

        def projection(start):
            return by_planes(low, weight, start, head_width)

        query_proj = projection(0)
        key_proj = projection(head_width)
        for head in range(head_width // HEAD_DIM):
            at = slice(head * HEAD_DIM, (head + 1) * HEAD_DIM)
            query[:, at] = (turn(query_proj[:, at]) * HEAD_DIM ** (-0.5)).astype(bf16)
            key[:, at] = turn(key_proj[:, at]).astype(bf16)
        value[...] = projection(2 * head_width).astype(bf16)

    def tile(width):
        return pl.BlockSpec((rows, width), lambda step: (step, 0))

    gain_block = height // 16 - 1
    shape = jax.ShapeDtypeStruct
    return pl.pallas_call(
        kernel,
        grid=(length // rows,),
        in_specs=[
            tile(model_width),
            pl.BlockSpec((planes, 3 * head_width, strip), lambda step: (0, 0, 0)),
            pl.BlockSpec((planes, 16, strip), lambda step: (0, gain_block, 0)),
            tile(HEAD_DIM),
            tile(HEAD_DIM),
        ],
        out_specs=[tile(model_width)] + [tile(head_width)] * 3,
        out_shape=[shape((length, model_width), bf16)] + [shape((length, head_width), bf16)] * 3,
        compiler_params=pltpu.CompilerParams(vmem_limit_bytes=60 * 1024 * 1024),
        cost_estimate=pl.CostEstimate(
            flops=6 * length * head_width * model_width,
            bytes_accessed=4 * length * model_width,
            transcendentals=0,
        ),
        name="project",
    )(all_tokens, units, units, cosine, sine_table)


def gain_row(gains, index):
    return jnp.concatenate(
        [gains[plane, index : index + 1, :] for plane in range(gains.shape[0])], axis=1
    ).astype(jnp.float32)


def by_planes(rows, units, start, height):
    strip = units.shape[2]
    total = contract_cols(rows[:, :strip], units[0, start : start + height, :])
    for plane in range(1, units.shape[0]):
        total = total + contract_cols(
            rows[:, plane * strip : (plane + 1) * strip], units[plane, start : start + height, :]
        )
    return total


def hidden_forward(normed_ffn, units, hidden):
    bf16, f32 = jnp.bfloat16, jnp.float32
    length, model_width = normed_ffn.shape
    rows = 256

    def kernel(normed, weights, mixed, gate_factor, up_factor):
        low = normed[...]
        gate_proj = by_planes(low, weights, 0, hidden)
        up_proj = by_planes(low, weights, hidden, hidden)
        sigmoid = 1.0 / (1.0 + jnp.exp(-gate_proj))
        silu = gate_proj * sigmoid
        up_factor[...] = silu
        gate_factor[...] = up_proj * sigmoid * (1.0 + gate_proj * (1.0 - sigmoid))
        mixed[...] = (silu * up_proj).astype(bf16)

    def tile(width):
        return pl.BlockSpec((rows, width), lambda step: (step, 0))

    shape = jax.ShapeDtypeStruct
    return pl.pallas_call(
        kernel,
        grid=(length // rows,),
        in_specs=[tile(model_width), in_spec(units.shape)],
        out_specs=[tile(hidden)] * 3,
        out_shape=[shape((length, hidden), bf16)] + [shape((length, hidden), f32)] * 2,
        compiler_params=pltpu.CompilerParams(vmem_limit_bytes=60 * 1024 * 1024),
        cost_estimate=pl.CostEstimate(
            flops=4 * length * hidden * model_width,
            bytes_accessed=4 * length * model_width,
            transcendentals=length * hidden,
        ),
        name="hidden_forward",
    )(normed_ffn, units)


def hidden_backward(gate_factor, up_factor, all_cotangent, units, hidden):
    bf16 = jnp.bfloat16
    length, model_width = all_cotangent.shape
    rows = 256

    def kernel(gate_ref, up_ref, cotangent, weights, grad_pair):
        grad_mixed = by_planes(cotangent[...], weights, 0, hidden)
        grad_gate, grad_up = grad_mixed * gate_ref[...], grad_mixed * up_ref[...]
        grad_pair[...] = jnp.concatenate([grad_gate, grad_up], axis=1).astype(bf16)

    def tile(width):
        return pl.BlockSpec((rows, width), lambda step: (step, 0))

    shape = jax.ShapeDtypeStruct
    return pl.pallas_call(
        kernel,
        grid=(length // rows,),
        in_specs=[tile(hidden), tile(hidden), tile(model_width), in_spec(units.shape)],
        out_specs=tile(2 * hidden),
        out_shape=shape((length, 2 * hidden), bf16),
        compiler_params=pltpu.CompilerParams(vmem_limit_bytes=60 * 1024 * 1024),
        cost_estimate=pl.CostEstimate(
            flops=2 * length * hidden * model_width,
            bytes_accessed=4 * length * model_width,
            transcendentals=length * hidden,
        ),
        name="hidden_backward",
    )(gate_factor, up_factor, all_cotangent, units)


def attention_backward_kernel(guests, *refs):
    count = len(guests)
    query, key, value, branch, weight, attended, log_total, first, cos, sin = refs[:10]
    grads, key_sum, value_sum = refs[10 + count], refs[11 + 2 * count], refs[12 + 2 * count]
    guest_scratch = refs[13 + 2 * count :]
    for number, guest in enumerate(guests):
        guest.bind(
            refs[10 + number], refs[11 + count + number], *guest_scratch[3 * number : 3 * number + 3]
        )
    tile = pl.program_id(0)

    @pl.when(tile == 0)
    def _():
        signal_and_wait(square_peers())
        for guest in guests:
            guest.begin()

    rows, width = query.shape
    heads = range(width // HEAD_DIM)
    grad_tiles = by_planes(branch[...], weight, 0, width)
    grad_low = grad_tiles.astype(jnp.bfloat16)
    product = grad_low.astype(jnp.float32) * attended[...]
    centre_rows = [
        jnp.transpose(jnp.sum(product[:, head_lanes(head)], axis=1, keepdims=True))
        for head in heads
    ]
    first_row = first[:1, :]
    key_index = lax.broadcasted_iota(jnp.int32, (rows, rows), 0)
    query_index = lax.broadcasted_iota(jnp.int32, (rows, rows), 1)

    def block(index, carry, diagonal):
        at = pl.ds(pl.multiple_of(index * rows, rows), rows)
        visible = key_index + index * rows >= first_row
        if diagonal:
            visible = visible & (key_index <= query_index)
        result = []
        for head in heads:
            lane = head_lanes(head)
            query_tile, grad_tile = query[:, lane], grad_low[:, lane]
            key_block = key[at, lane]
            scores = contract_cols(key_block, query_tile)
            probability = jnp.where(visible, jnp.exp(scores - log_total[head, :1, :]), 0.0)
            grad_prob = contract_cols(value[at, lane], grad_tile)
            grad_scores = (probability * (grad_prob - centre_rows[head])).astype(jnp.bfloat16)
            key_part = matmul(grad_scores, query_tile)
            value_part = matmul(probability.astype(jnp.bfloat16), grad_tile)
            if diagonal:
                key_sum[at, lane] = key_part
                value_sum[at, lane] = value_part
            else:
                key_sum[at, lane] += key_part
                value_sum[at, lane] += value_part
            result.append(carry[head] + contract_rows(grad_scores, key_block))
        return tuple(result)

    def turn_back(part, at):
        return part * cos[at, :] - pltpu.roll(part, HEAD_DIM // 2, 1) * sin[at, :]

    carry = tuple(jnp.zeros((rows, HEAD_DIM), jnp.float32) for _ in heads)
    carry = lax.fori_loop(0, tile, lambda index, kept: block(index, kept, False), carry)
    carry = block(tile, carry, True)
    here = pl.ds(pl.multiple_of(tile * rows, rows), rows)
    for head in heads:
        grads[0, here, head_lanes(head)] = (
            turn_back(carry[head], here) * HEAD_DIM ** (-0.5)
        ).astype(jnp.bfloat16)

    @pl.when(tile == pl.num_programs(0) - 1)
    def _():
        @pl.loop(0, pl.num_programs(0))
        def _(index):
            at = pl.ds(pl.multiple_of(index * rows, rows), rows)
            for head in heads:
                lane = head_lanes(head)
                grads[1, at, lane] = turn_back(key_sum[at, lane], at).astype(jnp.bfloat16)
                grads[2, at, lane] = value_sum[at, lane].astype(jnp.bfloat16)

        for guest in guests:
            guest.end()


def attention_backward(
    query,
    key,
    value,
    grad_branch,
    units,
    attended,
    log_total,
    first_key,
    cosine,
    sine_table,
    tile_rows,
    summed,
):
    guests = [SquareReturn(grad) for grad in summed]
    length, width = query.shape
    model_width = grad_branch.shape[1]
    heads = width // HEAD_DIM
    part = pl.BlockSpec((tile_rows, width), lambda tile: (tile, 0))
    shape = jax.ShapeDtypeStruct((3, length, width), jnp.bfloat16)
    return pl.pallas_call(
        functools.partial(attention_backward_kernel, guests),
        grid=(length // tile_rows,),
        in_specs=[
            part,
            in_spec(key.shape),
            in_spec(value.shape),
            pl.BlockSpec((tile_rows, model_width), lambda tile: (tile, 0)),
            pl.BlockSpec((units.shape[0], width, units.shape[2]), lambda tile: (0, 3, 0)),
            part,
            pl.BlockSpec((heads, 8, tile_rows), lambda tile: (0, 0, tile)),
            pl.BlockSpec((8, tile_rows), lambda tile: (0, tile)),
            in_spec(cosine.shape),
            in_spec(sine_table.shape),
        ]
        + [in_spec(grad.shape) for grad in summed],
        out_specs=[in_spec((3, length, width))]
        + [pl.BlockSpec(memory_space=pl.ANY)] * len(guests),
        out_shape=[shape] + [guest.shape for guest in guests],
        scratch_shapes=[
            pltpu.VMEM((length, width), jnp.float32),
            pltpu.VMEM((length, width), jnp.float32),
        ]
        + [sems for guest in guests for sems in guest.scratch],
        compiler_params=pltpu.CompilerParams(
            collective_id=6, has_side_effects=True, vmem_limit_bytes=60 * 1024 * 1024
        ),
        cost_estimate=pl.CostEstimate(
            flops=5 * length * length * width + 2 * length * width * model_width,
            bytes_accessed=24 * length * width,
            transcendentals=length * length * heads // 2,
        ),
        name="attention_backward",
    )(
        query,
        key,
        value,
        grad_branch,
        units,
        attended,
        log_total,
        first_key,
        cosine,
        sine_table,
        *summed,
    )


def group_device(
    tokens,
    doc_starts,
    query_weight,
    key_weight,
    value_weight,
    out_weight,
    gate_weight,
    up_weight,
    down_weight,
    attention_gain,
    feedforward_gain,
    cotangent,
):
    bf16, f32 = jnp.bfloat16, jnp.float32
    x_at, z_at, core = (lax.axis_index(name) for name in ("x", "z", "c"))
    _, shard_rows, model_width = tokens.shape
    slice_width = query_weight.shape[0]
    half_rows = shard_rows // 2
    length = 2 * MEMBERS * half_rows
    planes = lax.axis_size("z")
    strip = model_width // planes
    head_width = query_weight.shape[1] // QUARTERS
    hidden = gate_weight.shape[1] // QUARTERS

    def keep_naturally(kept, half, at, values):
        part = strip // 2
        for x in range(2):
            for plane in range(planes):
                start = plane * strip + x * part
                place = x * planes * part + plane * part
                kept[half, at, place : place + part] = values[:, start : start + part]

    def units_of(weight):
        return weight.reshape(QUARTERS, -1, slice_width)

    def far_sum(grads):
        return lax.psum_scatter(grads.astype(bf16), "z", scatter_dimension=1, tiled=True)

    gains = jnp.concatenate(
        [attention_gain[None], feedforward_gain[None], jnp.zeros((14, slice_width), bf16)]
    )
    gains = jnp.broadcast_to(gains[None], (QUARTERS, 16, slice_width))
    docs = jnp.zeros((8, 128), jnp.int32).at[:2, : doc_starts.shape[1]].set(doc_starts)
    own_tokens, own_cotangent, other_docs, attention_square, pair_square, down_square = deal(
        tokens,
        cotangent,
        [
            jnp.concatenate(
                [
                    units_of(query_weight.T),
                    units_of(key_weight.T),
                    units_of(value_weight.T),
                    units_of(out_weight),
                    gains,
                ],
                axis=1,
            ),
            jnp.concatenate([units_of(gate_weight.T), units_of(up_weight.T)], axis=1),
            units_of(down_weight),
        ],
        docs,
    )
    attention_units = lax.all_gather(attention_square, "z")
    all_tokens, all_cotangent = gather_rows(own_tokens, own_cotangent)
    pair_square, _ = lax.optimization_barrier((pair_square, all_tokens))
    pair_units = lax.all_gather(pair_square, "z")

    positions = jnp.arange(length, dtype=jnp.int32)
    cosine, sine_table = turning_tables(length)
    docs = jnp.where(plane_x(z_at) == x_at, docs, other_docs)
    starts = lax.dynamic_index_in_dim(docs, z_at // 2, 0, keepdims=False)[: doc_starts.shape[1]]
    first_key = jnp.max(
        jnp.where(starts[None, :] <= positions[:, None], starts[None, :], 0), axis=1
    )
    normed, query_rot, key_rot, value_low = project(
        all_tokens, attention_units, head_width, cosine, sine_table
    )
    down_square, _ = lax.optimization_barrier((down_square, query_rot))
    down_units = lax.all_gather(down_square, "z")
    tile_rows = min(512, length)
    attended, heads_out, log_total = attention_forward(
        query_rot, key_rot, value_low, first_key[:, None], tile_rows
    )
    gains_at = (attention_units, 16, attention_units.shape[1] // 16 - 1)

    def after_attention(total, half, at, states, kept, own):
        token_ref, gain_ref = states
        residual = token_ref[half, at, :].astype(f32) + total
        kept[half, at, :] = residual
        own[half, at, :] = (residual * rms_scale(residual) * gain_row(gain_ref, 1)).astype(bf16)

    residual, normed_ffn = exchange(
        "branch_exchange",
        2,
        [
            dict(
                lefts=[heads_out],
                rights=[(attention_units, head_width, 3)],
                states=[(own_tokens, None, 0), gains_at],
                finish=after_attention,
                kept=f32,
                gathers=True,
            )
        ],
        ("x", "y"),
    )
    mixed_hidden, gate_factor, up_factor = hidden_forward(normed_ffn, pair_units, hidden)
    grad_down_all = contract_rows(mixed_hidden, all_cotangent)
    grad_pair_low = hidden_backward(
        gate_factor, up_factor, all_cotangent, down_units, hidden
    )
    grad_down = far_sum(grad_down_all)
    grad_pair_all = contract_rows(grad_pair_low, normed_ffn).astype(bf16)
    grad_pair_low, grad_pair_all = lax.optimization_barrier((grad_pair_low, grad_pair_all))
    grad_pair = far_sum(grad_pair_all)

    def after_feedforward(total, half, at, states, kept, own):
        residual_ref, cotangent_ref, gain_ref = states
        rows = residual_ref[half, at, :]
        scale = rms_scale(rows)
        weighted = total * gain_row(gain_ref, 1)
        mean = jnp.mean(weighted * rows, axis=-1, keepdims=True)
        grad = cotangent_ref[half, at, :].astype(f32) + scale * weighted - rows * scale**3 * mean
        kept[half, at, :] = grad
        own[half, at, :] = grad.astype(bf16)

    grad_residual, grad_branch = exchange(
        "feedforward_exchange",
        3,
        [
            dict(
                lefts=[grad_pair_low],
                rights=[(pair_units, 2 * hidden, 0)],
                states=[(residual, None, 0), (own_cotangent, None, 0), gains_at],
                finish=after_feedforward,
                kept=f32,
                gathers=True,
            )
        ],
        ("x", "y"),
    )
    grad_out = contract_rows(heads_out, grad_branch).astype(bf16)
    grad_qkv, spread_down = attention_backward(
        query_rot,
        key_rot,
        value_low,
        grad_branch,
        attention_units,
        attended,
        log_total,
        jnp.broadcast_to(first_key[None], (8, length)),
        cosine,
        sine_table,
        tile_rows,
        [grad_down],
    )
    grad_projections = lax.dot_general(
        grad_qkv, normed, (((1,), (0,)), ((), ())), preferred_element_type=f32
    ).reshape(3 * head_width, model_width)
    grad_attention = jnp.concatenate([grad_projections.astype(bf16), grad_out])
    grad_attention, grad_pair = lax.optimization_barrier((grad_attention, grad_pair))
    grad_attention = far_sum(grad_attention)

    def after_hidden(total, half, at, states, kept, own):
        keep_naturally(kept, half, at, (states[0][half, at, :] + total).astype(bf16))

    def after_all(total, half, at, states, kept, own):
        token_ref, grad_ref, gain_ref = states
        rows = token_ref[half, at, :].astype(f32)
        scale = rms_scale(rows)
        weighted = total * gain_row(gain_ref, 0)
        mean = jnp.mean(weighted * rows, axis=-1, keepdims=True)
        grad = grad_ref[half, at, :] + scale * weighted - rows * scale**3 * mean
        keep_naturally(kept, half, at, grad.astype(bf16))

    _, own_output, got_tokens = exchange(
        "token_exchange",
        4,
        [
            dict(
                lefts=[(grad_qkv, at) for at in range(3)],
                rights=[(attention_units, head_width, at) for at in range(3)],
                states=[(own_tokens, None, 0), (grad_residual, None, 0), gains_at],
                finish=after_all,
                kept=bf16,
                gathers=False,
                hands=True,
            ),
            dict(
                lefts=[mixed_hidden],
                rights=[(down_units, hidden, 0)],
                states=[(residual, None, 0)],
                finish=after_hidden,
                kept=bf16,
                gathers=False,
            ),
        ],
        ("x", "y"),
    )
    spread_pair, spread_attention, output, grad_tokens = closing(
        [grad_pair, grad_attention], own_output, got_tokens
    )

    def columns(grads):
        return grads.reshape(-1, slice_width).astype(f32)

    grad_down_w, grad_gate_w, grad_up_w = (
        columns(grads)
        for grads in (spread_down, spread_pair[:, :hidden], spread_pair[:, hidden:])
    )
    grad_gate_w, grad_up_w = grad_gate_w.T, grad_up_w.T
    grad_query_w, grad_key_w, grad_value_w, grad_out_w = (
        columns(spread_attention[:, at * head_width : (at + 1) * head_width]) for at in range(4)
    )
    grad_query_w, grad_key_w, grad_value_w = grad_query_w.T, grad_key_w.T, grad_value_w.T

    def gain_sum(*pairs):
        return sum(jnp.sum(weight.astype(f32) * grad, axis=1) for weight, grad in pairs)

    sums = jnp.stack(
        [
            gain_sum(
                (query_weight, grad_query_w), (key_weight, grad_key_w), (value_weight, grad_value_w)
            ),
            gain_sum((gate_weight, grad_gate_w), (up_weight, grad_up_w)),
        ]
    )
    sums = sums + swap(sums, "c")
    return (
        output,
        grad_tokens,
        grad_query_w,
        grad_key_w,
        grad_value_w,
        grad_out_w,
        grad_gate_w,
        grad_up_w,
        grad_down_w,
        sums[0] / attention_gain.astype(f32),
        sums[1] / feedforward_gain.astype(f32),
    )


def placements(stream, seq, head):
    both = (stream + seq) if isinstance(stream, tuple) else (stream, seq)
    in_specs = (
        P(stream, seq, None),
        P(stream, None),
        P(both, head),
        P(both, head),
        P(both, head),
        P(head, both),
        P(both, head),
        P(both, head),
        P(head, both),
        P(both),
        P(both),
        P(stream, seq, None),
    )
    out_specs = (
        P(stream, seq, None),
        P(stream, seq, None),
        P(both, head),
        P(both, head),
        P(both, head),
        P(head, both),
        P(both, head),
        P(both, head),
        P(head, both),
        P(both),
        P(both),
    )
    return in_specs, out_specs


def solution(mesh):
    def run(*arguments):
        tokens, doc_starts = arguments[:2]
        sizes = dict(mesh.shape)
        grouped = (
            (sizes["stream"], sizes["seq"], sizes["head"]) == (2, 8, 2)
            and tokens.shape[0] == 4
            and tokens.shape[1] <= WIN
        )
        if grouped:
            split = Mesh(mesh.devices.reshape(2, 4, 2, 2), ("x", "z", "y", "c"))
            in_specs, out_specs = placements(("x",), ("z", "y"), "c")
            step = group_device
        else:
            split = mesh
            in_specs, out_specs = placements("stream", "seq", "head")
            step = per_device
        return jax.shard_map(
            step, mesh=split, in_specs=in_specs, out_specs=out_specs, check_vma=False
        )(*arguments)

    return run
```

```python
import functools
import math

import jax
import jax.numpy as jnp
import numpy as np
from jax import lax
from jax.experimental import pallas as pl
from jax.experimental.pallas import tpu as pltpu
from jax.sharding import Mesh
from jax.sharding import PartitionSpec as P

HEAD_DIM = 128
WIN = 2048


epsilon = 1e-06
masked_score = -1e30


def from_behind(value, axis, steps):
    count = lax.axis_size(axis)
    initial, last = (max(0, -steps), min(count, count - steps))
    return lax.ppermute(value, axis, [(source, source + steps) for source in range(initial, last)])


def matmul(left, right):
    return jnp.dot(left, right, preferred_element_type=jnp.float32)


def contract_rows(left, right):
    return lax.dot_general(
        left, right, (((0,), (0,)), ((), ())), preferred_element_type=jnp.float32
    )


def contract_cols(left, right):
    return lax.dot_general(
        left, right, (((1,), (1,)), ((), ())), preferred_element_type=jnp.float32
    )


def rotary_tables(positions):
    half_dim = HEAD_DIM // 2
    frequency = jnp.exp(
        jnp.arange(half_dim).astype(jnp.float32) * (-2.0 * math.log(10000.0) / HEAD_DIM)
    )
    angles = positions.astype(jnp.float32)[:, None] * frequency[None, :]
    return (jnp.cos(angles), jnp.sin(angles))


def rotate_pairs(values, cosine, sine_table):
    half_dim = values.shape[-1] // 2
    first_half = values[..., :half_dim]
    second_half = values[..., half_dim:]
    return jnp.concatenate(
        [
            first_half * cosine - second_half * sine_table,
            second_half * cosine + first_half * sine_table,
        ],
        axis=-1,
    )


def unrotate_pairs(values, cosine, sine_table):
    half_dim = values.shape[-1] // 2
    first_half = values[..., :half_dim]
    second_half = values[..., half_dim:]
    return jnp.concatenate(
        [
            first_half * cosine + second_half * sine_table,
            second_half * cosine - first_half * sine_table,
        ],
        axis=-1,
    )


def document_number(starts, positions):
    return jnp.sum((starts[:, None, :] <= positions[None, :, None]).astype(jnp.int32), axis=2)


def rms_scale(values):
    return lax.rsqrt(jnp.mean(values * values, axis=-1, keepdims=True) + epsilon)


def norm_backward(grad_normed, inputs, row_scale, gain_vector):
    gain_grad = jnp.sum(grad_normed * inputs * row_scale, axis=0)
    weighted = grad_normed * gain_vector
    grad_inputs = row_scale * weighted - inputs * row_scale**3 * jnp.mean(
        weighted * inputs, axis=-1, keepdims=True
    )
    return (grad_inputs, gain_grad)


def per_device(
    tokens,
    doc_starts,
    query_weight,
    key_weight,
    value_weight,
    out_weight,
    gate_weight,
    up_weight,
    down_weight,
    attention_gain,
    feedforward_gain,
    cotangent,
):
    gathered = (
        lax.all_gather(query_weight, ("stream", "seq"), axis=0, tiled=True),
        lax.all_gather(key_weight, ("stream", "seq"), axis=0, tiled=True),
        lax.all_gather(value_weight, ("stream", "seq"), axis=0, tiled=True),
        lax.all_gather(out_weight, ("stream", "seq"), axis=1, tiled=True),
        lax.all_gather(gate_weight, ("stream", "seq"), axis=0, tiled=True),
        lax.all_gather(up_weight, ("stream", "seq"), axis=0, tiled=True),
        lax.all_gather(down_weight, ("stream", "seq"), axis=1, tiled=True),
        lax.all_gather(attention_gain, ("stream", "seq"), axis=0, tiled=True),
        lax.all_gather(feedforward_gain, ("stream", "seq"), axis=0, tiled=True),
    )
    (
        full_query,
        full_key,
        full_value,
        full_out,
        full_gate,
        full_up,
        full_down,
        full_gain_first,
        full_gain_second,
    ) = gathered
    streams, shard_rows, model_width = tokens.shape
    head_width = full_query.shape[1]
    local_heads = head_width // HEAD_DIM
    flat_rows = streams * shard_rows
    seq_index = lax.axis_index("seq")
    halo_shards = min(WIN // shard_rows, lax.axis_size("seq") - 1)
    window_rows = (halo_shards + 1) * shard_rows
    inputs = tokens.reshape(flat_rows, model_width).astype(jnp.float32)
    scale_first = rms_scale(inputs)
    gain_first = full_gain_first.astype(jnp.float32)
    normed = (inputs * scale_first * gain_first).astype(jnp.bfloat16)
    query_proj = matmul(normed, full_query).reshape(streams, shard_rows, local_heads, HEAD_DIM)
    key_proj = matmul(normed, full_key).reshape(streams, shard_rows, local_heads, HEAD_DIM)
    value_low = (
        matmul(normed, full_value).astype(jnp.bfloat16).reshape(streams, shard_rows, head_width)
    )
    positions = seq_index * shard_rows + jnp.arange(shard_rows, dtype=jnp.int32)
    cosine, sine_table = rotary_tables(positions)
    cosine = cosine[None, :, None, :]
    sine_table = sine_table[None, :, None, :]
    query_rot = (rotate_pairs(query_proj, cosine, sine_table) * HEAD_DIM ** (-0.5)).astype(
        jnp.bfloat16
    )
    key_rot = rotate_pairs(key_proj, cosine, sine_table).astype(jnp.bfloat16)
    paired = jnp.stack([key_rot.reshape(streams, shard_rows, head_width), value_low])
    pieces = []
    for distance in range(halo_shards, 0, -1):
        pieces.append(from_behind(paired, "seq", distance))
    window = jnp.concatenate(pieces + [paired], axis=2)
    key_positions = (seq_index - halo_shards) * shard_rows + jnp.arange(
        window_rows, dtype=jnp.int32
    )
    query_docs = document_number(doc_starts, positions)
    key_docs = document_number(doc_starts, key_positions)
    offsets = positions[:, None] - key_positions[None, :]
    allowed = ((offsets >= 0) & (offsets < WIN))[None] & (
        query_docs[:, :, None] == key_docs[:, None, :]
    )
    query_heads = jnp.transpose(query_rot, (2, 0, 1, 3))
    key_heads = jnp.transpose(
        window[0].reshape(streams, window_rows, local_heads, HEAD_DIM), (2, 0, 1, 3)
    )
    value_heads = jnp.transpose(
        window[1].reshape(streams, window_rows, local_heads, HEAD_DIM), (2, 0, 1, 3)
    )

    def head_forward(operands):
        query_one, key_one, value_one = operands
        scores = jnp.einsum("sqe,ske->sqk", query_one, key_one, preferred_element_type=jnp.float32)
        scores = jnp.where(allowed, scores, masked_score)
        largest = jnp.max(scores, axis=-1, keepdims=True)
        weights = jnp.exp(scores - largest)
        totals = jnp.sum(weights, axis=-1, keepdims=True)
        probability = (weights / totals).astype(jnp.bfloat16)
        attended = jnp.einsum(
            "sqk,ske->sqe", probability, value_one, preferred_element_type=jnp.float32
        )
        return (attended, (largest + jnp.log(totals))[..., 0])

    attended, log_totals = lax.map(head_forward, (query_heads, key_heads, value_heads))
    heads_out = (
        jnp.transpose(attended, (1, 2, 0, 3)).reshape(flat_rows, head_width).astype(jnp.bfloat16)
    )
    attention_sum = lax.psum(matmul(heads_out, full_out), "head")
    residual = inputs + attention_sum
    scale_second = rms_scale(residual)
    gain_second = full_gain_second.astype(jnp.float32)
    normed_ffn = (residual * scale_second * gain_second).astype(jnp.bfloat16)
    gate_proj = matmul(normed_ffn, full_gate)
    up_proj = matmul(normed_ffn, full_up)
    sigmoid_gate = jax.nn.sigmoid(gate_proj)
    silu_gate = gate_proj * sigmoid_gate
    mixed_hidden = (silu_gate * up_proj).astype(jnp.bfloat16)
    feedforward_sum = lax.psum(matmul(mixed_hidden, full_down).astype(jnp.bfloat16), "head").astype(
        jnp.float32
    )
    output = (
        (residual + feedforward_sum).astype(jnp.bfloat16).reshape(streams, shard_rows, model_width)
    )
    gathered = (
        lax.all_gather(query_weight, ("stream", "seq"), axis=0, tiled=True),
        lax.all_gather(key_weight, ("stream", "seq"), axis=0, tiled=True),
        lax.all_gather(value_weight, ("stream", "seq"), axis=0, tiled=True),
        lax.all_gather(out_weight, ("stream", "seq"), axis=1, tiled=True),
        lax.all_gather(gate_weight, ("stream", "seq"), axis=0, tiled=True),
        lax.all_gather(up_weight, ("stream", "seq"), axis=0, tiled=True),
        lax.all_gather(down_weight, ("stream", "seq"), axis=1, tiled=True),
        lax.all_gather(attention_gain, ("stream", "seq"), axis=0, tiled=True),
        lax.all_gather(feedforward_gain, ("stream", "seq"), axis=0, tiled=True),
    )
    (
        full_query,
        full_key,
        full_value,
        full_out,
        full_gate,
        full_up,
        full_down,
        full_gain_first,
        full_gain_second,
    ) = gathered
    grad_output = cotangent.reshape(flat_rows, model_width)
    grad_down = contract_rows(mixed_hidden, grad_output)
    grad_mixed = contract_cols(grad_output, full_down)
    grad_gate_low = (
        grad_mixed * up_proj * sigmoid_gate * (1.0 + gate_proj * (1.0 - sigmoid_gate))
    ).astype(jnp.bfloat16)
    grad_up_low = (grad_mixed * silu_gate).astype(jnp.bfloat16)
    grad_gate_w = contract_rows(normed_ffn, grad_gate_low)
    grad_up_w = contract_rows(normed_ffn, grad_up_low)
    grad_normed_ffn = lax.psum(
        contract_cols(grad_gate_low, full_gate) + contract_cols(grad_up_low, full_up), "head"
    )
    grad_residual_norm, grad_gain_second = norm_backward(
        grad_normed_ffn, residual, scale_second, gain_second
    )
    grad_residual = grad_output.astype(jnp.float32) + grad_residual_norm
    grad_branch = grad_residual.astype(jnp.bfloat16)
    grad_out_w = contract_rows(heads_out, grad_branch)
    grad_heads = contract_cols(grad_branch, full_out).astype(jnp.bfloat16)
    grad_heads_major = jnp.transpose(
        grad_heads.reshape(streams, shard_rows, local_heads, HEAD_DIM), (2, 0, 1, 3)
    )

    def head_backward(operands):
        query_one, key_one, value_one, grad_one, log_one = operands
        scores = jnp.einsum("sqe,ske->sqk", query_one, key_one, preferred_element_type=jnp.float32)
        scores = jnp.where(allowed, scores, masked_score)
        probability = jnp.exp(scores - log_one[..., None])
        grad_prob = jnp.einsum(
            "sqe,ske->sqk", grad_one, value_one, preferred_element_type=jnp.float32
        )
        centre = jnp.sum(probability * grad_prob, axis=-1, keepdims=True)
        grad_scores = (probability * (grad_prob - centre)).astype(jnp.bfloat16)
        grad_query_one = jnp.einsum(
            "sqk,ske->sqe", grad_scores, key_one, preferred_element_type=jnp.float32
        )
        grad_key_one = jnp.einsum(
            "sqk,sqe->ske", grad_scores, query_one, preferred_element_type=jnp.float32
        )
        grad_value_one = jnp.einsum(
            "sqk,sqe->ske",
            probability.astype(jnp.bfloat16),
            grad_one,
            preferred_element_type=jnp.float32,
        )
        return (grad_query_one, grad_key_one, grad_value_one)

    grad_query_heads, grad_key_heads, grad_value_heads = lax.map(
        head_backward, (query_heads, key_heads, value_heads, grad_heads_major, log_totals)
    )
    grad_window = jnp.transpose(
        jnp.stack([grad_key_heads, grad_value_heads]), (0, 2, 3, 1, 4)
    ).reshape(2, streams, window_rows, head_width)
    grad_paired = grad_window[:, :, halo_shards * shard_rows :]
    for distance in range(halo_shards, 0, -1):
        index_piece = halo_shards - distance
        grad_paired = grad_paired + from_behind(
            grad_window[:, :, index_piece * shard_rows : (index_piece + 1) * shard_rows],
            "seq",
            -distance,
        )
    grad_key_rot = grad_paired[0].reshape(streams, shard_rows, local_heads, HEAD_DIM)
    grad_query_rot = jnp.transpose(grad_query_heads, (1, 2, 0, 3))
    grad_query_low = (
        (unrotate_pairs(grad_query_rot, cosine, sine_table) * HEAD_DIM ** (-0.5))
        .reshape(flat_rows, head_width)
        .astype(jnp.bfloat16)
    )
    grad_key_low = (
        unrotate_pairs(grad_key_rot, cosine, sine_table)
        .reshape(flat_rows, head_width)
        .astype(jnp.bfloat16)
    )
    grad_value_low = grad_paired[1].reshape(flat_rows, head_width).astype(jnp.bfloat16)
    grad_query_w = contract_rows(normed, grad_query_low)
    grad_key_w = contract_rows(normed, grad_key_low)
    grad_value_w = contract_rows(normed, grad_value_low)
    grad_normed = lax.psum(
        contract_cols(grad_query_low, full_query)
        + contract_cols(grad_key_low, full_key)
        + contract_cols(grad_value_low, full_value),
        "head",
    )
    grad_inputs_norm, grad_gain_first = norm_backward(grad_normed, inputs, scale_first, gain_first)
    grad_tokens = (grad_residual + grad_inputs_norm).reshape(streams, shard_rows, model_width)
    reduced = (
        lax.psum_scatter(grad_query_w, ("stream", "seq"), scatter_dimension=0, tiled=True),
        lax.psum_scatter(grad_key_w, ("stream", "seq"), scatter_dimension=0, tiled=True),
        lax.psum_scatter(grad_value_w, ("stream", "seq"), scatter_dimension=0, tiled=True),
        lax.psum_scatter(grad_out_w, ("stream", "seq"), scatter_dimension=1, tiled=True),
        lax.psum_scatter(grad_gate_w, ("stream", "seq"), scatter_dimension=0, tiled=True),
        lax.psum_scatter(grad_up_w, ("stream", "seq"), scatter_dimension=0, tiled=True),
        lax.psum_scatter(grad_down, ("stream", "seq"), scatter_dimension=1, tiled=True),
        lax.psum_scatter(grad_gain_first, ("stream", "seq"), scatter_dimension=0, tiled=True),
        lax.psum_scatter(grad_gain_second, ("stream", "seq"), scatter_dimension=0, tiled=True),
    )
    return (
        output,
        grad_tokens,
        reduced[0],
        reduced[1],
        reduced[2],
        reduced[3],
        reduced[4],
        reduced[5],
        reduced[6],
        reduced[7],
        reduced[8],
    )


GROUP = ("x", "y", "c")
MEMBERS = 8
QUARTERS = 4
MESH = pl.DeviceIdType.MESH


def turning_tables(length):
    half_dim = HEAD_DIM // 2
    frequency = np.exp(
        np.arange(half_dim).astype(np.float32) * np.float32(-2.0 * math.log(10000.0) / HEAD_DIM)
    )
    angles = np.arange(length).astype(np.float32)[:, None] * frequency[None, :]
    cosine, sine = np.cos(angles), np.sin(angles)
    return (
        jnp.asarray(np.concatenate([cosine, cosine], axis=1)),
        jnp.asarray(np.concatenate([-sine, sine], axis=1)),
    )


def swap(value, axis):
    return lax.ppermute(value, axis, [(0, 1), (1, 0)])


def remote_copy(source, target, sent, landed, peer):
    return pltpu.make_async_remote_copy(
        source, target, sent, landed, device_id=peer, device_id_type=MESH
    )


def lanes(index, size):
    return pl.ds(pl.multiple_of(index * size, size), size)


def plane_x(plane):
    return (plane + plane // 2) % 2


def plane_of(x, index):
    return x * (1 + index) + (1 - x) * 3 * index


def keeper_x(plane, core):
    return (1 - plane_x(plane) + core) % 2


def source_plane(half, x, core):
    side = (x + core) % 2
    return 2 * half + (side if half else 1 - side)


def slot_of(half, x, y, core):
    side = (x + core) % 2
    return 4 * (side if half else 1 - side) + 2 * y + core


def square_peers():
    x, y = lax.axis_index("x"), lax.axis_index("y")
    return [{"y": 1 - y}, {"x": 1 - x}, {"x": 1 - x, "y": 1 - y}]


def signal_and_wait(peers, others=()):
    barrier = pltpu.get_barrier_semaphore()
    number = len(peers)
    for peer in peers:
        pl.semaphore_signal(barrier, inc=1, device_id=peer, device_id_type=MESH)
    for peer, own in others:
        number = number + jnp.where(own, 0, 1)

        @pl.when(jnp.logical_not(own))
        def _(peer=peer):
            pl.semaphore_signal(barrier, inc=1, device_id=peer, device_id_type=MESH)

    pl.semaphore_wait(barrier, number)


class HandBack:
    def __init__(self, kept, got, out_sems, in_sems, local):
        x, z, core = (lax.axis_index(axis) for axis in ("x", "z", "c"))
        self.stays = (core == 1) & (plane_x(z) == x)
        self.home = z // 2
        targets = [{"x": plane_x(z), "z": source_plane(half, x, core)} for half in range(2)]
        senders = [{"x": keeper_x(z, core), "z": plane_of(x, index)} for index in range(2)]
        self.others = [
            (peer, self.stays & (self.home == number))
            for group in (targets, senders)
            for number, peer in enumerate(group)
        ]
        self.kept, self.got, self.sems = kept, got, (out_sems, in_sems)
        self.targets, self.senders, self.local = targets, senders, local

    def here(self, half):
        return pltpu.make_async_copy(self.kept.at[half], self.got(self.home), self.local)

    def away(self, half):
        out_sems, in_sems = self.sems
        return remote_copy(
            self.kept.at[half],
            self.got(self.home),
            out_sems.at[half],
            in_sems.at[self.home],
            self.targets[half],
        )

    def start(self, half):
        own = self.stays & (self.home == half)

        @pl.when(own)
        def _():
            self.here(half).start()

        @pl.when(jnp.logical_not(own))
        def _():
            self.away(half).start()

    def wait_recv(self, index):
        own = self.stays & (self.home == index)
        out_sems, in_sems = self.sems
        place = self.got(index)

        @pl.when(own)
        def _():
            self.here(index).wait()

        @pl.when(jnp.logical_not(own))
        def _():
            remote_copy(
                place, place, out_sems.at[index], in_sems.at[index], self.senders[index]
            ).wait_recv()

    def wait_send(self):
        for half in range(2):
            own = self.stays & (self.home == half)

            @pl.when(jnp.logical_not(own))
            def _(half=half):
                self.away(half).wait_send()


def in_spec(shape):
    return pl.BlockSpec(shape, lambda *step: (0,) * len(shape), pipeline_mode=pl.Buffered(1))


class SquareSpread:
    def __init__(self, parts):
        _, self.height, self.width = parts.shape
        dma = pltpu.SemaphoreType.DMA
        self.shape = jax.ShapeDtypeStruct((self.height, QUARTERS * self.width), parts.dtype)
        self.scratch = [dma((3,)), dma((3,)), dma(())]

    def bind(self, parts, square, sent, landed, local):
        x, y = lax.axis_index("x"), lax.axis_index("y")
        chip = 2 * x + y
        place = square.at[:, lanes(chip, self.width)]
        others = (chip + 1 - 2 * y, chip + 2 - 4 * x, 3 - chip)
        self.copies = [
            remote_copy(parts.at[other], place, sent.at[index], landed.at[index], peer)
            for index, (peer, other) in enumerate(zip(square_peers(), others))
        ]
        self.copies.append(pltpu.make_async_copy(parts.at[chip], place, local))

    def begin(self):
        for copy in self.copies:
            copy.start()

    def end(self):
        for copy in self.copies:
            copy.wait()


class SquareReturn:
    def __init__(self, grads, start=0, height=None):
        whole_height, width = grads.shape
        self.start, self.height = start, height or whole_height
        self.width = width // QUARTERS
        dma = pltpu.SemaphoreType.DMA
        self.shape = jax.ShapeDtypeStruct((QUARTERS, self.height, self.width), grads.dtype)
        self.scratch = [dma((3,)), dma((3,)), dma(())]

    def bind(self, grads, got, sent, landed, local):
        grads = grads.at[pl.ds(self.start, self.height)]
        x, y = lax.axis_index("x"), lax.axis_index("y")
        chip = 2 * x + y
        others = (chip + 1 - 2 * y, chip + 2 - 4 * x, 3 - chip)
        self.copies = [
            remote_copy(
                grads.at[:, lanes(other, self.width)],
                got.at[chip],
                sent.at[index],
                landed.at[index],
                peer,
            )
            for index, (peer, other) in enumerate(zip(square_peers(), others))
        ]
        here = grads.at[:, lanes(chip, self.width)]
        self.copies.append(pltpu.make_async_copy(here, got.at[chip], local))

    def begin(self):
        for copy in self.copies:
            copy.start()

    def end(self):
        for copy in self.copies:
            copy.wait()


class GroupGather:
    scratch_sizes = (14, 14, 2)

    def __init__(self, own, full, sent, landed, local, to_peer, extra):
        x, y, core = (lax.axis_index(axis) for axis in GROUP)
        self.extra = extra
        self.other = ["x" if axis == "y" else "y" for axis in extra]

        def copy(index, source, half, slot, axis):
            return remote_copy(
                source, full.at[half, slot], sent.at[index], landed.at[index], to_peer[axis]
            )

        def place(half, axis):
            return slot_of(half, 1 - x if axis in ("x", "xy") else x, 1 - y if "y" in axis else y, core)

        def onward(index, half, near, axis):
            slot = place(half, near)
            return copy(index, full.at[half, slot], half, slot, axis)

        halves = range(2)
        me = [slot_of(half, x, y, core) for half in halves]
        self.direct = {
            (axis, half): copy(2 * number + half, own.at[half], half, me[half], axis)
            for number, axis in enumerate(("y", "x"))
            for half in halves
        }
        self.diagonal = [onward(4 + half, half, self.other[half], extra[half]) for half in halves]
        self.shared = [copy(6 + half, own.at[half], half, me[half], "c") for half in halves]
        self.across = [
            onward(8 + 2 * number + half, half, axis, "c")
            for number, axis in enumerate(("y", "x"))
            for half in halves
        ]
        self.last = [onward(12 + half, half, "xy", "c") for half in halves]
        self.here = [
            pltpu.make_async_copy(own.at[half], full.at[half, me[half]], local.at[half])
            for half in halves
        ]

    def start(self, half):
        self.direct[self.other[half], half].start()
        self.direct[self.extra[half], half].start()
        self.shared[half].start()
        self.here[half].start()

    def turn(self, half):
        self.direct[self.other[half], half].wait_recv()
        self.diagonal[half].start()

    def cross(self):
        for half in range(2):
            self.direct[self.extra[half], half].wait_recv()
        for copy in self.across:
            copy.start()

    def end(self):
        for half in range(2):
            self.diagonal[half].wait_recv()
            self.last[half].start()
        for copy in self.shared + self.across + self.last:
            copy.wait_recv()
        for copy in list(self.direct.values()) + self.diagonal + self.shared:
            copy.wait_send()
        for copy in self.across + self.last:
            copy.wait_send()
        for copy in self.here:
            copy.wait()


def deal(tokens, cotangent, parts, docs):
    bf16 = jnp.bfloat16
    _, shard_rows, model_width = tokens.shape
    rows = shard_rows // 2
    guests = [SquareSpread(part) for part in parts]
    part = QUARTERS * parts[0].shape[2] // 2
    planes = model_width // part // 2

    count = len(parts)

    def kernel(tokens_ref, cotangent_ref, docs_ref, *refs):
        part_refs = refs[:count]
        own_first, own_second, other_docs = refs[count : count + 3]
        square_refs = refs[count + 3 : 2 * count + 3]
        row_out, row_in, doc_out, doc_in, staged, here_sems, *scratch = refs[2 * count + 3 :]
        x, z, core = (lax.axis_index(axis) for axis in ("x", "z", "c"))
        home, stays = z // 2, (core == 1) & (plane_x(z) == x)
        targets = [{"x": keeper_x(z, core), "z": plane_of(x, index)} for index in range(2)]
        sources = [{"x": plane_x(z), "z": source_plane(half, x, core)} for half in range(2)]
        square = square_peers()
        others = [
            (peer, stays & (home == number))
            for group in (targets, sources)
            for number, peer in enumerate(group)
        ]
        signal_and_wait(square, others)
        for number, guest in enumerate(guests):
            guest.bind(
                part_refs[number], square_refs[number], *scratch[3 * number : 3 * number + 3]
            )
        guests[0].begin()
        swapped = remote_copy(docs_ref, other_docs, doc_out, doc_in, square[1])
        swapped.start()
        at = pl.ds(pl.multiple_of(core * rows, rows), rows)
        def when_own(number, index, local, away):
            source, own = staged.at[number, index], (own_first, own_second)[number]
            here = pltpu.make_async_copy(source, own.at[home], here_sems.at[number])
            sent = remote_copy(
                source,
                own.at[home],
                row_out.at[2 * number + index],
                row_in.at[2 * number + home],
                targets[index],
            )

            @pl.when(stays & (home == index))
            def _():
                local(here)

            @pl.when(jnp.logical_not(stays & (home == index)))
            def _():
                away(sent)

        for number, source in enumerate((tokens_ref, cotangent_ref)):
            for index in range(2):
                for x_part in range(2):
                    for plane in range(planes):
                        place = (2 * plane + x_part) * part
                        start = (planes * x_part + plane) * part
                        staged[number, index, :, place : place + part] = source[
                            index, at, start : start + part
                        ]
                when_own(number, index, lambda copy: copy.start(), lambda copy: copy.start())
        for guest in guests[1:]:
            guest.begin()
        for guest in guests:
            guest.end()
        swapped.wait()
        for number, own in enumerate((own_first, own_second)):
            for half in range(2):
                slot = 2 * number + half

                @pl.when(jnp.logical_not(stays & (home == half)))
                def _():
                    remote_copy(
                        own.at[half], own.at[half], row_out.at[slot], row_in.at[slot], sources[half]
                    ).wait_recv()

        for number in range(2):
            for index in range(2):
                when_own(number, index, lambda copy: copy.wait(), lambda copy: copy.wait_send())

    inside = pl.BlockSpec(memory_space=pltpu.VMEM)
    anywhere = pl.BlockSpec(memory_space=pl.ANY)
    dma = pltpu.SemaphoreType.DMA
    shape = jax.ShapeDtypeStruct
    return pl.pallas_call(
        kernel,
        in_specs=[inside] * (3 + count),
        out_specs=[inside] * 3 + [anywhere] * count,
        out_shape=[shape((2, rows, model_width), bf16)] * 2
        + [shape(docs.shape, docs.dtype)]
        + [guest.shape for guest in guests],
        scratch_shapes=[
            dma((4,)),
            dma((4,)),
            dma(()),
            dma(()),
            pltpu.VMEM((2, 2, rows, model_width), bf16),
            dma((2,)),
        ]
        + [sems for guest in guests for sems in guest.scratch],
        compiler_params=pltpu.CompilerParams(
            collective_id=0, has_side_effects=True, vmem_limit_bytes=32 * 1024 * 1024
        ),
        cost_estimate=pl.CostEstimate(flops=0, bytes_accessed=2**27, transcendentals=0),
        name="deal",
    )(tokens, cotangent, docs, *parts)


def gather_rows(first, second):
    bf16 = jnp.bfloat16
    _, rows, model_width = first.shape

    def kernel(own_first, own_second, full_first, full_second, *scratch):
        x, y, core = (lax.axis_index(axis) for axis in GROUP)
        to_peer = {"x": {"x": 1 - x}, "y": {"y": 1 - y}, "c": {"c": 1 - core}}
        signal_and_wait([to_peer[axis] for axis in GROUP])
        gathers = [
            GroupGather(own, full, *scratch[3 * number : 3 * number + 3], to_peer, ("x", "y"))
            for number, (own, full) in enumerate(
                ((own_first, full_first), (own_second, full_second))
            )
        ]
        for gather in gathers:
            for half in range(2):
                gather.start(half)
        for gather in gathers:
            for half in range(2):
                gather.turn(half)
            gather.cross()
        for gather in gathers:
            gather.end()

    dma = pltpu.SemaphoreType.DMA
    anywhere = pl.BlockSpec(memory_space=pl.ANY)
    inside = pl.BlockSpec(memory_space=pltpu.VMEM)
    full = jax.ShapeDtypeStruct((2, MEMBERS, rows, model_width), bf16)
    results = pl.pallas_call(
        kernel,
        in_specs=[inside] * 2,
        out_specs=[anywhere] * 2,
        out_shape=[full, full],
        scratch_shapes=[dma((size,)) for size in GroupGather.scratch_sizes] * 2,
        compiler_params=pltpu.CompilerParams(collective_id=1, has_side_effects=True),
        cost_estimate=pl.CostEstimate(flops=0, bytes_accessed=2**28, transcendentals=0),
        name="gather_rows",
    )(first, second)
    return [result.reshape(2 * MEMBERS * rows, model_width) for result in results]


def exchange(name, collective_id, jobs, extra, summed=()):
    bf16, f32 = jnp.bfloat16, jnp.float32
    planes, _, strip = jobs[0]["rights"][0][0].shape
    model_width = planes * strip
    first = jobs[0]["lefts"][0]
    length = first[0].shape[1] if isinstance(first, tuple) else first.shape[0]
    rows = length // (2 * MEMBERS)
    gathers = jobs[-1]["gathers"]
    handing = [job for job in jobs if job.get("hands")]
    guests = [SquareReturn(*grad) for grad in summed]

    def block(shape, index):
        return pl.BlockSpec(shape, lambda step: index, pipeline_mode=pl.Buffered(1))

    def whole(shape):
        return block(shape, (0,) * len(shape))

    anywhere = pl.BlockSpec(memory_space=pl.ANY)
    arrays, in_specs, out_shape, out_specs = [], [], [], []
    for job in jobs:
        for left in job["lefts"]:
            if isinstance(left, tuple):
                left, at = left
                in_specs.append(block((None,) + left.shape[1:], (at, 0, 0)))
            else:
                in_specs.append(whole(left.shape))
            arrays.append(left)
        for array, height, at in job["rights"]:
            arrays.append(array)
            in_specs.append(block((planes, height, strip), (0, at, 0)))
        for array, height, at in job["states"]:
            arrays.append(array)
            in_specs.append(
                whole(array.shape) if height is None else block((planes, height, strip), (0, at, 0))
            )
        out_shape.append(jax.ShapeDtypeStruct((2, rows, model_width), job["kept"]))
        out_specs.append(whole((2, rows, model_width)))
    if gathers:
        out_shape.append(jax.ShapeDtypeStruct((2, MEMBERS, rows, model_width), bf16))
        out_specs.append(anywhere)
    for job in handing:
        out_shape.append(jax.ShapeDtypeStruct((2, rows, model_width), job["kept"]))
        out_specs.append(anywhere)
    for grad, guest in zip(summed, guests):
        arrays.append(grad[0])
        in_specs.append(whole(grad[0].shape))
        out_shape.append(guest.shape)
        out_specs.append(anywhere)
    dma = pltpu.SemaphoreType.DMA
    count = len(jobs)
    scratch = [
        pltpu.VMEM((4, 2, rows, model_width), bf16),
        pltpu.VMEM((4, 2, rows, model_width), bf16),
        pltpu.VMEM((4, 2, rows, model_width), f32),
        pltpu.VMEM((6, rows, model_width), bf16),
        pltpu.VMEM((6, rows, model_width), bf16),
        pltpu.VMEM((2, rows, model_width), bf16),
        dma((4 * count,)),
        dma((4 * count,)),
        dma((6 * count,)),
        dma((6 * count,)),
        dma((2,)),
        dma((2,)),
        dma(()),
        pltpu.SemaphoreType.REGULAR((3,)),
    ]
    for guest in guests:
        scratch += guest.scratch
    scratch += [dma((size,)) for size in GroupGather.scratch_sizes]

    def kernel(*refs):
        refs = list(refs)

        def take(number):
            taken = refs[:number]
            del refs[:number]
            return taken

        job_refs = [
            (take(len(job["lefts"])), take(len(job["rights"])), take(len(job["states"])))
            for job in jobs
        ]
        guest_inputs = take(len(guests))
        kept_refs = take(count)
        full = take(1)[0] if gathers else None
        handed = take(len(handing))
        guest_outputs = take(len(guests))
        (core_send, core_got, sums, link_send, link_got, own) = take(6)
        (core_out, core_in, link_out, link_in, hand_out, hand_in, hand_here, ready) = take(8)
        guest_scratch = [take(3) for _ in guests]
        x, y, core = (lax.axis_index(axis) for axis in GROUP)
        to_peer = {"x": {"x": 1 - x}, "y": {"y": 1 - y}, "c": {"c": 1 - core}}
        peers = [to_peer[axis] for axis in GROUP]
        hands = []
        for number, job in enumerate(jobs):
            if job.get("hands"):
                hands.append(
                    HandBack(
                        kept_refs[number],
                        lambda index: handed[0].at[index],
                        hand_out,
                        hand_in,
                        hand_here,
                    )
                )
        corner = square_peers()[2:] if guests else []
        signal_and_wait(peers + corner, hands[0].others if hands else ())
        for number, guest in enumerate(guests):
            guest.bind(guest_inputs[number], guest_outputs[number], *guest_scratch[number])
            guest.begin()
        gather = GroupGather(own, full, *refs, to_peer, extra) if gathers else None

        chips = ((1 - x, 1 - y), (1 - x, y), (x, 1 - y), (x, y))

        def phases(number):
            left_refs, right_refs, state_refs = job_refs[number]
            finish, kept = jobs[number]["finish"], kept_refs[number]

            def produce(chip, mine):
                at = [
                    half * MEMBERS + slot_of(half, *chips[chip], core if mine else 1 - core)
                    for half in range(2)
                ]
                at = [pl.ds(pl.multiple_of(index * rows, rows), rows) for index in at]
                blocks = [
                    jnp.concatenate([ref[at[0], :], ref[at[1], :]], axis=0) for ref in left_refs
                ]

                @pl.loop(0, planes)
                def _(step):
                    columns = lanes(step, strip)
                    product = matmul(blocks[0], right_refs[0][step])
                    for part, ref in zip(blocks[1:], right_refs[1:]):
                        product = product + matmul(part, ref[step])
                    for half in range(2):
                        piece = product[half * rows : (half + 1) * rows]
                        if mine:
                            sums[chip, half, :, columns] = piece
                        else:
                            core_send[chip, half, :, columns] = piece.astype(bf16)

            core_copies = [
                remote_copy(
                    core_send.at[chip],
                    core_got.at[chip],
                    core_out.at[4 * number + chip],
                    core_in.at[4 * number + chip],
                    to_peer["c"],
                )
                for chip in range(4)
            ]

            axes = [extra[index % 2] for index in range(4)]
            axes += ["x" if extra[half] == "y" else "y" for half in range(2)]
            chip_on = {"x": 1, "y": 2}
            links = [
                remote_copy(
                    link_send.at[index],
                    link_got.at[index],
                    link_out.at[6 * number + index],
                    link_in.at[6 * number + index],
                    to_peer[axes[index]],
                )
                for index in range(6)
            ]

            def send(index):
                half = index % 2
                chip = 0 if index < 2 else chip_on[axes[index]]
                link_send[index] = sums[chip, half].astype(bf16)
                links[index].start()

            def settle(chip):
                core_copies[chip].wait_recv()
                for half in range(2):
                    sums[chip, half] += core_got[chip, half].astype(f32)

            def begin(previous):
                if number > 0:
                    for copy in previous[0]:
                        copy.wait_send()
                    pl.semaphore_signal(
                        ready.at[2], inc=1, device_id=peers[2], device_id_type=MESH
                    )
                produce(0, False)
                if number > 0:
                    pl.semaphore_wait(ready.at[2], 1)
                core_copies[0].start()
                produce(0, True)

            def middle(previous):
                if number > 0:
                    for copy in previous[1]:
                        copy.wait_send()
                    for index in range(2):
                        pl.semaphore_signal(
                            ready.at[index], inc=1, device_id=peers[index], device_id_type=MESH
                        )
                settle(0)
                if number > 0:
                    pl.semaphore_wait(ready.at[0], 1)
                    pl.semaphore_wait(ready.at[1], 1)
                send(0)
                send(1)
                produce(1, False)
                core_copies[1].start()
                produce(1, True)
                produce(2, False)
                core_copies[2].start()
                settle(1)
                for index in (2, 3):
                    if axes[index] == "x":
                        send(index)
                produce(2, True)
                produce(3, False)
                core_copies[3].start()
                settle(2)
                for index in (2, 3):
                    if axes[index] == "y":
                        send(index)
                for half in range(2):
                    links[half].wait_recv()
                    sums[chip_on[axes[4 + half]], half] += link_got[half].astype(f32)
                    send(4 + half)
                    if half == 0:
                        produce(3, True)
                        settle(3)

            def close():
                for half in range(2):
                    links[2 + half].wait_recv()
                    links[4 + half].wait_recv()

                    @pl.loop(0, rows // 32)
                    def _(step):
                        at = pl.ds(pl.multiple_of(step * 32, 32), 32)
                        total = sums[3, half, at, :] + link_got[2 + half, at, :].astype(f32)
                        total = total + link_got[4 + half, at, :].astype(f32)
                        finish(total, half, at, state_refs, kept, own)

                    if jobs[number]["gathers"]:
                        gather.start(half)
                    if jobs[number].get("hands"):
                        hands[0].start(half)
                if jobs[number]["gathers"]:
                    for half in range(2):
                        gather.turn(half)
                    gather.cross()
                    gather.end()

            return begin, middle, close, (core_copies, links)

        steps = [phases(number) for number in range(count)]
        steps[0][0](None)
        for number, (_, middle, close, copies) in enumerate(steps):
            middle(steps[number - 1][3])
            if number + 1 < count:
                steps[number + 1][0](copies)
            close()
        for hand in hands:
            for index in range(2):
                hand.wait_recv(index)
            hand.wait_send()
        for copy in steps[-1][3][0] + steps[-1][3][1]:
            copy.wait_send()
        for guest in guests:
            guest.end()

    depth = sum(height for job in jobs for _, height, _ in job["rights"])
    results = list(
        pl.pallas_call(
            kernel,
            grid=(1,),
            in_specs=in_specs,
            out_specs=out_specs,
            out_shape=out_shape,
            scratch_shapes=scratch,
            compiler_params=pltpu.CompilerParams(
                collective_id=collective_id,
                has_side_effects=True,
                vmem_limit_bytes=60 * 1024 * 1024,
            ),
            cost_estimate=pl.CostEstimate(
                flops=2 * length * depth * model_width,
                bytes_accessed=200 * 1024 * 1024,
                transcendentals=0,
            ),
            name=name,
        )(*arrays)
    )
    if gathers:
        results[count] = results[count].reshape(length, model_width)
    return results


def closing(grads, own_output, got_tokens):
    bf16, f32 = jnp.bfloat16, jnp.float32
    _, rows, model_width = own_output.shape
    count = len(grads)
    guests = [SquareReturn(*grad) for grad in grads]

    def kernel(*refs):
        grad_refs = refs[:count]
        out_ref, tokens_ref = refs[count : count + 2]
        got_refs = refs[count + 2 : 2 * count + 2]
        output, tokens = refs[2 * count + 2 : 2 * count + 4]
        wide, hand_out, hand_in, core_out, core_in, local = refs[2 * count + 4 : 2 * count + 10]
        guest_scratch = refs[2 * count + 10 :]
        core = lax.axis_index("c")
        to_core = {"c": 1 - core}
        at = pl.ds(pl.multiple_of(core * rows, rows), rows)
        hand = HandBack(
            out_ref, lambda index: output.at[index, at], hand_out, hand_in, local.at[2]
        )
        signal_and_wait(square_peers() + [to_core], hand.others)
        for half in range(2):
            hand.start(half)
        for number, guest in enumerate(guests):
            guest.bind(
                grad_refs[number], got_refs[number], *guest_scratch[3 * number : 3 * number + 3]
            )
            guest.begin()
        copies = []
        for index in range(2):
            wide[index] = tokens_ref[index].astype(f32)
            copies += [
                remote_copy(
                    wide.at[index],
                    tokens.at[index, at],
                    core_out.at[index],
                    core_in.at[index],
                    to_core,
                ),
                pltpu.make_async_copy(wide.at[index], tokens.at[index, at], local.at[index]),
            ]
        for copy in copies:
            copy.start()
        for index in range(2):
            place = output.at[index, at]
            hand.wait_recv(index)
            copies.append(
                remote_copy(
                    place, place, core_out.at[2 + index], core_in.at[2 + index], to_core
                )
            )
            copies[-1].start()
        hand.wait_send()
        for copy in copies:
            copy.wait()
        for guest in guests:
            guest.end()

    anywhere = pl.BlockSpec(memory_space=pl.ANY)
    shape = jax.ShapeDtypeStruct
    dma = pltpu.SemaphoreType.DMA
    operands = (*(grad[0] for grad in grads), own_output, got_tokens)
    return pl.pallas_call(
        kernel,
        grid=(1,),
        in_specs=[in_spec(array.shape) for array in operands],
        out_specs=[anywhere] * (count + 2),
        out_shape=[guest.shape for guest in guests]
        + [shape((2, 2 * rows, model_width), bf16), shape((2, 2 * rows, model_width), f32)],
        scratch_shapes=[
            pltpu.VMEM((2, rows, model_width), f32),
            dma((2,)),
            dma((2,)),
            dma((4,)),
            dma((4,)),
            dma((3,)),
        ]
        + [sems for guest in guests for sems in guest.scratch],
        compiler_params=pltpu.CompilerParams(
            collective_id=5, has_side_effects=True, vmem_limit_bytes=60 * 1024 * 1024
        ),
        cost_estimate=pl.CostEstimate(flops=0, bytes_accessed=2**27, transcendentals=0),
        name="closing",
    )(*operands)


def head_lanes(head):
    return slice(head * HEAD_DIM, (head + 1) * HEAD_DIM)


def attention_forward_kernel(query, key, value, first, attended, heads_out, log_total):
    tile = pl.program_id(0)
    rows, width = query.shape
    heads = range(width // HEAD_DIM)
    first_key = first[...]
    row_index = lax.broadcasted_iota(jnp.int32, (rows, rows), 0)
    column_index = lax.broadcasted_iota(jnp.int32, (rows, rows), 1)

    def block(index, carry, diagonal):
        at = pl.ds(pl.multiple_of(index * rows, rows), rows)
        visible = column_index + index * rows >= first_key
        if diagonal:
            visible = visible & (column_index <= row_index)
        result = []
        for head in heads:
            lane = head_lanes(head)
            largest, total, summed = carry[head]
            scores = contract_cols(query[:, lane], key[at, lane])
            scores = jnp.where(visible, scores, masked_score)
            new_largest = jnp.maximum(largest, jnp.max(scores, axis=1, keepdims=True))
            weights = jnp.where(visible, jnp.exp(scores - new_largest), 0.0)
            scaling = jnp.exp(largest - new_largest)
            total = total * scaling + jnp.sum(weights, axis=1, keepdims=True)
            summed = summed * scaling + matmul(weights.astype(jnp.bfloat16), value[at, lane])
            result.append((new_largest, total, summed))
        return tuple(result)

    carry = tuple(
        (
            jnp.full((rows, 1), masked_score, jnp.float32),
            jnp.zeros((rows, 1), jnp.float32),
            jnp.zeros((rows, HEAD_DIM), jnp.float32),
        )
        for _ in heads
    )
    carry = lax.fori_loop(0, tile, lambda index, kept: block(index, kept, False), carry)
    carry = block(tile, carry, True)
    for head in heads:
        largest, total, summed = carry[head]
        summed = summed / total
        attended[:, head_lanes(head)] = summed
        heads_out[:, head_lanes(head)] = summed.astype(jnp.bfloat16)
        log_total[head, :, :] = jnp.broadcast_to(
            jnp.transpose(largest + jnp.log(total)), log_total.shape[1:]
        )


def attention_forward(query, key, value, first_key, tile_rows):
    length, width = query.shape
    heads = width // HEAD_DIM
    part = pl.BlockSpec((tile_rows, width), lambda tile: (tile, 0))
    return pl.pallas_call(
        attention_forward_kernel,
        grid=(length // tile_rows,),
        in_specs=[
            part,
            in_spec(key.shape),
            in_spec(value.shape),
            pl.BlockSpec((tile_rows, 1), lambda tile: (tile, 0)),
        ],
        out_specs=[
            part,
            part,
            pl.BlockSpec((heads, 8, tile_rows), lambda tile: (0, 0, tile)),
        ],
        out_shape=[
            jax.ShapeDtypeStruct((length, width), jnp.float32),
            jax.ShapeDtypeStruct((length, width), jnp.bfloat16),
            jax.ShapeDtypeStruct((heads, 8, length), jnp.float32),
        ],
        compiler_params=pltpu.CompilerParams(vmem_limit_bytes=60 * 1024 * 1024),
        cost_estimate=pl.CostEstimate(
            flops=2 * length * length * width,
            bytes_accessed=10 * length * width,
            transcendentals=length * length * heads // 2,
        ),
        name="attention_forward",
    )(query, key, value, first_key)


def project(all_tokens, units, head_width, cosine, sine_table):
    bf16, f32 = jnp.bfloat16, jnp.float32
    length, model_width = all_tokens.shape
    planes, height, strip = units.shape
    rows = 512

    def kernel(tokens, weight, gains, cos, sin, normed, query, key, value):
        values = tokens[...].astype(f32)
        low = (values * rms_scale(values) * gain_row(gains, 0)).astype(bf16)
        normed[...] = low

        def turn(part):
            return part * cos[...] + pltpu.roll(part, HEAD_DIM // 2, 1) * sin[...]

        def projection(start):
            return by_planes(low, weight, start, head_width)

        query_proj = projection(0)
        key_proj = projection(head_width)
        for head in range(head_width // HEAD_DIM):
            at = slice(head * HEAD_DIM, (head + 1) * HEAD_DIM)
            query[:, at] = (turn(query_proj[:, at]) * HEAD_DIM ** (-0.5)).astype(bf16)
            key[:, at] = turn(key_proj[:, at]).astype(bf16)
        value[...] = projection(2 * head_width).astype(bf16)

    def tile(width):
        return pl.BlockSpec((rows, width), lambda step: (step, 0))

    gain_block = height // 16 - 1
    shape = jax.ShapeDtypeStruct
    return pl.pallas_call(
        kernel,
        grid=(length // rows,),
        in_specs=[
            tile(model_width),
            pl.BlockSpec((planes, 3 * head_width, strip), lambda step: (0, 0, 0)),
            pl.BlockSpec((planes, 16, strip), lambda step: (0, gain_block, 0)),
            tile(HEAD_DIM),
            tile(HEAD_DIM),
        ],
        out_specs=[tile(model_width)] + [tile(head_width)] * 3,
        out_shape=[shape((length, model_width), bf16)] + [shape((length, head_width), bf16)] * 3,
        compiler_params=pltpu.CompilerParams(vmem_limit_bytes=60 * 1024 * 1024),
        cost_estimate=pl.CostEstimate(
            flops=6 * length * head_width * model_width,
            bytes_accessed=4 * length * model_width,
            transcendentals=0,
        ),
        name="project",
    )(all_tokens, units, units, cosine, sine_table)


def gain_row(gains, index):
    return jnp.concatenate(
        [gains[plane, index : index + 1, :] for plane in range(gains.shape[0])], axis=1
    ).astype(jnp.float32)


def by_planes(rows, units, start, height):
    strip = units.shape[2]
    total = contract_cols(rows[:, :strip], units[0, start : start + height, :])
    for plane in range(1, units.shape[0]):
        total = total + contract_cols(
            rows[:, plane * strip : (plane + 1) * strip], units[plane, start : start + height, :]
        )
    return total


def hidden_forward(normed_ffn, units, hidden):
    bf16, f32 = jnp.bfloat16, jnp.float32
    length, model_width = normed_ffn.shape
    rows = 256

    def kernel(normed, weights, mixed, gate_factor, up_factor):
        low = normed[...]
        gate_proj = by_planes(low, weights, 0, hidden)
        up_proj = by_planes(low, weights, hidden, hidden)
        sigmoid = 1.0 / (1.0 + jnp.exp(-gate_proj))
        silu = gate_proj * sigmoid
        up_factor[...] = silu
        gate_factor[...] = up_proj * sigmoid * (1.0 + gate_proj * (1.0 - sigmoid))
        mixed[...] = (silu * up_proj).astype(bf16)

    def tile(width):
        return pl.BlockSpec((rows, width), lambda step: (step, 0))

    shape = jax.ShapeDtypeStruct
    return pl.pallas_call(
        kernel,
        grid=(length // rows,),
        in_specs=[tile(model_width), in_spec(units.shape)],
        out_specs=[tile(hidden)] * 3,
        out_shape=[shape((length, hidden), bf16)] + [shape((length, hidden), f32)] * 2,
        compiler_params=pltpu.CompilerParams(vmem_limit_bytes=60 * 1024 * 1024),
        cost_estimate=pl.CostEstimate(
            flops=4 * length * hidden * model_width,
            bytes_accessed=4 * length * model_width,
            transcendentals=length * hidden,
        ),
        name="hidden_forward",
    )(normed_ffn, units)


def hidden_backward(gate_factor, up_factor, all_cotangent, units, hidden):
    bf16 = jnp.bfloat16
    length, model_width = all_cotangent.shape
    rows = 512

    def kernel(gate_ref, up_ref, cotangent, weights, grad_pair):
        grad_mixed = by_planes(cotangent[...], weights, 0, hidden)
        grad_gate, grad_up = grad_mixed * gate_ref[...], grad_mixed * up_ref[...]
        grad_pair[...] = jnp.concatenate([grad_gate, grad_up], axis=1).astype(bf16)

    def tile(width):
        return pl.BlockSpec((rows, width), lambda step: (step, 0))

    shape = jax.ShapeDtypeStruct
    return pl.pallas_call(
        kernel,
        grid=(length // rows,),
        in_specs=[tile(hidden), tile(hidden), tile(model_width), in_spec(units.shape)],
        out_specs=tile(2 * hidden),
        out_shape=shape((length, 2 * hidden), bf16),
        compiler_params=pltpu.CompilerParams(vmem_limit_bytes=60 * 1024 * 1024),
        cost_estimate=pl.CostEstimate(
            flops=2 * length * hidden * model_width,
            bytes_accessed=4 * length * model_width,
            transcendentals=length * hidden,
        ),
        name="hidden_backward",
    )(gate_factor, up_factor, all_cotangent, units)


def attention_backward_kernel(guests, *refs):
    count = len(guests)
    query, key, value, branch, weight, attended, log_total, first, cos, sin = refs[:10]
    grads, key_sum, value_sum = refs[10 + count], refs[11 + 2 * count], refs[12 + 2 * count]
    guest_scratch = refs[13 + 2 * count :]
    for number, guest in enumerate(guests):
        guest.bind(
            refs[10 + number], refs[11 + count + number], *guest_scratch[3 * number : 3 * number + 3]
        )
    tile = pl.program_id(0)

    @pl.when(tile == 0)
    def _():
        signal_and_wait(square_peers())
        for guest in guests:
            guest.begin()

    rows, width = query.shape
    heads = range(width // HEAD_DIM)
    grad_tiles = by_planes(branch[...], weight, 0, width)
    grad_low = grad_tiles.astype(jnp.bfloat16)
    product = grad_low.astype(jnp.float32) * attended[...]
    centre_rows = [
        jnp.transpose(jnp.sum(product[:, head_lanes(head)], axis=1, keepdims=True))
        for head in heads
    ]
    first_row = first[:1, :]
    key_index = lax.broadcasted_iota(jnp.int32, (rows, rows), 0)
    query_index = lax.broadcasted_iota(jnp.int32, (rows, rows), 1)

    def block(index, carry, diagonal):
        at = pl.ds(pl.multiple_of(index * rows, rows), rows)
        visible = key_index + index * rows >= first_row
        if diagonal:
            visible = visible & (key_index <= query_index)
        result = []
        for head in heads:
            lane = head_lanes(head)
            query_tile, grad_tile = query[:, lane], grad_low[:, lane]
            key_block = key[at, lane]
            scores = contract_cols(key_block, query_tile)
            probability = jnp.where(visible, jnp.exp(scores - log_total[head, :1, :]), 0.0)
            grad_prob = contract_cols(value[at, lane], grad_tile)
            grad_scores = (probability * (grad_prob - centre_rows[head])).astype(jnp.bfloat16)
            key_part = matmul(grad_scores, query_tile)
            value_part = matmul(probability.astype(jnp.bfloat16), grad_tile)
            if diagonal:
                key_sum[at, lane] = key_part
                value_sum[at, lane] = value_part
            else:
                key_sum[at, lane] += key_part
                value_sum[at, lane] += value_part
            result.append(carry[head] + contract_rows(grad_scores, key_block))
        return tuple(result)

    def turn_back(part, at):
        return part * cos[at, :] - pltpu.roll(part, HEAD_DIM // 2, 1) * sin[at, :]

    carry = tuple(jnp.zeros((rows, HEAD_DIM), jnp.float32) for _ in heads)
    carry = lax.fori_loop(0, tile, lambda index, kept: block(index, kept, False), carry)
    carry = block(tile, carry, True)
    here = pl.ds(pl.multiple_of(tile * rows, rows), rows)
    for head in heads:
        grads[0, here, head_lanes(head)] = (
            turn_back(carry[head], here) * HEAD_DIM ** (-0.5)
        ).astype(jnp.bfloat16)

    @pl.when(tile == pl.num_programs(0) - 1)
    def _():
        @pl.loop(0, pl.num_programs(0))
        def _(index):
            at = pl.ds(pl.multiple_of(index * rows, rows), rows)
            for head in heads:
                lane = head_lanes(head)
                grads[1, at, lane] = turn_back(key_sum[at, lane], at).astype(jnp.bfloat16)
                grads[2, at, lane] = value_sum[at, lane].astype(jnp.bfloat16)

        for guest in guests:
            guest.end()


def attention_backward(
    query,
    key,
    value,
    grad_branch,
    units,
    attended,
    log_total,
    first_key,
    cosine,
    sine_table,
    tile_rows,
    summed,
):
    guests = [SquareReturn(grad) for grad in summed]
    length, width = query.shape
    model_width = grad_branch.shape[1]
    heads = width // HEAD_DIM
    part = pl.BlockSpec((tile_rows, width), lambda tile: (tile, 0))
    shape = jax.ShapeDtypeStruct((3, length, width), jnp.bfloat16)
    return pl.pallas_call(
        functools.partial(attention_backward_kernel, guests),
        grid=(length // tile_rows,),
        in_specs=[
            part,
            in_spec(key.shape),
            in_spec(value.shape),
            pl.BlockSpec((tile_rows, model_width), lambda tile: (tile, 0)),
            pl.BlockSpec((units.shape[0], width, units.shape[2]), lambda tile: (0, 3, 0)),
            part,
            pl.BlockSpec((heads, 8, tile_rows), lambda tile: (0, 0, tile)),
            pl.BlockSpec((8, tile_rows), lambda tile: (0, tile)),
            in_spec(cosine.shape),
            in_spec(sine_table.shape),
        ]
        + [in_spec(grad.shape) for grad in summed],
        out_specs=[in_spec((3, length, width))]
        + [pl.BlockSpec(memory_space=pl.ANY)] * len(guests),
        out_shape=[shape] + [guest.shape for guest in guests],
        scratch_shapes=[
            pltpu.VMEM((length, width), jnp.float32),
            pltpu.VMEM((length, width), jnp.float32),
        ]
        + [sems for guest in guests for sems in guest.scratch],
        compiler_params=pltpu.CompilerParams(
            collective_id=6, has_side_effects=True, vmem_limit_bytes=60 * 1024 * 1024
        ),
        cost_estimate=pl.CostEstimate(
            flops=5 * length * length * width + 2 * length * width * model_width,
            bytes_accessed=24 * length * width,
            transcendentals=length * length * heads // 2,
        ),
        name="attention_backward",
    )(
        query,
        key,
        value,
        grad_branch,
        units,
        attended,
        log_total,
        first_key,
        cosine,
        sine_table,
        *summed,
    )


def group_device(
    tokens,
    doc_starts,
    query_weight,
    key_weight,
    value_weight,
    out_weight,
    gate_weight,
    up_weight,
    down_weight,
    attention_gain,
    feedforward_gain,
    cotangent,
):
    bf16, f32 = jnp.bfloat16, jnp.float32
    x_at, z_at, core = (lax.axis_index(name) for name in ("x", "z", "c"))
    _, shard_rows, model_width = tokens.shape
    slice_width = query_weight.shape[0]
    half_rows = shard_rows // 2
    length = 2 * MEMBERS * half_rows
    planes = lax.axis_size("z")
    strip = model_width // planes
    head_width = query_weight.shape[1] // QUARTERS
    hidden = gate_weight.shape[1] // QUARTERS

    def keep_naturally(kept, half, at, values):
        part = strip // 2
        for x in range(2):
            for plane in range(planes):
                start = plane * strip + x * part
                place = x * planes * part + plane * part
                kept[half, at, place : place + part] = values[:, start : start + part]

    def units_of(weight):
        return weight.reshape(QUARTERS, -1, slice_width)

    def far_sum(grads):
        return lax.psum_scatter(grads.astype(bf16), "z", scatter_dimension=1, tiled=True)

    gains = jnp.concatenate(
        [attention_gain[None], feedforward_gain[None], jnp.zeros((14, slice_width), bf16)]
    )
    gains = jnp.broadcast_to(gains[None], (QUARTERS, 16, slice_width))
    docs = jnp.zeros((8, 128), jnp.int32).at[:2, : doc_starts.shape[1]].set(doc_starts)
    own_tokens, own_cotangent, other_docs, attention_square, pair_square, down_square = deal(
        tokens,
        cotangent,
        [
            jnp.concatenate(
                [
                    units_of(query_weight.T),
                    units_of(key_weight.T),
                    units_of(value_weight.T),
                    units_of(out_weight),
                    gains,
                ],
                axis=1,
            ),
            jnp.concatenate([units_of(gate_weight.T), units_of(up_weight.T)], axis=1),
            units_of(down_weight),
        ],
        docs,
    )
    attention_units = lax.all_gather(attention_square, "z")
    all_tokens, all_cotangent = gather_rows(own_tokens, own_cotangent)
    pair_square, _ = lax.optimization_barrier((pair_square, all_tokens))
    pair_units = lax.all_gather(pair_square, "z")

    positions = jnp.arange(length, dtype=jnp.int32)
    cosine, sine_table = turning_tables(length)
    docs = jnp.where(plane_x(z_at) == x_at, docs, other_docs)
    starts = lax.dynamic_index_in_dim(docs, z_at // 2, 0, keepdims=False)[: doc_starts.shape[1]]
    first_key = jnp.max(
        jnp.where(starts[None, :] <= positions[:, None], starts[None, :], 0), axis=1
    )
    normed, query_rot, key_rot, value_low = project(
        all_tokens, attention_units, head_width, cosine, sine_table
    )
    down_square, _ = lax.optimization_barrier((down_square, query_rot))
    down_units = lax.all_gather(down_square, "z")
    tile_rows = min(512, length)
    attended, heads_out, log_total = attention_forward(
        query_rot, key_rot, value_low, first_key[:, None], tile_rows
    )
    gains_at = (attention_units, 16, attention_units.shape[1] // 16 - 1)

    def after_attention(total, half, at, states, kept, own):
        token_ref, gain_ref = states
        residual = token_ref[half, at, :].astype(f32) + total
        kept[half, at, :] = residual
        own[half, at, :] = (residual * rms_scale(residual) * gain_row(gain_ref, 1)).astype(bf16)

    residual, normed_ffn = exchange(
        "branch_exchange",
        2,
        [
            dict(
                lefts=[heads_out],
                rights=[(attention_units, head_width, 3)],
                states=[(own_tokens, None, 0), gains_at],
                finish=after_attention,
                kept=f32,
                gathers=True,
            )
        ],
        ("x", "y"),
    )
    mixed_hidden, gate_factor, up_factor = hidden_forward(normed_ffn, pair_units, hidden)
    grad_down_all = contract_rows(mixed_hidden, all_cotangent)
    grad_pair_low = hidden_backward(
        gate_factor, up_factor, all_cotangent, down_units, hidden
    )
    grad_down = far_sum(grad_down_all)
    grad_pair_all = contract_rows(grad_pair_low, normed_ffn).astype(bf16)
    grad_pair_low, grad_pair_all = lax.optimization_barrier((grad_pair_low, grad_pair_all))
    grad_pair = far_sum(grad_pair_all)

    def after_feedforward(total, half, at, states, kept, own):
        residual_ref, cotangent_ref, gain_ref = states
        rows = residual_ref[half, at, :]
        scale = rms_scale(rows)
        weighted = total * gain_row(gain_ref, 1)
        mean = jnp.mean(weighted * rows, axis=-1, keepdims=True)
        grad = cotangent_ref[half, at, :].astype(f32) + scale * weighted - rows * scale**3 * mean
        kept[half, at, :] = grad
        own[half, at, :] = grad.astype(bf16)

    grad_residual, grad_branch = exchange(
        "feedforward_exchange",
        3,
        [
            dict(
                lefts=[grad_pair_low],
                rights=[(pair_units, 2 * hidden, 0)],
                states=[(residual, None, 0), (own_cotangent, None, 0), gains_at],
                finish=after_feedforward,
                kept=f32,
                gathers=True,
            )
        ],
        ("x", "y"),
    )
    grad_out = contract_rows(heads_out, grad_branch).astype(bf16)
    grad_qkv, spread_down = attention_backward(
        query_rot,
        key_rot,
        value_low,
        grad_branch,
        attention_units,
        attended,
        log_total,
        jnp.broadcast_to(first_key[None], (8, length)),
        cosine,
        sine_table,
        tile_rows,
        [grad_down],
    )
    grad_projections = lax.dot_general(
        grad_qkv, normed, (((1,), (0,)), ((), ())), preferred_element_type=f32
    ).reshape(3 * head_width, model_width)
    grad_attention = jnp.concatenate([grad_projections.astype(bf16), grad_out])
    grad_attention, grad_pair = lax.optimization_barrier((grad_attention, grad_pair))
    grad_attention = far_sum(grad_attention)

    def after_hidden(total, half, at, states, kept, own):
        keep_naturally(kept, half, at, (states[0][half, at, :] + total).astype(bf16))

    def after_all(total, half, at, states, kept, own):
        token_ref, grad_ref, gain_ref = states
        rows = token_ref[half, at, :].astype(f32)
        scale = rms_scale(rows)
        weighted = total * gain_row(gain_ref, 0)
        mean = jnp.mean(weighted * rows, axis=-1, keepdims=True)
        grad = grad_ref[half, at, :] + scale * weighted - rows * scale**3 * mean
        keep_naturally(kept, half, at, grad.astype(bf16))

    _, own_output, got_tokens, spread_gate = exchange(
        "token_exchange",
        4,
        [
            dict(
                lefts=[(grad_qkv, at) for at in range(3)],
                rights=[(attention_units, head_width, at) for at in range(3)],
                states=[(own_tokens, None, 0), (grad_residual, None, 0), gains_at],
                finish=after_all,
                kept=bf16,
                gathers=False,
                hands=True,
            ),
            dict(
                lefts=[mixed_hidden],
                rights=[(down_units, hidden, 0)],
                states=[(residual, None, 0)],
                finish=after_hidden,
                kept=bf16,
                gathers=False,
            ),
        ],
        ("x", "y"),
        [(grad_pair, 0, hidden)],
    )
    spread_up, spread_attention, output, grad_tokens = closing(
        [(grad_pair, hidden, hidden), (grad_attention,)], own_output, got_tokens
    )

    def columns(grads):
        return grads.reshape(-1, slice_width).astype(f32)

    grad_down_w, grad_gate_w, grad_up_w = (
        columns(grads)
        for grads in (spread_down, spread_gate, spread_up)
    )
    grad_gate_w, grad_up_w = grad_gate_w.T, grad_up_w.T
    grad_query_w, grad_key_w, grad_value_w, grad_out_w = (
        columns(spread_attention[:, at * head_width : (at + 1) * head_width]) for at in range(4)
    )
    grad_query_w, grad_key_w, grad_value_w = grad_query_w.T, grad_key_w.T, grad_value_w.T

    def gain_sum(*pairs):
        return sum(jnp.sum(weight.astype(f32) * grad, axis=1) for weight, grad in pairs)

    sums = jnp.stack(
        [
            gain_sum(
                (query_weight, grad_query_w), (key_weight, grad_key_w), (value_weight, grad_value_w)
            ),
            gain_sum((gate_weight, grad_gate_w), (up_weight, grad_up_w)),
        ]
    )
    sums = sums + swap(sums, "c")
    return (
        output,
        grad_tokens,
        grad_query_w,
        grad_key_w,
        grad_value_w,
        grad_out_w,
        grad_gate_w,
        grad_up_w,
        grad_down_w,
        sums[0] / attention_gain.astype(f32),
        sums[1] / feedforward_gain.astype(f32),
    )


def placements(stream, seq, head):
    both = (stream + seq) if isinstance(stream, tuple) else (stream, seq)
    in_specs = (
        P(stream, seq, None),
        P(stream, None),
        P(both, head),
        P(both, head),
        P(both, head),
        P(head, both),
        P(both, head),
        P(both, head),
        P(head, both),
        P(both),
        P(both),
        P(stream, seq, None),
    )
    out_specs = (
        P(stream, seq, None),
        P(stream, seq, None),
        P(both, head),
        P(both, head),
        P(both, head),
        P(head, both),
        P(both, head),
        P(both, head),
        P(head, both),
        P(both),
        P(both),
    )
    return in_specs, out_specs


def solution(mesh):
    def run(*arguments):
        tokens, doc_starts = arguments[:2]
        sizes = dict(mesh.shape)
        grouped = (
            (sizes["stream"], sizes["seq"], sizes["head"]) == (2, 8, 2)
            and tokens.shape[0] == 4
            and tokens.shape[1] <= WIN
        )
        if grouped:
            split = Mesh(mesh.devices.reshape(2, 4, 2, 2), ("x", "z", "y", "c"))
            in_specs, out_specs = placements(("x",), ("z", "y"), "c")
            step = group_device
        else:
            split = mesh
            in_specs, out_specs = placements("stream", "seq", "head")
            step = per_device
        return jax.shard_map(
            step, mesh=split, in_specs=in_specs, out_specs=out_specs, check_vma=False
        )(*arguments)

    return run
```

```python
import functools
import math

import jax
import jax.numpy as jnp
import numpy as np
from jax import lax
from jax.experimental import pallas as pl
from jax.experimental.pallas import tpu as pltpu
from jax.sharding import Mesh
from jax.sharding import PartitionSpec as P

HEAD_DIM = 128
WIN = 2048


epsilon = 1e-06
masked_score = -1e30


def from_behind(value, axis, steps):
    count = lax.axis_size(axis)
    initial, last = (max(0, -steps), min(count, count - steps))
    return lax.ppermute(value, axis, [(source, source + steps) for source in range(initial, last)])


def matmul(left, right):
    return jnp.dot(left, right, preferred_element_type=jnp.float32)


def contract_rows(left, right):
    return lax.dot_general(
        left, right, (((0,), (0,)), ((), ())), preferred_element_type=jnp.float32
    )


def contract_cols(left, right):
    return lax.dot_general(
        left, right, (((1,), (1,)), ((), ())), preferred_element_type=jnp.float32
    )


def rotary_tables(positions):
    half_dim = HEAD_DIM // 2
    frequency = jnp.exp(
        jnp.arange(half_dim).astype(jnp.float32) * (-2.0 * math.log(10000.0) / HEAD_DIM)
    )
    angles = positions.astype(jnp.float32)[:, None] * frequency[None, :]
    return (jnp.cos(angles), jnp.sin(angles))


def rotate_pairs(values, cosine, sine_table):
    half_dim = values.shape[-1] // 2
    first_half = values[..., :half_dim]
    second_half = values[..., half_dim:]
    return jnp.concatenate(
        [
            first_half * cosine - second_half * sine_table,
            second_half * cosine + first_half * sine_table,
        ],
        axis=-1,
    )


def unrotate_pairs(values, cosine, sine_table):
    half_dim = values.shape[-1] // 2
    first_half = values[..., :half_dim]
    second_half = values[..., half_dim:]
    return jnp.concatenate(
        [
            first_half * cosine + second_half * sine_table,
            second_half * cosine - first_half * sine_table,
        ],
        axis=-1,
    )


def document_number(starts, positions):
    return jnp.sum((starts[:, None, :] <= positions[None, :, None]).astype(jnp.int32), axis=2)


def rms_scale(values):
    return lax.rsqrt(jnp.mean(values * values, axis=-1, keepdims=True) + epsilon)


def norm_backward(grad_normed, inputs, row_scale, gain_vector):
    gain_grad = jnp.sum(grad_normed * inputs * row_scale, axis=0)
    weighted = grad_normed * gain_vector
    grad_inputs = row_scale * weighted - inputs * row_scale**3 * jnp.mean(
        weighted * inputs, axis=-1, keepdims=True
    )
    return (grad_inputs, gain_grad)


def per_device(
    tokens,
    doc_starts,
    query_weight,
    key_weight,
    value_weight,
    out_weight,
    gate_weight,
    up_weight,
    down_weight,
    attention_gain,
    feedforward_gain,
    cotangent,
):
    gathered = (
        lax.all_gather(query_weight, ("stream", "seq"), axis=0, tiled=True),
        lax.all_gather(key_weight, ("stream", "seq"), axis=0, tiled=True),
        lax.all_gather(value_weight, ("stream", "seq"), axis=0, tiled=True),
        lax.all_gather(out_weight, ("stream", "seq"), axis=1, tiled=True),
        lax.all_gather(gate_weight, ("stream", "seq"), axis=0, tiled=True),
        lax.all_gather(up_weight, ("stream", "seq"), axis=0, tiled=True),
        lax.all_gather(down_weight, ("stream", "seq"), axis=1, tiled=True),
        lax.all_gather(attention_gain, ("stream", "seq"), axis=0, tiled=True),
        lax.all_gather(feedforward_gain, ("stream", "seq"), axis=0, tiled=True),
    )
    (
        full_query,
        full_key,
        full_value,
        full_out,
        full_gate,
        full_up,
        full_down,
        full_gain_first,
        full_gain_second,
    ) = gathered
    streams, shard_rows, model_width = tokens.shape
    head_width = full_query.shape[1]
    local_heads = head_width // HEAD_DIM
    flat_rows = streams * shard_rows
    seq_index = lax.axis_index("seq")
    halo_shards = min(WIN // shard_rows, lax.axis_size("seq") - 1)
    window_rows = (halo_shards + 1) * shard_rows
    inputs = tokens.reshape(flat_rows, model_width).astype(jnp.float32)
    scale_first = rms_scale(inputs)
    gain_first = full_gain_first.astype(jnp.float32)
    normed = (inputs * scale_first * gain_first).astype(jnp.bfloat16)
    query_proj = matmul(normed, full_query).reshape(streams, shard_rows, local_heads, HEAD_DIM)
    key_proj = matmul(normed, full_key).reshape(streams, shard_rows, local_heads, HEAD_DIM)
    value_low = (
        matmul(normed, full_value).astype(jnp.bfloat16).reshape(streams, shard_rows, head_width)
    )
    positions = seq_index * shard_rows + jnp.arange(shard_rows, dtype=jnp.int32)
    cosine, sine_table = rotary_tables(positions)
    cosine = cosine[None, :, None, :]
    sine_table = sine_table[None, :, None, :]
    query_rot = (rotate_pairs(query_proj, cosine, sine_table) * HEAD_DIM ** (-0.5)).astype(
        jnp.bfloat16
    )
    key_rot = rotate_pairs(key_proj, cosine, sine_table).astype(jnp.bfloat16)
    paired = jnp.stack([key_rot.reshape(streams, shard_rows, head_width), value_low])
    pieces = []
    for distance in range(halo_shards, 0, -1):
        pieces.append(from_behind(paired, "seq", distance))
    window = jnp.concatenate(pieces + [paired], axis=2)
    key_positions = (seq_index - halo_shards) * shard_rows + jnp.arange(
        window_rows, dtype=jnp.int32
    )
    query_docs = document_number(doc_starts, positions)
    key_docs = document_number(doc_starts, key_positions)
    offsets = positions[:, None] - key_positions[None, :]
    allowed = ((offsets >= 0) & (offsets < WIN))[None] & (
        query_docs[:, :, None] == key_docs[:, None, :]
    )
    query_heads = jnp.transpose(query_rot, (2, 0, 1, 3))
    key_heads = jnp.transpose(
        window[0].reshape(streams, window_rows, local_heads, HEAD_DIM), (2, 0, 1, 3)
    )
    value_heads = jnp.transpose(
        window[1].reshape(streams, window_rows, local_heads, HEAD_DIM), (2, 0, 1, 3)
    )

    def head_forward(operands):
        query_one, key_one, value_one = operands
        scores = jnp.einsum("sqe,ske->sqk", query_one, key_one, preferred_element_type=jnp.float32)
        scores = jnp.where(allowed, scores, masked_score)
        largest = jnp.max(scores, axis=-1, keepdims=True)
        weights = jnp.exp(scores - largest)
        totals = jnp.sum(weights, axis=-1, keepdims=True)
        probability = (weights / totals).astype(jnp.bfloat16)
        attended = jnp.einsum(
            "sqk,ske->sqe", probability, value_one, preferred_element_type=jnp.float32
        )
        return (attended, (largest + jnp.log(totals))[..., 0])

    attended, log_totals = lax.map(head_forward, (query_heads, key_heads, value_heads))
    heads_out = (
        jnp.transpose(attended, (1, 2, 0, 3)).reshape(flat_rows, head_width).astype(jnp.bfloat16)
    )
    attention_sum = lax.psum(matmul(heads_out, full_out), "head")
    residual = inputs + attention_sum
    scale_second = rms_scale(residual)
    gain_second = full_gain_second.astype(jnp.float32)
    normed_ffn = (residual * scale_second * gain_second).astype(jnp.bfloat16)
    gate_proj = matmul(normed_ffn, full_gate)
    up_proj = matmul(normed_ffn, full_up)
    sigmoid_gate = jax.nn.sigmoid(gate_proj)
    silu_gate = gate_proj * sigmoid_gate
    mixed_hidden = (silu_gate * up_proj).astype(jnp.bfloat16)
    feedforward_sum = lax.psum(matmul(mixed_hidden, full_down).astype(jnp.bfloat16), "head").astype(
        jnp.float32
    )
    output = (
        (residual + feedforward_sum).astype(jnp.bfloat16).reshape(streams, shard_rows, model_width)
    )
    gathered = (
        lax.all_gather(query_weight, ("stream", "seq"), axis=0, tiled=True),
        lax.all_gather(key_weight, ("stream", "seq"), axis=0, tiled=True),
        lax.all_gather(value_weight, ("stream", "seq"), axis=0, tiled=True),
        lax.all_gather(out_weight, ("stream", "seq"), axis=1, tiled=True),
        lax.all_gather(gate_weight, ("stream", "seq"), axis=0, tiled=True),
        lax.all_gather(up_weight, ("stream", "seq"), axis=0, tiled=True),
        lax.all_gather(down_weight, ("stream", "seq"), axis=1, tiled=True),
        lax.all_gather(attention_gain, ("stream", "seq"), axis=0, tiled=True),
        lax.all_gather(feedforward_gain, ("stream", "seq"), axis=0, tiled=True),
    )
    (
        full_query,
        full_key,
        full_value,
        full_out,
        full_gate,
        full_up,
        full_down,
        full_gain_first,
        full_gain_second,
    ) = gathered
    grad_output = cotangent.reshape(flat_rows, model_width)
    grad_down = contract_rows(mixed_hidden, grad_output)
    grad_mixed = contract_cols(grad_output, full_down)
    grad_gate_low = (
        grad_mixed * up_proj * sigmoid_gate * (1.0 + gate_proj * (1.0 - sigmoid_gate))
    ).astype(jnp.bfloat16)
    grad_up_low = (grad_mixed * silu_gate).astype(jnp.bfloat16)
    grad_gate_w = contract_rows(normed_ffn, grad_gate_low)
    grad_up_w = contract_rows(normed_ffn, grad_up_low)
    grad_normed_ffn = lax.psum(
        contract_cols(grad_gate_low, full_gate) + contract_cols(grad_up_low, full_up), "head"
    )
    grad_residual_norm, grad_gain_second = norm_backward(
        grad_normed_ffn, residual, scale_second, gain_second
    )
    grad_residual = grad_output.astype(jnp.float32) + grad_residual_norm
    grad_branch = grad_residual.astype(jnp.bfloat16)
    grad_out_w = contract_rows(heads_out, grad_branch)
    grad_heads = contract_cols(grad_branch, full_out).astype(jnp.bfloat16)
    grad_heads_major = jnp.transpose(
        grad_heads.reshape(streams, shard_rows, local_heads, HEAD_DIM), (2, 0, 1, 3)
    )

    def head_backward(operands):
        query_one, key_one, value_one, grad_one, log_one = operands
        scores = jnp.einsum("sqe,ske->sqk", query_one, key_one, preferred_element_type=jnp.float32)
        scores = jnp.where(allowed, scores, masked_score)
        probability = jnp.exp(scores - log_one[..., None])
        grad_prob = jnp.einsum(
            "sqe,ske->sqk", grad_one, value_one, preferred_element_type=jnp.float32
        )
        centre = jnp.sum(probability * grad_prob, axis=-1, keepdims=True)
        grad_scores = (probability * (grad_prob - centre)).astype(jnp.bfloat16)
        grad_query_one = jnp.einsum(
            "sqk,ske->sqe", grad_scores, key_one, preferred_element_type=jnp.float32
        )
        grad_key_one = jnp.einsum(
            "sqk,sqe->ske", grad_scores, query_one, preferred_element_type=jnp.float32
        )
        grad_value_one = jnp.einsum(
            "sqk,sqe->ske",
            probability.astype(jnp.bfloat16),
            grad_one,
            preferred_element_type=jnp.float32,
        )
        return (grad_query_one, grad_key_one, grad_value_one)

    grad_query_heads, grad_key_heads, grad_value_heads = lax.map(
        head_backward, (query_heads, key_heads, value_heads, grad_heads_major, log_totals)
    )
    grad_window = jnp.transpose(
        jnp.stack([grad_key_heads, grad_value_heads]), (0, 2, 3, 1, 4)
    ).reshape(2, streams, window_rows, head_width)
    grad_paired = grad_window[:, :, halo_shards * shard_rows :]
    for distance in range(halo_shards, 0, -1):
        index_piece = halo_shards - distance
        grad_paired = grad_paired + from_behind(
            grad_window[:, :, index_piece * shard_rows : (index_piece + 1) * shard_rows],
            "seq",
            -distance,
        )
    grad_key_rot = grad_paired[0].reshape(streams, shard_rows, local_heads, HEAD_DIM)
    grad_query_rot = jnp.transpose(grad_query_heads, (1, 2, 0, 3))
    grad_query_low = (
        (unrotate_pairs(grad_query_rot, cosine, sine_table) * HEAD_DIM ** (-0.5))
        .reshape(flat_rows, head_width)
        .astype(jnp.bfloat16)
    )
    grad_key_low = (
        unrotate_pairs(grad_key_rot, cosine, sine_table)
        .reshape(flat_rows, head_width)
        .astype(jnp.bfloat16)
    )
    grad_value_low = grad_paired[1].reshape(flat_rows, head_width).astype(jnp.bfloat16)
    grad_query_w = contract_rows(normed, grad_query_low)
    grad_key_w = contract_rows(normed, grad_key_low)
    grad_value_w = contract_rows(normed, grad_value_low)
    grad_normed = lax.psum(
        contract_cols(grad_query_low, full_query)
        + contract_cols(grad_key_low, full_key)
        + contract_cols(grad_value_low, full_value),
        "head",
    )
    grad_inputs_norm, grad_gain_first = norm_backward(grad_normed, inputs, scale_first, gain_first)
    grad_tokens = (grad_residual + grad_inputs_norm).reshape(streams, shard_rows, model_width)
    reduced = (
        lax.psum_scatter(grad_query_w, ("stream", "seq"), scatter_dimension=0, tiled=True),
        lax.psum_scatter(grad_key_w, ("stream", "seq"), scatter_dimension=0, tiled=True),
        lax.psum_scatter(grad_value_w, ("stream", "seq"), scatter_dimension=0, tiled=True),
        lax.psum_scatter(grad_out_w, ("stream", "seq"), scatter_dimension=1, tiled=True),
        lax.psum_scatter(grad_gate_w, ("stream", "seq"), scatter_dimension=0, tiled=True),
        lax.psum_scatter(grad_up_w, ("stream", "seq"), scatter_dimension=0, tiled=True),
        lax.psum_scatter(grad_down, ("stream", "seq"), scatter_dimension=1, tiled=True),
        lax.psum_scatter(grad_gain_first, ("stream", "seq"), scatter_dimension=0, tiled=True),
        lax.psum_scatter(grad_gain_second, ("stream", "seq"), scatter_dimension=0, tiled=True),
    )
    return (
        output,
        grad_tokens,
        reduced[0],
        reduced[1],
        reduced[2],
        reduced[3],
        reduced[4],
        reduced[5],
        reduced[6],
        reduced[7],
        reduced[8],
    )


GROUP = ("x", "y", "c")
MEMBERS = 8
QUARTERS = 4
MESH = pl.DeviceIdType.MESH


def turning_tables(length):
    half_dim = HEAD_DIM // 2
    frequency = np.exp(
        np.arange(half_dim).astype(np.float32) * np.float32(-2.0 * math.log(10000.0) / HEAD_DIM)
    )
    angles = np.arange(length).astype(np.float32)[:, None] * frequency[None, :]
    cosine, sine = np.cos(angles), np.sin(angles)
    return (
        jnp.asarray(np.concatenate([cosine, cosine], axis=1)),
        jnp.asarray(np.concatenate([-sine, sine], axis=1)),
    )


def swap(value, axis):
    return lax.ppermute(value, axis, [(0, 1), (1, 0)])


def remote_copy(source, target, sent, landed, peer):
    return pltpu.make_async_remote_copy(
        source, target, sent, landed, device_id=peer, device_id_type=MESH
    )


def lanes(index, size):
    return pl.ds(pl.multiple_of(index * size, size), size)


def plane_x(plane):
    return (plane + plane // 2) % 2


def plane_of(x, index):
    return x * (1 + index) + (1 - x) * 3 * index


def keeper_x(plane, core):
    return (1 - plane_x(plane) + core) % 2


def source_plane(half, x, core):
    side = (x + core) % 2
    return 2 * half + (side if half else 1 - side)


def slot_of(half, x, y, core):
    side = (x + core) % 2
    return 4 * (side if half else 1 - side) + 2 * y + core


def square_peers():
    x, y = lax.axis_index("x"), lax.axis_index("y")
    return [{"y": 1 - y}, {"x": 1 - x}, {"x": 1 - x, "y": 1 - y}]


def signal_and_wait(peers, others=()):
    barrier = pltpu.get_barrier_semaphore()
    number = len(peers)
    for peer in peers:
        pl.semaphore_signal(barrier, inc=1, device_id=peer, device_id_type=MESH)
    for peer, own in others:
        number = number + jnp.where(own, 0, 1)

        @pl.when(jnp.logical_not(own))
        def _(peer=peer):
            pl.semaphore_signal(barrier, inc=1, device_id=peer, device_id_type=MESH)

    pl.semaphore_wait(barrier, number)


class HandBack:
    def __init__(self, kept, got, out_sems, in_sems, local):
        x, z, core = (lax.axis_index(axis) for axis in ("x", "z", "c"))
        self.stays = (core == 1) & (plane_x(z) == x)
        self.home = z // 2
        targets = [{"x": plane_x(z), "z": source_plane(half, x, core)} for half in range(2)]
        senders = [{"x": keeper_x(z, core), "z": plane_of(x, index)} for index in range(2)]
        self.others = [
            (peer, self.stays & (self.home == number))
            for group in (targets, senders)
            for number, peer in enumerate(group)
        ]
        self.kept, self.got, self.sems = kept, got, (out_sems, in_sems)
        self.targets, self.senders, self.local = targets, senders, local

    def here(self, half):
        return pltpu.make_async_copy(self.kept.at[half], self.got(self.home), self.local)

    def away(self, half):
        out_sems, in_sems = self.sems
        return remote_copy(
            self.kept.at[half],
            self.got(self.home),
            out_sems.at[half],
            in_sems.at[self.home],
            self.targets[half],
        )

    def start(self, half):
        own = self.stays & (self.home == half)

        @pl.when(own)
        def _():
            self.here(half).start()

        @pl.when(jnp.logical_not(own))
        def _():
            self.away(half).start()

    def wait_recv(self, index):
        own = self.stays & (self.home == index)
        out_sems, in_sems = self.sems
        place = self.got(index)

        @pl.when(own)
        def _():
            self.here(index).wait()

        @pl.when(jnp.logical_not(own))
        def _():
            remote_copy(
                place, place, out_sems.at[index], in_sems.at[index], self.senders[index]
            ).wait_recv()

    def wait_send(self):
        for half in range(2):
            own = self.stays & (self.home == half)

            @pl.when(jnp.logical_not(own))
            def _(half=half):
                self.away(half).wait_send()


def in_spec(shape):
    return pl.BlockSpec(shape, lambda *step: (0,) * len(shape), pipeline_mode=pl.Buffered(1))


class SquareSpread:
    def __init__(self, parts):
        _, self.height, self.width = parts.shape
        dma = pltpu.SemaphoreType.DMA
        self.shape = jax.ShapeDtypeStruct((self.height, QUARTERS * self.width), parts.dtype)
        self.scratch = [dma((3,)), dma((3,)), dma(())]

    def bind(self, parts, square, sent, landed, local):
        x, y = lax.axis_index("x"), lax.axis_index("y")
        chip = 2 * x + y
        place = square.at[:, lanes(chip, self.width)]
        others = (chip + 1 - 2 * y, chip + 2 - 4 * x, 3 - chip)
        self.copies = [
            remote_copy(parts.at[other], place, sent.at[index], landed.at[index], peer)
            for index, (peer, other) in enumerate(zip(square_peers(), others))
        ]
        self.copies.append(pltpu.make_async_copy(parts.at[chip], place, local))

    def begin(self):
        for copy in self.copies:
            copy.start()

    def end(self):
        for copy in self.copies:
            copy.wait()


class SquareReturn:
    def __init__(self, grads, start=0, height=None):
        whole_height, width = grads.shape
        self.start, self.height = start, height or whole_height
        self.width = width // QUARTERS
        dma = pltpu.SemaphoreType.DMA
        self.shape = jax.ShapeDtypeStruct((QUARTERS, self.height, self.width), grads.dtype)
        self.scratch = [dma((3,)), dma((3,)), dma(())]

    def bind(self, grads, got, sent, landed, local):
        grads = grads.at[pl.ds(self.start, self.height)]
        x, y = lax.axis_index("x"), lax.axis_index("y")
        chip = 2 * x + y
        others = (chip + 1 - 2 * y, chip + 2 - 4 * x, 3 - chip)
        self.copies = [
            remote_copy(
                grads.at[:, lanes(other, self.width)],
                got.at[chip],
                sent.at[index],
                landed.at[index],
                peer,
            )
            for index, (peer, other) in enumerate(zip(square_peers(), others))
        ]
        here = grads.at[:, lanes(chip, self.width)]
        self.copies.append(pltpu.make_async_copy(here, got.at[chip], local))

    def begin(self):
        for copy in self.copies:
            copy.start()

    def end(self):
        for copy in self.copies:
            copy.wait()


class GroupGather:
    scratch_sizes = (14, 14, 2)

    def __init__(self, own, full, sent, landed, local, to_peer, extra):
        x, y, core = (lax.axis_index(axis) for axis in GROUP)
        self.extra = extra
        self.other = ["x" if axis == "y" else "y" for axis in extra]

        def copy(index, source, half, slot, axis):
            return remote_copy(
                source, full.at[half, slot], sent.at[index], landed.at[index], to_peer[axis]
            )

        def place(half, axis):
            return slot_of(half, 1 - x if axis in ("x", "xy") else x, 1 - y if "y" in axis else y, core)

        def onward(index, half, near, axis):
            slot = place(half, near)
            return copy(index, full.at[half, slot], half, slot, axis)

        halves = range(2)
        me = [slot_of(half, x, y, core) for half in halves]
        self.direct = {
            (axis, half): copy(2 * number + half, own.at[half], half, me[half], axis)
            for number, axis in enumerate(("y", "x"))
            for half in halves
        }
        self.diagonal = [onward(4 + half, half, self.other[half], extra[half]) for half in halves]
        self.shared = [copy(6 + half, own.at[half], half, me[half], "c") for half in halves]
        self.across = [
            onward(8 + 2 * number + half, half, axis, "c")
            for number, axis in enumerate(("y", "x"))
            for half in halves
        ]
        self.last = [onward(12 + half, half, "xy", "c") for half in halves]
        self.here = [
            pltpu.make_async_copy(own.at[half], full.at[half, me[half]], local.at[half])
            for half in halves
        ]

    def start(self, half):
        self.direct[self.other[half], half].start()
        self.direct[self.extra[half], half].start()
        self.shared[half].start()
        self.here[half].start()

    def turn(self, half):
        self.direct[self.other[half], half].wait_recv()
        self.diagonal[half].start()

    def cross(self):
        for half in range(2):
            self.direct[self.extra[half], half].wait_recv()
        for copy in self.across:
            copy.start()

    def end(self):
        for half in range(2):
            self.diagonal[half].wait_recv()
            self.last[half].start()
        for copy in self.shared + self.across + self.last:
            copy.wait_recv()
        for copy in list(self.direct.values()) + self.diagonal + self.shared:
            copy.wait_send()
        for copy in self.across + self.last:
            copy.wait_send()
        for copy in self.here:
            copy.wait()


def deal(tokens, cotangent, parts, docs):
    bf16 = jnp.bfloat16
    _, shard_rows, model_width = tokens.shape
    rows = shard_rows // 2
    guests = [SquareSpread(part) for part in parts]
    part = QUARTERS * parts[0].shape[2] // 2
    planes = model_width // part // 2

    count = len(parts)

    def kernel(tokens_ref, cotangent_ref, docs_ref, *refs):
        part_refs = refs[:count]
        own_first, own_second, other_docs = refs[count : count + 3]
        square_refs = refs[count + 3 : 2 * count + 3]
        row_out, row_in, doc_out, doc_in, staged, here_sems, *scratch = refs[2 * count + 3 :]
        x, z, core = (lax.axis_index(axis) for axis in ("x", "z", "c"))
        home, stays = z // 2, (core == 1) & (plane_x(z) == x)
        targets = [{"x": keeper_x(z, core), "z": plane_of(x, index)} for index in range(2)]
        sources = [{"x": plane_x(z), "z": source_plane(half, x, core)} for half in range(2)]
        square = square_peers()
        others = [
            (peer, stays & (home == number))
            for group in (targets, sources)
            for number, peer in enumerate(group)
        ]
        signal_and_wait(square, others)
        for number, guest in enumerate(guests):
            guest.bind(
                part_refs[number], square_refs[number], *scratch[3 * number : 3 * number + 3]
            )
        guests[0].begin()
        swapped = remote_copy(docs_ref, other_docs, doc_out, doc_in, square[1])
        swapped.start()
        at = pl.ds(pl.multiple_of(core * rows, rows), rows)
        def when_own(number, index, local, away):
            source, own = staged.at[number, index], (own_first, own_second)[number]
            here = pltpu.make_async_copy(source, own.at[home], here_sems.at[number])
            sent = remote_copy(
                source,
                own.at[home],
                row_out.at[2 * number + index],
                row_in.at[2 * number + home],
                targets[index],
            )

            @pl.when(stays & (home == index))
            def _():
                local(here)

            @pl.when(jnp.logical_not(stays & (home == index)))
            def _():
                away(sent)

        for number, source in enumerate((tokens_ref, cotangent_ref)):
            for index in range(2):
                for x_part in range(2):
                    for plane in range(planes):
                        place = (2 * plane + x_part) * part
                        start = (planes * x_part + plane) * part
                        staged[number, index, :, place : place + part] = source[
                            index, at, start : start + part
                        ]
                when_own(number, index, lambda copy: copy.start(), lambda copy: copy.start())
        for guest in guests[1:]:
            guest.begin()
        for guest in guests:
            guest.end()
        swapped.wait()
        for number, own in enumerate((own_first, own_second)):
            for half in range(2):
                slot = 2 * number + half

                @pl.when(jnp.logical_not(stays & (home == half)))
                def _():
                    remote_copy(
                        own.at[half], own.at[half], row_out.at[slot], row_in.at[slot], sources[half]
                    ).wait_recv()

        for number in range(2):
            for index in range(2):
                when_own(number, index, lambda copy: copy.wait(), lambda copy: copy.wait_send())

    inside = pl.BlockSpec(memory_space=pltpu.VMEM)
    anywhere = pl.BlockSpec(memory_space=pl.ANY)
    dma = pltpu.SemaphoreType.DMA
    shape = jax.ShapeDtypeStruct
    return pl.pallas_call(
        kernel,
        in_specs=[inside] * (3 + count),
        out_specs=[inside] * 3 + [anywhere] * count,
        out_shape=[shape((2, rows, model_width), bf16)] * 2
        + [shape(docs.shape, docs.dtype)]
        + [guest.shape for guest in guests],
        scratch_shapes=[
            dma((4,)),
            dma((4,)),
            dma(()),
            dma(()),
            pltpu.VMEM((2, 2, rows, model_width), bf16),
            dma((2,)),
        ]
        + [sems for guest in guests for sems in guest.scratch],
        compiler_params=pltpu.CompilerParams(
            collective_id=0, has_side_effects=True, vmem_limit_bytes=32 * 1024 * 1024
        ),
        cost_estimate=pl.CostEstimate(flops=0, bytes_accessed=2**27, transcendentals=0),
        name="deal",
    )(tokens, cotangent, docs, *parts)


def gather_rows(first, second):
    bf16 = jnp.bfloat16
    _, rows, model_width = first.shape

    def kernel(own_first, own_second, full_first, full_second, *scratch):
        x, y, core = (lax.axis_index(axis) for axis in GROUP)
        to_peer = {"x": {"x": 1 - x}, "y": {"y": 1 - y}, "c": {"c": 1 - core}}
        signal_and_wait([to_peer[axis] for axis in GROUP])
        gathers = [
            GroupGather(own, full, *scratch[3 * number : 3 * number + 3], to_peer, ("x", "y"))
            for number, (own, full) in enumerate(
                ((own_first, full_first), (own_second, full_second))
            )
        ]
        for gather in gathers:
            for half in range(2):
                gather.start(half)
        for gather in gathers:
            for half in range(2):
                gather.turn(half)
            gather.cross()
        for gather in gathers:
            gather.end()

    dma = pltpu.SemaphoreType.DMA
    anywhere = pl.BlockSpec(memory_space=pl.ANY)
    inside = pl.BlockSpec(memory_space=pltpu.VMEM)
    full = jax.ShapeDtypeStruct((2, MEMBERS, rows, model_width), bf16)
    results = pl.pallas_call(
        kernel,
        in_specs=[inside] * 2,
        out_specs=[anywhere] * 2,
        out_shape=[full, full],
        scratch_shapes=[dma((size,)) for size in GroupGather.scratch_sizes] * 2,
        compiler_params=pltpu.CompilerParams(collective_id=1, has_side_effects=True),
        cost_estimate=pl.CostEstimate(flops=0, bytes_accessed=2**28, transcendentals=0),
        name="gather_rows",
    )(first, second)
    return [result.reshape(2 * MEMBERS * rows, model_width) for result in results]


def exchange(name, collective_id, jobs, extra, summed=()):
    bf16, f32 = jnp.bfloat16, jnp.float32
    planes, _, strip = jobs[0]["rights"][0][0].shape
    model_width = planes * strip
    first = jobs[0]["lefts"][0]
    length = first[0].shape[1] if isinstance(first, tuple) else first.shape[0]
    rows = length // (2 * MEMBERS)
    gathers = jobs[-1]["gathers"]
    handing = [job for job in jobs if job.get("hands")]
    guests = [SquareReturn(*grad) for grad in summed]

    def block(shape, index):
        return pl.BlockSpec(shape, lambda step: index, pipeline_mode=pl.Buffered(1))

    def whole(shape):
        return block(shape, (0,) * len(shape))

    anywhere = pl.BlockSpec(memory_space=pl.ANY)
    arrays, in_specs, out_shape, out_specs = [], [], [], []
    for job in jobs:
        for left in job["lefts"]:
            if isinstance(left, tuple):
                left, at = left
                in_specs.append(block((None,) + left.shape[1:], (at, 0, 0)))
            else:
                in_specs.append(whole(left.shape))
            arrays.append(left)
        for array, height, at in job["rights"]:
            arrays.append(array)
            in_specs.append(block((planes, height, strip), (0, at, 0)))
        for array, height, at in job["states"]:
            arrays.append(array)
            in_specs.append(
                whole(array.shape) if height is None else block((planes, height, strip), (0, at, 0))
            )
        out_shape.append(jax.ShapeDtypeStruct((2, rows, model_width), job["kept"]))
        out_specs.append(whole((2, rows, model_width)))
    if gathers:
        out_shape.append(jax.ShapeDtypeStruct((2, MEMBERS, rows, model_width), bf16))
        out_specs.append(anywhere)
    for job in handing:
        out_shape.append(jax.ShapeDtypeStruct((2, rows, model_width), job["kept"]))
        out_specs.append(anywhere)
    for grad, guest in zip(summed, guests):
        arrays.append(grad[0])
        in_specs.append(whole(grad[0].shape))
        out_shape.append(guest.shape)
        out_specs.append(anywhere)
    dma = pltpu.SemaphoreType.DMA
    count = len(jobs)
    scratch = [
        pltpu.VMEM((4, 2, rows, model_width), bf16),
        pltpu.VMEM((4, 2, rows, model_width), bf16),
        pltpu.VMEM((4, 2, rows, model_width), f32),
        pltpu.VMEM((6, rows, model_width), bf16),
        pltpu.VMEM((6, rows, model_width), bf16),
        pltpu.VMEM((2, rows, model_width), bf16),
        dma((4 * count,)),
        dma((4 * count,)),
        dma((6 * count,)),
        dma((6 * count,)),
        dma((2,)),
        dma((2,)),
        dma(()),
        pltpu.SemaphoreType.REGULAR((3,)),
    ]
    for guest in guests:
        scratch += guest.scratch
    scratch += [dma((size,)) for size in GroupGather.scratch_sizes]

    def kernel(*refs):
        refs = list(refs)

        def take(number):
            taken = refs[:number]
            del refs[:number]
            return taken

        job_refs = [
            (take(len(job["lefts"])), take(len(job["rights"])), take(len(job["states"])))
            for job in jobs
        ]
        guest_inputs = take(len(guests))
        kept_refs = take(count)
        full = take(1)[0] if gathers else None
        handed = take(len(handing))
        guest_outputs = take(len(guests))
        (core_send, core_got, sums, link_send, link_got, own) = take(6)
        (core_out, core_in, link_out, link_in, hand_out, hand_in, hand_here, ready) = take(8)
        guest_scratch = [take(3) for _ in guests]
        x, y, core = (lax.axis_index(axis) for axis in GROUP)
        to_peer = {"x": {"x": 1 - x}, "y": {"y": 1 - y}, "c": {"c": 1 - core}}
        peers = [to_peer[axis] for axis in GROUP]
        hands = []
        for number, job in enumerate(jobs):
            if job.get("hands"):
                hands.append(
                    HandBack(
                        kept_refs[number],
                        lambda index: handed[0].at[index],
                        hand_out,
                        hand_in,
                        hand_here,
                    )
                )
        corner = square_peers()[2:] if guests else []
        signal_and_wait(peers + corner, hands[0].others if hands else ())
        for number, guest in enumerate(guests):
            guest.bind(guest_inputs[number], guest_outputs[number], *guest_scratch[number])
            guest.begin()
        gather = GroupGather(own, full, *refs, to_peer, extra) if gathers else None

        chips = ((1 - x, 1 - y), (1 - x, y), (x, 1 - y), (x, y))

        def phases(number):
            left_refs, right_refs, state_refs = job_refs[number]
            finish, kept = jobs[number]["finish"], kept_refs[number]

            def produce(chip, mine):
                at = [
                    half * MEMBERS + slot_of(half, *chips[chip], core if mine else 1 - core)
                    for half in range(2)
                ]
                at = [pl.ds(pl.multiple_of(index * rows, rows), rows) for index in at]
                blocks = [
                    jnp.concatenate([ref[at[0], :], ref[at[1], :]], axis=0) for ref in left_refs
                ]

                @pl.loop(0, planes)
                def _(step):
                    columns = lanes(step, strip)
                    product = matmul(blocks[0], right_refs[0][step])
                    for part, ref in zip(blocks[1:], right_refs[1:]):
                        product = product + matmul(part, ref[step])
                    for half in range(2):
                        piece = product[half * rows : (half + 1) * rows]
                        if mine:
                            sums[chip, half, :, columns] = piece
                        else:
                            core_send[chip, half, :, columns] = piece.astype(bf16)

            core_copies = [
                remote_copy(
                    core_send.at[chip],
                    core_got.at[chip],
                    core_out.at[4 * number + chip],
                    core_in.at[4 * number + chip],
                    to_peer["c"],
                )
                for chip in range(4)
            ]

            axes = [extra[index % 2] for index in range(4)]
            axes += ["x" if extra[half] == "y" else "y" for half in range(2)]
            chip_on = {"x": 1, "y": 2}
            links = [
                remote_copy(
                    link_send.at[index],
                    link_got.at[index],
                    link_out.at[6 * number + index],
                    link_in.at[6 * number + index],
                    to_peer[axes[index]],
                )
                for index in range(6)
            ]

            def send(index):
                half = index % 2
                chip = 0 if index < 2 else chip_on[axes[index]]
                link_send[index] = sums[chip, half].astype(bf16)
                links[index].start()

            def settle(chip):
                core_copies[chip].wait_recv()
                for half in range(2):
                    sums[chip, half] += core_got[chip, half].astype(f32)

            def begin(previous):
                if number > 0:
                    for copy in previous[0]:
                        copy.wait_send()
                    pl.semaphore_signal(
                        ready.at[2], inc=1, device_id=peers[2], device_id_type=MESH
                    )
                produce(0, False)
                if number > 0:
                    pl.semaphore_wait(ready.at[2], 1)
                core_copies[0].start()
                produce(0, True)

            def middle(previous):
                if number > 0:
                    for copy in previous[1]:
                        copy.wait_send()
                    for index in range(2):
                        pl.semaphore_signal(
                            ready.at[index], inc=1, device_id=peers[index], device_id_type=MESH
                        )
                settle(0)
                if number > 0:
                    pl.semaphore_wait(ready.at[0], 1)
                    pl.semaphore_wait(ready.at[1], 1)
                send(0)
                send(1)
                produce(1, False)
                core_copies[1].start()
                produce(1, True)
                produce(2, False)
                core_copies[2].start()
                settle(1)
                for index in (2, 3):
                    if axes[index] == "x":
                        send(index)
                produce(2, True)
                produce(3, False)
                core_copies[3].start()
                settle(2)
                for index in (2, 3):
                    if axes[index] == "y":
                        send(index)
                for half in range(2):
                    links[half].wait_recv()
                    sums[chip_on[axes[4 + half]], half] += link_got[half].astype(f32)
                    send(4 + half)
                    if half == 0:
                        produce(3, True)
                        settle(3)

            def close():
                for half in range(2):
                    links[2 + half].wait_recv()
                    links[4 + half].wait_recv()

                    @pl.loop(0, rows // 32)
                    def _(step):
                        at = pl.ds(pl.multiple_of(step * 32, 32), 32)
                        total = sums[3, half, at, :] + link_got[2 + half, at, :].astype(f32)
                        total = total + link_got[4 + half, at, :].astype(f32)
                        finish(total, half, at, state_refs, kept, own)

                    if jobs[number]["gathers"]:
                        gather.start(half)
                    if jobs[number].get("hands"):
                        hands[0].start(half)
                if jobs[number]["gathers"]:
                    for half in range(2):
                        gather.turn(half)
                    gather.cross()
                    gather.end()

            return begin, middle, close, (core_copies, links)

        steps = [phases(number) for number in range(count)]
        steps[0][0](None)
        for number, (_, middle, close, copies) in enumerate(steps):
            middle(steps[number - 1][3])
            if number + 1 < count:
                steps[number + 1][0](copies)
            close()
        for hand in hands:
            for index in range(2):
                hand.wait_recv(index)
            hand.wait_send()
        for copy in steps[-1][3][0] + steps[-1][3][1]:
            copy.wait_send()
        for guest in guests:
            guest.end()

    depth = sum(height for job in jobs for _, height, _ in job["rights"])
    results = list(
        pl.pallas_call(
            kernel,
            grid=(1,),
            in_specs=in_specs,
            out_specs=out_specs,
            out_shape=out_shape,
            scratch_shapes=scratch,
            compiler_params=pltpu.CompilerParams(
                collective_id=collective_id,
                has_side_effects=True,
                vmem_limit_bytes=60 * 1024 * 1024,
            ),
            cost_estimate=pl.CostEstimate(
                flops=2 * length * depth * model_width,
                bytes_accessed=200 * 1024 * 1024,
                transcendentals=0,
            ),
            name=name,
        )(*arrays)
    )
    if gathers:
        results[count] = results[count].reshape(length, model_width)
    return results


def closing(grads, own_output, got_tokens):
    bf16, f32 = jnp.bfloat16, jnp.float32
    _, rows, model_width = own_output.shape
    count = len(grads)
    guests = [SquareReturn(*grad) for grad in grads]

    def kernel(*refs):
        grad_refs = refs[:count]
        out_ref, tokens_ref = refs[count : count + 2]
        got_refs = refs[count + 2 : 2 * count + 2]
        output, tokens = refs[2 * count + 2 : 2 * count + 4]
        wide, hand_out, hand_in, core_out, core_in, local = refs[2 * count + 4 : 2 * count + 10]
        guest_scratch = refs[2 * count + 10 :]
        core = lax.axis_index("c")
        to_core = {"c": 1 - core}
        at = pl.ds(pl.multiple_of(core * rows, rows), rows)
        hand = HandBack(
            out_ref, lambda index: output.at[index, at], hand_out, hand_in, local.at[2]
        )
        signal_and_wait(square_peers() + [to_core], hand.others)
        for half in range(2):
            hand.start(half)
        for number, guest in enumerate(guests):
            guest.bind(
                grad_refs[number], got_refs[number], *guest_scratch[3 * number : 3 * number + 3]
            )
            guest.begin()
        copies = []
        for index in range(2):
            wide[index] = tokens_ref[index].astype(f32)
            copies += [
                remote_copy(
                    wide.at[index],
                    tokens.at[index, at],
                    core_out.at[index],
                    core_in.at[index],
                    to_core,
                ),
                pltpu.make_async_copy(wide.at[index], tokens.at[index, at], local.at[index]),
            ]
        for copy in copies:
            copy.start()
        for index in range(2):
            place = output.at[index, at]
            hand.wait_recv(index)
            copies.append(
                remote_copy(
                    place, place, core_out.at[2 + index], core_in.at[2 + index], to_core
                )
            )
            copies[-1].start()
        hand.wait_send()
        for copy in copies:
            copy.wait()
        for guest in guests:
            guest.end()

    anywhere = pl.BlockSpec(memory_space=pl.ANY)
    shape = jax.ShapeDtypeStruct
    dma = pltpu.SemaphoreType.DMA
    operands = (*(grad[0] for grad in grads), own_output, got_tokens)
    return pl.pallas_call(
        kernel,
        grid=(1,),
        in_specs=[in_spec(array.shape) for array in operands],
        out_specs=[anywhere] * (count + 2),
        out_shape=[guest.shape for guest in guests]
        + [shape((2, 2 * rows, model_width), bf16), shape((2, 2 * rows, model_width), f32)],
        scratch_shapes=[
            pltpu.VMEM((2, rows, model_width), f32),
            dma((2,)),
            dma((2,)),
            dma((4,)),
            dma((4,)),
            dma((3,)),
        ]
        + [sems for guest in guests for sems in guest.scratch],
        compiler_params=pltpu.CompilerParams(
            collective_id=5, has_side_effects=True, vmem_limit_bytes=60 * 1024 * 1024
        ),
        cost_estimate=pl.CostEstimate(flops=0, bytes_accessed=2**27, transcendentals=0),
        name="closing",
    )(*operands)


def head_lanes(head):
    return slice(head * HEAD_DIM, (head + 1) * HEAD_DIM)


def attention_forward_kernel(query, key, value, first, attended, heads_out, log_total):
    tile = pl.program_id(0)
    rows, width = query.shape
    heads = range(width // HEAD_DIM)
    first_key = first[...]
    row_index = lax.broadcasted_iota(jnp.int32, (rows, rows), 0)
    column_index = lax.broadcasted_iota(jnp.int32, (rows, rows), 1)

    def block(index, carry, diagonal):
        at = pl.ds(pl.multiple_of(index * rows, rows), rows)
        visible = column_index + index * rows >= first_key
        if diagonal:
            visible = visible & (column_index <= row_index)
        result = []
        for head in heads:
            lane = head_lanes(head)
            largest, total, summed = carry[head]
            scores = contract_cols(query[:, lane], key[at, lane])
            scores = jnp.where(visible, scores, masked_score)
            new_largest = jnp.maximum(largest, jnp.max(scores, axis=1, keepdims=True))
            weights = jnp.where(visible, jnp.exp(scores - new_largest), 0.0)
            scaling = jnp.exp(largest - new_largest)
            total = total * scaling + jnp.sum(weights, axis=1, keepdims=True)
            summed = summed * scaling + matmul(weights.astype(jnp.bfloat16), value[at, lane])
            result.append((new_largest, total, summed))
        return tuple(result)

    carry = tuple(
        (
            jnp.full((rows, 1), masked_score, jnp.float32),
            jnp.zeros((rows, 1), jnp.float32),
            jnp.zeros((rows, HEAD_DIM), jnp.float32),
        )
        for _ in heads
    )
    carry = lax.fori_loop(0, tile, lambda index, kept: block(index, kept, False), carry)
    carry = block(tile, carry, True)
    for head in heads:
        largest, total, summed = carry[head]
        summed = summed / total
        attended[:, head_lanes(head)] = summed
        heads_out[:, head_lanes(head)] = summed.astype(jnp.bfloat16)
        log_total[head, :, :] = jnp.broadcast_to(
            jnp.transpose(largest + jnp.log(total)), log_total.shape[1:]
        )


def attention_forward(query, key, value, first_key, tile_rows):
    length, width = query.shape
    heads = width // HEAD_DIM
    part = pl.BlockSpec((tile_rows, width), lambda tile: (tile, 0))
    return pl.pallas_call(
        attention_forward_kernel,
        grid=(length // tile_rows,),
        in_specs=[
            part,
            in_spec(key.shape),
            in_spec(value.shape),
            pl.BlockSpec((tile_rows, 1), lambda tile: (tile, 0)),
        ],
        out_specs=[
            part,
            part,
            pl.BlockSpec((heads, 8, tile_rows), lambda tile: (0, 0, tile)),
        ],
        out_shape=[
            jax.ShapeDtypeStruct((length, width), jnp.float32),
            jax.ShapeDtypeStruct((length, width), jnp.bfloat16),
            jax.ShapeDtypeStruct((heads, 8, length), jnp.float32),
        ],
        compiler_params=pltpu.CompilerParams(vmem_limit_bytes=60 * 1024 * 1024),
        cost_estimate=pl.CostEstimate(
            flops=2 * length * length * width,
            bytes_accessed=10 * length * width,
            transcendentals=length * length * heads // 2,
        ),
        name="attention_forward",
    )(query, key, value, first_key)


def project(all_tokens, units, head_width, cosine, sine_table):
    bf16, f32 = jnp.bfloat16, jnp.float32
    length, model_width = all_tokens.shape
    planes, height, strip = units.shape
    rows = 512

    def kernel(tokens, weight, gains, cos, sin, normed, query, key, value):
        values = tokens[...].astype(f32)
        low = (values * rms_scale(values) * gain_row(gains, 0)).astype(bf16)
        normed[...] = low

        def turn(part):
            return part * cos[...] + pltpu.roll(part, HEAD_DIM // 2, 1) * sin[...]

        def projection(start):
            return by_planes(low, weight, start, head_width)

        query_proj = projection(0)
        key_proj = projection(head_width)
        for head in range(head_width // HEAD_DIM):
            at = slice(head * HEAD_DIM, (head + 1) * HEAD_DIM)
            query[:, at] = (turn(query_proj[:, at]) * HEAD_DIM ** (-0.5)).astype(bf16)
            key[:, at] = turn(key_proj[:, at]).astype(bf16)
        value[...] = projection(2 * head_width).astype(bf16)

    def tile(width):
        return pl.BlockSpec((rows, width), lambda step: (step, 0))

    gain_block = height // 16 - 1
    shape = jax.ShapeDtypeStruct
    return pl.pallas_call(
        kernel,
        grid=(length // rows,),
        in_specs=[
            tile(model_width),
            pl.BlockSpec((planes, 3 * head_width, strip), lambda step: (0, 0, 0)),
            pl.BlockSpec((planes, 16, strip), lambda step: (0, gain_block, 0)),
            tile(HEAD_DIM),
            tile(HEAD_DIM),
        ],
        out_specs=[tile(model_width)] + [tile(head_width)] * 3,
        out_shape=[shape((length, model_width), bf16)] + [shape((length, head_width), bf16)] * 3,
        compiler_params=pltpu.CompilerParams(vmem_limit_bytes=60 * 1024 * 1024),
        cost_estimate=pl.CostEstimate(
            flops=6 * length * head_width * model_width,
            bytes_accessed=4 * length * model_width,
            transcendentals=0,
        ),
        name="project",
    )(all_tokens, units, units, cosine, sine_table)


def gain_row(gains, index):
    return jnp.concatenate(
        [gains[plane, index : index + 1, :] for plane in range(gains.shape[0])], axis=1
    ).astype(jnp.float32)


def by_planes(rows, units, start, height):
    strip = units.shape[2]
    total = contract_cols(rows[:, :strip], units[0, start : start + height, :])
    for plane in range(1, units.shape[0]):
        total = total + contract_cols(
            rows[:, plane * strip : (plane + 1) * strip], units[plane, start : start + height, :]
        )
    return total


def hidden_forward(normed_ffn, units, hidden):
    bf16, f32 = jnp.bfloat16, jnp.float32
    length, model_width = normed_ffn.shape
    rows = 256

    def kernel(normed, weights, mixed, gate_factor, up_factor):
        low = normed[...]
        gate_proj = by_planes(low, weights, 0, hidden)
        up_proj = by_planes(low, weights, hidden, hidden)
        sigmoid = 1.0 / (1.0 + jnp.exp(-gate_proj))
        silu = gate_proj * sigmoid
        up_factor[...] = silu
        gate_factor[...] = up_proj * sigmoid * (1.0 + gate_proj * (1.0 - sigmoid))
        mixed[...] = (silu * up_proj).astype(bf16)

    def tile(width):
        return pl.BlockSpec((rows, width), lambda step: (step, 0))

    shape = jax.ShapeDtypeStruct
    return pl.pallas_call(
        kernel,
        grid=(length // rows,),
        in_specs=[tile(model_width), in_spec(units.shape)],
        out_specs=[tile(hidden)] * 3,
        out_shape=[shape((length, hidden), bf16)] + [shape((length, hidden), f32)] * 2,
        compiler_params=pltpu.CompilerParams(vmem_limit_bytes=60 * 1024 * 1024),
        cost_estimate=pl.CostEstimate(
            flops=4 * length * hidden * model_width,
            bytes_accessed=4 * length * model_width,
            transcendentals=length * hidden,
        ),
        name="hidden_forward",
    )(normed_ffn, units)


def hidden_backward(gate_factor, up_factor, all_cotangent, units, hidden):
    bf16 = jnp.bfloat16
    length, model_width = all_cotangent.shape
    rows = 512

    def kernel(gate_ref, up_ref, cotangent, weights, grad_pair):
        grad_mixed = by_planes(cotangent[...], weights, 0, hidden)
        grad_gate, grad_up = grad_mixed * gate_ref[...], grad_mixed * up_ref[...]
        grad_pair[...] = jnp.concatenate([grad_gate, grad_up], axis=1).astype(bf16)

    def tile(width):
        return pl.BlockSpec((rows, width), lambda step: (step, 0))

    shape = jax.ShapeDtypeStruct
    return pl.pallas_call(
        kernel,
        grid=(length // rows,),
        in_specs=[tile(hidden), tile(hidden), tile(model_width), in_spec(units.shape)],
        out_specs=tile(2 * hidden),
        out_shape=shape((length, 2 * hidden), bf16),
        compiler_params=pltpu.CompilerParams(vmem_limit_bytes=60 * 1024 * 1024),
        cost_estimate=pl.CostEstimate(
            flops=2 * length * hidden * model_width,
            bytes_accessed=4 * length * model_width,
            transcendentals=length * hidden,
        ),
        name="hidden_backward",
    )(gate_factor, up_factor, all_cotangent, units)


def attention_backward_kernel(guests, *refs):
    count = len(guests)
    query, key, value, branch, weight, attended, log_total, first, cos, sin = refs[:10]
    grads, key_sum, value_sum = refs[10 + count], refs[11 + 2 * count], refs[12 + 2 * count]
    guest_scratch = refs[13 + 2 * count :]
    for number, guest in enumerate(guests):
        guest.bind(
            refs[10 + number], refs[11 + count + number], *guest_scratch[3 * number : 3 * number + 3]
        )
    tile = pl.program_id(0)

    @pl.when(tile == 0)
    def _():
        signal_and_wait(square_peers())
        for guest in guests:
            guest.begin()

    rows, width = query.shape
    heads = range(width // HEAD_DIM)
    grad_tiles = by_planes(branch[...], weight, 0, width)
    grad_low = grad_tiles.astype(jnp.bfloat16)
    product = grad_low.astype(jnp.float32) * attended[...]
    centre_rows = [
        jnp.transpose(jnp.sum(product[:, head_lanes(head)], axis=1, keepdims=True))
        for head in heads
    ]
    first_row = first[:1, :]
    key_index = lax.broadcasted_iota(jnp.int32, (rows, rows), 0)
    query_index = lax.broadcasted_iota(jnp.int32, (rows, rows), 1)

    def block(index, carry, diagonal):
        at = pl.ds(pl.multiple_of(index * rows, rows), rows)
        visible = key_index + index * rows >= first_row
        if diagonal:
            visible = visible & (key_index <= query_index)
        result = []
        for head in heads:
            lane = head_lanes(head)
            query_tile, grad_tile = query[:, lane], grad_low[:, lane]
            key_block = key[at, lane]
            scores = contract_cols(key_block, query_tile)
            probability = jnp.where(visible, jnp.exp(scores - log_total[head, :1, :]), 0.0)
            grad_prob = contract_cols(value[at, lane], grad_tile)
            grad_scores = (probability * (grad_prob - centre_rows[head])).astype(jnp.bfloat16)
            key_part = matmul(grad_scores, query_tile)
            value_part = matmul(probability.astype(jnp.bfloat16), grad_tile)
            if diagonal:
                key_sum[at, lane] = key_part
                value_sum[at, lane] = value_part
            else:
                key_sum[at, lane] += key_part
                value_sum[at, lane] += value_part
            result.append(carry[head] + contract_rows(grad_scores, key_block))
        return tuple(result)

    def turn_back(part, at):
        return part * cos[at, :] - pltpu.roll(part, HEAD_DIM // 2, 1) * sin[at, :]

    carry = tuple(jnp.zeros((rows, HEAD_DIM), jnp.float32) for _ in heads)
    carry = lax.fori_loop(0, tile, lambda index, kept: block(index, kept, False), carry)
    carry = block(tile, carry, True)
    here = pl.ds(pl.multiple_of(tile * rows, rows), rows)
    for head in heads:
        grads[0, here, head_lanes(head)] = (
            turn_back(carry[head], here) * HEAD_DIM ** (-0.5)
        ).astype(jnp.bfloat16)

    @pl.when(tile == pl.num_programs(0) - 1)
    def _():
        @pl.loop(0, pl.num_programs(0))
        def _(index):
            at = pl.ds(pl.multiple_of(index * rows, rows), rows)
            for head in heads:
                lane = head_lanes(head)
                grads[1, at, lane] = turn_back(key_sum[at, lane], at).astype(jnp.bfloat16)
                grads[2, at, lane] = value_sum[at, lane].astype(jnp.bfloat16)

        for guest in guests:
            guest.end()


def attention_backward(
    query,
    key,
    value,
    grad_branch,
    units,
    attended,
    log_total,
    first_key,
    cosine,
    sine_table,
    tile_rows,
    summed,
):
    guests = [SquareReturn(grad) for grad in summed]
    length, width = query.shape
    model_width = grad_branch.shape[1]
    heads = width // HEAD_DIM
    part = pl.BlockSpec((tile_rows, width), lambda tile: (tile, 0))
    shape = jax.ShapeDtypeStruct((3, length, width), jnp.bfloat16)
    return pl.pallas_call(
        functools.partial(attention_backward_kernel, guests),
        grid=(length // tile_rows,),
        in_specs=[
            part,
            in_spec(key.shape),
            in_spec(value.shape),
            pl.BlockSpec((tile_rows, model_width), lambda tile: (tile, 0)),
            pl.BlockSpec((units.shape[0], width, units.shape[2]), lambda tile: (0, 3, 0)),
            part,
            pl.BlockSpec((heads, 8, tile_rows), lambda tile: (0, 0, tile)),
            pl.BlockSpec((8, tile_rows), lambda tile: (0, tile)),
            in_spec(cosine.shape),
            in_spec(sine_table.shape),
        ]
        + [in_spec(grad.shape) for grad in summed],
        out_specs=[in_spec((3, length, width))]
        + [pl.BlockSpec(memory_space=pl.ANY)] * len(guests),
        out_shape=[shape] + [guest.shape for guest in guests],
        scratch_shapes=[
            pltpu.VMEM((length, width), jnp.float32),
            pltpu.VMEM((length, width), jnp.float32),
        ]
        + [sems for guest in guests for sems in guest.scratch],
        compiler_params=pltpu.CompilerParams(
            collective_id=6, has_side_effects=True, vmem_limit_bytes=60 * 1024 * 1024
        ),
        cost_estimate=pl.CostEstimate(
            flops=5 * length * length * width + 2 * length * width * model_width,
            bytes_accessed=24 * length * width,
            transcendentals=length * length * heads // 2,
        ),
        name="attention_backward",
    )(
        query,
        key,
        value,
        grad_branch,
        units,
        attended,
        log_total,
        first_key,
        cosine,
        sine_table,
        *summed,
    )


def group_device(
    tokens,
    doc_starts,
    query_weight,
    key_weight,
    value_weight,
    out_weight,
    gate_weight,
    up_weight,
    down_weight,
    attention_gain,
    feedforward_gain,
    cotangent,
):
    bf16, f32 = jnp.bfloat16, jnp.float32
    x_at, z_at, core = (lax.axis_index(name) for name in ("x", "z", "c"))
    _, shard_rows, model_width = tokens.shape
    slice_width = query_weight.shape[0]
    half_rows = shard_rows // 2
    length = 2 * MEMBERS * half_rows
    planes = lax.axis_size("z")
    strip = model_width // planes
    head_width = query_weight.shape[1] // QUARTERS
    hidden = gate_weight.shape[1] // QUARTERS

    def keep_naturally(kept, half, at, values):
        part = strip // 2
        for x in range(2):
            for plane in range(planes):
                start = plane * strip + x * part
                place = x * planes * part + plane * part
                kept[half, at, place : place + part] = values[:, start : start + part]

    def units_of(weight):
        return weight.reshape(QUARTERS, -1, slice_width)

    def far_sum(grads):
        return lax.psum_scatter(grads.astype(bf16), "z", scatter_dimension=1, tiled=True)

    gains = jnp.concatenate(
        [attention_gain[None], feedforward_gain[None], jnp.zeros((14, slice_width), bf16)]
    )
    gains = jnp.broadcast_to(gains[None], (QUARTERS, 16, slice_width))
    docs = jnp.zeros((8, 128), jnp.int32).at[:2, : doc_starts.shape[1]].set(doc_starts)
    own_tokens, own_cotangent, other_docs, attention_square, pair_square, down_square = deal(
        tokens,
        cotangent,
        [
            jnp.concatenate(
                [
                    units_of(query_weight.T),
                    units_of(key_weight.T),
                    units_of(value_weight.T),
                    units_of(out_weight),
                    gains,
                ],
                axis=1,
            ),
            jnp.concatenate([units_of(gate_weight.T), units_of(up_weight.T)], axis=1),
            units_of(down_weight),
        ],
        docs,
    )
    attention_units = lax.all_gather(attention_square, "z")
    all_tokens, all_cotangent = gather_rows(own_tokens, own_cotangent)
    pair_square, _ = lax.optimization_barrier((pair_square, all_tokens))
    pair_units = lax.all_gather(pair_square, "z")

    positions = jnp.arange(length, dtype=jnp.int32)
    cosine, sine_table = turning_tables(length)
    docs = jnp.where(plane_x(z_at) == x_at, docs, other_docs)
    starts = lax.dynamic_index_in_dim(docs, z_at // 2, 0, keepdims=False)[: doc_starts.shape[1]]
    first_key = jnp.max(
        jnp.where(starts[None, :] <= positions[:, None], starts[None, :], 0), axis=1
    )
    all_tokens, first_column = lax.optimization_barrier((all_tokens, first_key[:, None]))
    normed, query_rot, key_rot, value_low = project(
        all_tokens, attention_units, head_width, cosine, sine_table
    )
    down_square, _ = lax.optimization_barrier((down_square, query_rot))
    down_units = lax.all_gather(down_square, "z")
    tile_rows = min(512, length)
    attended, heads_out, log_total = attention_forward(
        query_rot, key_rot, value_low, first_column, tile_rows
    )
    gains_at = (attention_units, 16, attention_units.shape[1] // 16 - 1)

    def after_attention(total, half, at, states, kept, own):
        token_ref, gain_ref = states
        residual = token_ref[half, at, :].astype(f32) + total
        kept[half, at, :] = residual
        own[half, at, :] = (residual * rms_scale(residual) * gain_row(gain_ref, 1)).astype(bf16)

    residual, normed_ffn = exchange(
        "branch_exchange",
        2,
        [
            dict(
                lefts=[heads_out],
                rights=[(attention_units, head_width, 3)],
                states=[(own_tokens, None, 0), gains_at],
                finish=after_attention,
                kept=f32,
                gathers=True,
            )
        ],
        ("x", "y"),
    )
    mixed_hidden, gate_factor, up_factor = hidden_forward(normed_ffn, pair_units, hidden)
    grad_down_all = contract_rows(mixed_hidden, all_cotangent)
    grad_pair_low = hidden_backward(
        gate_factor, up_factor, all_cotangent, down_units, hidden
    )
    grad_down = far_sum(grad_down_all)
    grad_pair_all = contract_rows(grad_pair_low, normed_ffn).astype(bf16)
    grad_pair_low, grad_pair_all = lax.optimization_barrier((grad_pair_low, grad_pair_all))
    grad_pair = far_sum(grad_pair_all)

    def after_feedforward(total, half, at, states, kept, own):
        residual_ref, cotangent_ref, gain_ref = states
        rows = residual_ref[half, at, :]
        scale = rms_scale(rows)
        weighted = total * gain_row(gain_ref, 1)
        mean = jnp.mean(weighted * rows, axis=-1, keepdims=True)
        grad = cotangent_ref[half, at, :].astype(f32) + scale * weighted - rows * scale**3 * mean
        kept[half, at, :] = grad
        own[half, at, :] = grad.astype(bf16)

    grad_residual, grad_branch = exchange(
        "feedforward_exchange",
        3,
        [
            dict(
                lefts=[grad_pair_low],
                rights=[(pair_units, 2 * hidden, 0)],
                states=[(residual, None, 0), (own_cotangent, None, 0), gains_at],
                finish=after_feedforward,
                kept=f32,
                gathers=True,
            )
        ],
        ("x", "y"),
    )
    grad_out = contract_rows(heads_out, grad_branch).astype(bf16)
    grad_qkv, spread_down = attention_backward(
        query_rot,
        key_rot,
        value_low,
        grad_branch,
        attention_units,
        attended,
        log_total,
        jnp.broadcast_to(first_key[None], (8, length)),
        cosine,
        sine_table,
        tile_rows,
        [grad_down],
    )
    grad_projections = lax.dot_general(
        grad_qkv, normed, (((1,), (0,)), ((), ())), preferred_element_type=f32
    ).reshape(3 * head_width, model_width)
    grad_attention = jnp.concatenate([grad_projections.astype(bf16), grad_out])
    grad_attention, grad_pair = lax.optimization_barrier((grad_attention, grad_pair))
    grad_attention = far_sum(grad_attention)

    def after_hidden(total, half, at, states, kept, own):
        keep_naturally(kept, half, at, (states[0][half, at, :] + total).astype(bf16))

    def after_all(total, half, at, states, kept, own):
        token_ref, grad_ref, gain_ref = states
        rows = token_ref[half, at, :].astype(f32)
        scale = rms_scale(rows)
        weighted = total * gain_row(gain_ref, 0)
        mean = jnp.mean(weighted * rows, axis=-1, keepdims=True)
        grad = grad_ref[half, at, :] + scale * weighted - rows * scale**3 * mean
        keep_naturally(kept, half, at, grad.astype(bf16))

    _, own_output, got_tokens, spread_gate = exchange(
        "token_exchange",
        4,
        [
            dict(
                lefts=[(grad_qkv, at) for at in range(3)],
                rights=[(attention_units, head_width, at) for at in range(3)],
                states=[(own_tokens, None, 0), (grad_residual, None, 0), gains_at],
                finish=after_all,
                kept=bf16,
                gathers=False,
                hands=True,
            ),
            dict(
                lefts=[mixed_hidden],
                rights=[(down_units, hidden, 0)],
                states=[(residual, None, 0)],
                finish=after_hidden,
                kept=bf16,
                gathers=False,
            ),
        ],
        ("x", "y"),
        [(grad_pair, 0, hidden)],
    )
    spread_up, spread_attention, output, grad_tokens = closing(
        [(grad_pair, hidden, hidden), (grad_attention,)], own_output, got_tokens
    )

    def columns(grads):
        return grads.reshape(-1, slice_width).astype(f32)

    grad_down_w, grad_gate_w, grad_up_w = (
        columns(grads)
        for grads in (spread_down, spread_gate, spread_up)
    )
    grad_gate_w, grad_up_w = grad_gate_w.T, grad_up_w.T
    grad_query_w, grad_key_w, grad_value_w, grad_out_w = (
        columns(spread_attention[:, at * head_width : (at + 1) * head_width]) for at in range(4)
    )
    grad_query_w, grad_key_w, grad_value_w = grad_query_w.T, grad_key_w.T, grad_value_w.T

    def gain_sum(*pairs):
        return sum(jnp.sum(weight.astype(f32) * grad, axis=1) for weight, grad in pairs)

    sums = jnp.stack(
        [
            gain_sum(
                (query_weight, grad_query_w), (key_weight, grad_key_w), (value_weight, grad_value_w)
            ),
            gain_sum((gate_weight, grad_gate_w), (up_weight, grad_up_w)),
        ]
    )
    sums = sums + swap(sums, "c")
    return (
        output,
        grad_tokens,
        grad_query_w,
        grad_key_w,
        grad_value_w,
        grad_out_w,
        grad_gate_w,
        grad_up_w,
        grad_down_w,
        sums[0] / attention_gain.astype(f32),
        sums[1] / feedforward_gain.astype(f32),
    )


def placements(stream, seq, head):
    both = (stream + seq) if isinstance(stream, tuple) else (stream, seq)
    in_specs = (
        P(stream, seq, None),
        P(stream, None),
        P(both, head),
        P(both, head),
        P(both, head),
        P(head, both),
        P(both, head),
        P(both, head),
        P(head, both),
        P(both),
        P(both),
        P(stream, seq, None),
    )
    out_specs = (
        P(stream, seq, None),
        P(stream, seq, None),
        P(both, head),
        P(both, head),
        P(both, head),
        P(head, both),
        P(both, head),
        P(both, head),
        P(head, both),
        P(both),
        P(both),
    )
    return in_specs, out_specs


def solution(mesh):
    def run(*arguments):
        tokens, doc_starts = arguments[:2]
        sizes = dict(mesh.shape)
        grouped = (
            (sizes["stream"], sizes["seq"], sizes["head"]) == (2, 8, 2)
            and tokens.shape[0] == 4
            and tokens.shape[1] <= WIN
        )
        if grouped:
            split = Mesh(mesh.devices.reshape(2, 4, 2, 2), ("x", "z", "y", "c"))
            in_specs, out_specs = placements(("x",), ("z", "y"), "c")
            step = group_device
        else:
            split = mesh
            in_specs, out_specs = placements("stream", "seq", "head")
            step = per_device
        return jax.shard_map(
            step, mesh=split, in_specs=in_specs, out_specs=out_specs, check_vma=False
        )(*arguments)

    return run
```
